256 devices in a mesh: gx: 8 (over z), gy: 16 (over y_lo, x, core), gz: 2 (over y_hi).
Axes of the slice: x: 4, y: 4 (y_hi: 2, y_lo: 2; y = y_hi * 2 + y_lo), z: 8, core: 2. Of those that a mesh axis runs over, the one named last changes fastest.
Arguments:
- plume_flow_variables: float32 [6, 64, 256, 256], P(None, 'gx', 'gy', 'gz'), may hold values from -6 to 6
- thermal_field: float32 [128, 128, 512], P(None, ('gx', 'gz'), 'gy'), may hold values from -6 to 6
- matter_condition: int32 [128, 128, 512], P(None, ('gx', 'gz'), 'gy'), may hold values from 0 to 2
- pool_boundary_level: int32 [64, 256], P('gx', 'gy'), may hold values from 0 to 127
- beam_focus_path: int32 [4, 2], replicated, may hold values from 0 to 511, as said below
Outputs:
- gas_out: float32 [6, 64, 256, 256], P(None, 'gx', 'gy', 'gz')
- temperature_out: float32 [128, 128, 512], P(None, ('gx', 'gz'), 'gy')
The draws below stay inside these ranges and needn't reach their ends.
Inputs may be any that keep to these rules, and one draw needn't show every extreme that they name: `beam_focus_path`: column 0 is a position along the part's first lateral dimension, below 128; column 1 along the second, below 512.
All inputs are finite; a program needn't handle non-finite values.
Results may differ from the reference program's by a relative error of at most 0.0001.
Values sent between devices are 32-bit elements; how exact they have to be, the bound alone decides.
A program may use at most 64 MiB of HBM per device.

```python
import jax
import jax.numpy as jnp

GZC = 128
WORKPIECE_LAYERS = 128
STEPS = 2
SUBSTEPS = 2
NXG = 64
NYG = 256
NZG = 256
WORKPIECE_ROWS = 128
WORKPIECE_COLS = 512
NSUB = 4


def draw_beam_focus_path(key, part):
    key_rows, key_cols = jax.random.split(jax.random.fold_in(key, 17))
    along_first = jax.random.randint(key_rows, (NSUB, 1), 0, WORKPIECE_ROWS)
    along_second = jax.random.randint(key_cols, (NSUB, 1), 0, WORKPIECE_COLS)
    path_rows = jnp.concatenate([along_first, along_second], axis=1).astype(jnp.int32)
    path_rows = path_rows.at[0, 0].set(0)
    path_rows = path_rows.at[NSUB - 1, 0].set(WORKPIECE_ROWS - 1)
    path_rows = path_rows.at[NSUB - 1, 1].set(WORKPIECE_COLS - 1)
    return path_rows.astype(jnp.int32)


def place_ends(drawn, key, least, high):
    shape = drawn.shape
    place = [jax.random.randint(jax.random.fold_in(key, axis), (), 0, shape[axis]) for axis in range(len(shape))]
    drawn = drawn.at[tuple(place)].set(least)
    longest = shape.index(max(shape))
    place[longest] = (place[longest] + 1) % shape[longest]
    return drawn.at[tuple(place)].set(high)


def shard_levels(own_key, extent, cuts, smallest, largest):
    def one(position, blocks):
        steps = jax.random.uniform(jax.random.fold_in(jax.random.fold_in(own_key, 6), position), (blocks,), jnp.float32, smallest / len(cuts), largest / len(cuts))
        return jnp.repeat(jnp.exp(steps), extent[position] // blocks).reshape((-1,) + (1,) * (len(extent) - position - 1))

    factor_of = one(*cuts[0])
    for cut in cuts[1:]:
        factor_of = factor_of * one(*cut)
    return factor_of


def centred(stream_key, extent, deviation, most, cuts=(), kind=jnp.bfloat16):
    drawn = deviation * jax.random.normal(stream_key, extent, jnp.float32)
    if cuts:
        drawn = drawn * shard_levels(stream_key, extent, cuts, -0.22, 0.18)
    return jnp.clip(drawn, -most, most).astype(kind)


def setup_inputs(seed: int = 0) -> dict:
    keys = jax.random.split(jax.random.key(seed), 6)
    return {
        "plume_flow_variables": centred(keys[0], (6, NXG, NYG, NZG), 1.0, 6.0, ((1, 8), (2, 16), (3, 2)), jnp.float32),
        "thermal_field": centred(keys[1], (WORKPIECE_LAYERS, WORKPIECE_ROWS, WORKPIECE_COLS), 1.0, 6.0, ((1, 16), (2, 16)), jnp.float32),
        "matter_condition": place_ends(jax.random.randint(keys[2], (WORKPIECE_LAYERS, WORKPIECE_ROWS, WORKPIECE_COLS), 0, 3), jax.random.fold_in(keys[2], 1), 0, 2).astype(jnp.int32),
        "pool_boundary_level": place_ends(jax.random.randint(keys[3], (NXG, NYG), 0, GZC), jax.random.fold_in(keys[3], 1), 0, GZC - 1).astype(jnp.int32),
        "beam_focus_path": draw_beam_focus_path(jax.random.fold_in(keys[5], 71), 0),
    }


GAS_STEP = 0.3
DRIFT_SPEED = 0.5
VAPOR_LOAD = 0.3
AMBIENT_LOAD = 0.7
STIFFNESS = 1.0
VISCOSITY = (0.2, 0.1, 0.15, 0.15, 0.15, 0.2)
HEAT_STEP = 1.0
POWDER_COND = 0.04
SOLID_COND = 0.15
LIQUID_COND = 0.09
LASER_POWER = 3.0
SPOT_RADIUS = 6.0
ABSORB_DEPTH = 4.0
BOIL_LEVEL = 1.0
BACK_PRESSURE = 0.5
LATENT_HEAT = 0.3
VAPOR_SOURCE = 0.5
RECOIL_PUSH = 0.4
RECOIL_PRESSURE = 0.6


def gas_rate(padded):
    center = padded[:, 1:-1, 1:-1, 1:-1]
    east_side = padded[:, 2:, 1:-1, 1:-1]
    west_side = padded[:, :-2, 1:-1, 1:-1]
    north_side = padded[:, 1:-1, 2:, 1:-1]
    south_side = padded[:, 1:-1, :-2, 1:-1]
    upper_side = padded[:, 1:-1, 1:-1, 2:]
    lower_side = padded[:, 1:-1, 1:-1, :-2]
    slope_x = 0.5 * (east_side - west_side)
    slope_y = 0.5 * (north_side - south_side)
    slope_z = 0.5 * (upper_side - lower_side)
    laplace = east_side + west_side + north_side + south_side + upper_side + lower_side - 6.0 * center
    spread = slope_x[2] + slope_y[3] + slope_z[4]
    viscous = jnp.array(VISCOSITY, jnp.float32).reshape(6, 1, 1, 1)
    coupled = jnp.stack([-VAPOR_LOAD * spread, -AMBIENT_LOAD * spread, -slope_x[5], -slope_y[5], -slope_z[5], -STIFFNESS * spread])
    return coupled - DRIFT_SPEED * slope_z + viscous * laplace


def neighbours(padded):
    return [padded[2:, 1:-1, 1:-1], padded[:-2, 1:-1, 1:-1], padded[1:-1, 2:, 1:-1],
            padded[1:-1, :-2, 1:-1], padded[1:-1, 1:-1, 2:], padded[1:-1, 1:-1, :-2]]


def heat_rate(padded_temp, padded_cond):
    center = padded_temp[1:-1, 1:-1, 1:-1]
    cond_center = padded_cond[1:-1, 1:-1, 1:-1]
    total = jnp.zeros_like(center)
    for temp_side, cond_side in zip(neighbours(padded_temp), neighbours(padded_cond)):
        total = total + 0.5 * (cond_center + cond_side) * (temp_side - center)
    return total


def conductivity(matter_condition):
    return jnp.where(matter_condition == 0, POWDER_COND, jnp.where(matter_condition == 1, SOLID_COND, LIQUID_COND)).astype(jnp.float32)


def laser_heat(x_cells, y_cells, depth_cells, target):
    along_x = jnp.exp(-((x_cells - target[0].astype(jnp.float32)) / SPOT_RADIUS) ** 2)
    along_y = jnp.exp(-((y_cells - target[1].astype(jnp.float32)) / SPOT_RADIUS) ** 2)
    along_depth = jnp.exp(-depth_cells / ABSORB_DEPTH)
    return LASER_POWER * along_depth[:, None, None] * along_x[None, :, None] * along_y[None, None, :]


def evaporation(surface_temp, pressure):
    return jax.nn.softplus(surface_temp - BOIL_LEVEL - BACK_PRESSURE * pressure)


def refine(values):
    return jnp.repeat(jnp.repeat(values, 2, axis=0), 2, axis=1)


def coarsen(values):
    rows, cols = values.shape
    return 0.25 * jnp.sum(values.reshape(rows // 2, 2, cols // 2, 2), axis=(1, 3))


def reference(plume_flow_variables, thermal_field, matter_condition, pool_boundary_level, beam_focus_path):
    vapor_state = plume_flow_variables
    workpiece_thermal_mesh = thermal_field
    padded_cond = jnp.pad(conductivity(matter_condition), 1)
    heights = jnp.arange(NZG, dtype=jnp.int32)
    surface_mask = (heights[None, None, :] == pool_boundary_level[:, :, None]).astype(jnp.float32)
    x_cells = jnp.arange(WORKPIECE_ROWS, dtype=jnp.int32).astype(jnp.float32)
    y_cells = jnp.arange(WORKPIECE_COLS, dtype=jnp.int32).astype(jnp.float32)
    depth_cells = jnp.arange(WORKPIECE_LAYERS, dtype=jnp.int32).astype(jnp.float32)
    rim = ((0, 0), (1, 1), (1, 1), (1, 1))
    for outer_step in range(STEPS):
        first_section = vapor_state + GAS_STEP * gas_rate(jnp.pad(vapor_state, rim))
        vapor_state = 0.5 * (vapor_state + first_section + GAS_STEP * gas_rate(jnp.pad(first_section, rim)))
        pressure = jnp.sum(vapor_state[5] * surface_mask, axis=2)
        fine_pressure = refine(pressure)
        for substep in range(SUBSTEPS):
            target = beam_focus_path[outer_step * SUBSTEPS + substep]
            change = heat_rate(jnp.pad(workpiece_thermal_mesh, 1), padded_cond) + laser_heat(x_cells, y_cells, depth_cells, target)
            cooling = LATENT_HEAT * evaporation(workpiece_thermal_mesh[0], fine_pressure)
            change = change.at[0].add(-cooling)
            workpiece_thermal_mesh = workpiece_thermal_mesh + HEAT_STEP * change
        surface_temp = coarsen(workpiece_thermal_mesh[0])
        vapor_mass = evaporation(surface_temp, pressure)[:, :, None] * surface_mask
        vapor_state = vapor_state.at[0].add(VAPOR_SOURCE * vapor_mass)
        vapor_state = vapor_state.at[4].add(RECOIL_PUSH * vapor_mass)
        vapor_state = vapor_state.at[5].add(RECOIL_PRESSURE * vapor_mass)
    return vapor_state, workpiece_thermal_mesh
```

```python
import functools
import math

import jax
import jax.numpy as jnp
from jax import lax
from jax.experimental import pallas as pl
from jax.experimental.pallas import tpu as pltpu
from jax.sharding import PartitionSpec as P

MESH = pl.DeviceIdType.MESH
HI = lax.Precision.HIGHEST
F32 = jnp.float32

NU = (0.2, 0.1, 0.15, 0.15, 0.15, 0.2)
BASE = tuple(1.0 - 1.8 * n for n in NU)
SIDE = tuple(0.3 * n for n in NU)
UPC = tuple(0.3 * n - 0.075 for n in NU)
DNC = tuple(0.3 * n + 0.075 for n in NU)
LASER_POWER = 3.0
LATENT_HEAT = 0.3


def softplus(x):
    return jnp.maximum(x, 0.0) + jnp.log1p(jnp.exp(-jnp.abs(x)))


def nt(a, b, precision=HI):
    return lax.dot_general(
        a, b, (((1,), (1,)), ((), ())), precision=precision, preferred_element_type=F32
    )


def nn(a, b):
    return lax.dot_general(
        a, b, (((1,), (0,)), ((), ())), precision=HI, preferred_element_type=F32
    )


def iota(shape, dim):
    return lax.broadcasted_iota(jnp.int32, shape, dim)


def forward_euler(load, edge):
    def vertical(c):
        center, other = load(c, 0, 0), edge(c)
        lane = iota(center.shape, 1)
        up = pltpu.roll(jnp.where(lane == 0, other, center), 127, 1)
        down = pltpu.roll(jnp.where(lane == 127, other, center), 1, 1)
        return up, down

    u_e, u_w = load(2, 1, 0), load(2, -1, 0)
    v_n, v_s = load(3, 0, 1), load(3, 0, -1)
    w_up, w_dn = vertical(4)
    spread = (u_e - u_w) + (v_n - v_s) + (w_up - w_dn)
    p_e, p_w, p_n, p_s = load(5, 1, 0), load(5, -1, 0), load(5, 0, 1), load(5, 0, -1)
    p_up, p_dn = vertical(5)
    coupled = (
        -0.045 * spread,
        -0.105 * spread,
        -0.15 * (p_e - p_w),
        -0.15 * (p_n - p_s),
        -0.15 * (p_up - p_dn),
        -0.15 * spread,
    )
    out = []
    for c in range(6):
        if c == 4:
            up, dn = w_up, w_dn
        elif c == 5:
            up, dn = p_up, p_dn
        else:
            up, dn = vertical(c)
        sides = (load(c, 1, 0) + load(c, -1, 0)) + (load(c, 0, 1) + load(c, 0, -1))
        out.append(
            BASE[c] * load(c, 0, 0) + SIDE[c] * sides + UPC[c] * up + DNC[c] * dn + coupled[c]
        )
    return out


def kernel(
    sizes,
    u_hbm, t_hbm, m_hbm, lvl_ref, path_ref,
    uo_ref, to_ref,
    A, B, F, UE, FE, ZS, ZR, SS, SR, PS, PR,
    TA, MA, TB, TC, KB, GX, GY, GD, LXB, LYD,
    SA, SB, SK, SGX, SGY, SGD, SGB, SL, SM, LO, LL, MM,
    in_sem, us_sem, ur_sem, zs_sem, zr_sem, ss_sem, sr_sem, ps_sem, pr_sem,
    bs_sem, br_sem,
):
    nx, ny = sizes
    gx, gy, gz = lax.axis_index("gx"), lax.axis_index("gy"), lax.axis_index("gz")
    other = 1 - gz

    def dev(dx, dy, z):
        return (lax.rem(gx + dx + nx, nx), lax.rem(gy + dy + ny, ny), z)

    loads = [
        pltpu.make_async_copy(u_hbm, A.at[:, 2:10, 8:24], in_sem.at[0]),
        pltpu.make_async_copy(t_hbm, TA.at[2:10, 8:40], in_sem.at[1]),
        pltpu.make_async_copy(m_hbm, MA.at[2:10, 8:40], in_sem.at[2]),
    ]
    for copy in loads:
        copy.start()

    barrier = pltpu.get_barrier_semaphore()
    for dx in (-1, 0, 1):
        for dy in (-1, 0, 1):
            for z in (gz, other):
                if dx == 0 and dy == 0 and z is gz:
                    continue
                pl.semaphore_signal(
                    barrier, inc=1, device_id=dev(dx, dy, z), device_id_type=MESH
                )

    sent = []

    def send(src, dst, s_sem, r_sem, target):
        copy = pltpu.make_async_remote_copy(
            src_ref=src, dst_ref=dst, send_sem=s_sem, recv_sem=r_sem,
            device_id=target, device_id_type=MESH,
        )
        copy.start()
        sent.append(copy)

    def arrive(dst, s_sem, r_sem):
        pltpu.make_async_remote_copy(
            src_ref=dst, dst_ref=dst, send_sem=s_sem, recv_sem=r_sem,
            device_id=dev(1, 0, gz), device_id_type=MESH,
        ).wait_recv()

    def vapor_slots(X):
        slots = [X.at[:, 0:2, 8:24], X.at[:, 10:12, 8:24], X.at[:, 2:10, 0:8], X.at[:, 2:10, 24:32]]
        for xi in (1, 10):
            for row in (0, 24):
                slots.append(X.at[:, xi:xi + 1, row:row + 8])
        return slots

    def vapor_sources(own):
        sources = [own(6, 2, 0, 16), own(0, 2, 0, 16), own(0, 8, 8, 8), own(0, 8, 0, 8)]
        for x in (7, 0):
            for y in (8, 0):
                sources.append(own(x, 1, y, 8))
        return sources

    vapor_targets = [(1, 0), (-1, 0), (0, 1), (0, -1), (1, 1), (1, -1), (-1, 1), (-1, -1)]

    def send_vapor(step, own, X):
        slots, sources = vapor_slots(X), vapor_sources(own)
        for n in (0, 1, 4, 5, 6, 7, 2, 3):
            send(sources[n], slots[n], us_sem.at[step, n], ur_sem.at[step, n],
                 dev(*vapor_targets[n], gz))

    def await_vapor(step, X):
        slots = vapor_slots(X)
        for n in range(8):
            arrive(slots[n], us_sem.at[step, n], ur_sem.at[step, n])

    lane8 = iota((8, 128), 1)
    sub8 = iota((8, 128), 0)

    def pack_z(step, X):
        shift = jnp.where(gz == 0, 2, 0)
        turned = lax.rem(lane8 + shift, 128) // 2
        for half in range(2):
            acc = jnp.zeros((8, 128), F32)
            for k in range(64 if half == 0 else 32):
                n = half * 64 + k
                c, x, yt = n // 16, (n // 2) % 8, n % 2
                v = X[c, x + 2, 8 + 8 * yt:16 + 8 * yt, :]
                if k:
                    v = pltpu.roll(v, 2 * k, 1)
                acc = jnp.where(turned == k, v, acc)
            ZS[step, half] = acc

    z_targets = [(0, 0), (1, 0), (-1, 0), (0, 1), (0, -1)]

    def send_z(step):
        for n in range(5):
            send(ZS.at[step], ZR.at[step, n], zs_sem.at[step, n], zr_sem.at[step, n],
                 dev(*z_targets[n], other))

    def await_z(step):
        for n in range(5):
            arrive(ZR.at[step, n], zs_sem.at[step, n], zr_sem.at[step, n])

    edge_keep = lax.rem(lane8 + 2 * gz, 128) < 2

    def flag(cond):
        return jnp.where(cond, 1.0, 0.0)

    def rim_flags():
        return jnp.where(sub8 < 4, flag(gy < ny - 1), flag(gy > 0)) > 0.5

    def unpack_z(step):
        def tile(slot, c, x, yt):
            n = c * 16 + x * 2 + yt
            v = ZR[step, slot, n // 64]
            k = 2 * (n % 64)
            if k:
                v = pltpu.roll(v, 128 - k, 1)
            return jnp.where(edge_keep, v, 0.0)

        for c in range(6):
            for yt in range(2):
                rows = slice(8 + 8 * yt, 16 + 8 * yt)
                for x in range(8):
                    UE[c, x + 1, rows, :] = tile(0, c, x, yt)
                UE[c, 0, rows, :] = tile(1, c, 7, yt)
                UE[c, 9, rows, :] = tile(2, c, 0, yt)
            for x in range(8):
                low, high = tile(3, c, x, 1), tile(4, c, x, 0)
                rim = jnp.where(sub8 < 4, high, low)
                UE[c, x + 1, 0:8, :] = rim
                UE[c, x + 1, 24:32, :] = rim

    def clear_outside(X):
        @pl.when(gx == 0)
        def _():
            X[:, 0:2] = jnp.zeros((6, 2, 32, 128), F32)
            UE[:, 0:1] = jnp.zeros((6, 1, 32, 128), F32)

        @pl.when(gx == nx - 1)
        def _():
            X[:, 10:12] = jnp.zeros((6, 2, 32, 128), F32)
            UE[:, 9:10] = jnp.zeros((6, 1, 32, 128), F32)

        rim_valid = rim_flags()

        @pl.loop(0, 60)
        def _(n):
            c, xi = n // 10, 1 + lax.rem(n, 10)
            rim = jnp.where(sub8 < 4, X[c, xi, 24:32, :], X[c, xi, 0:8, :])
            rim = jnp.where(rim_valid, rim, 0.0)
            X[c, xi, 0:8, :] = rim
            X[c, xi, 24:32, :] = rim

        @pl.when((gy == 0) | (gy == ny - 1))
        def _():
            @pl.loop(0, 60)
            def _(n):
                c, xi = n // 10, lax.rem(n, 10)
                rim = jnp.where(rim_valid, UE[c, xi, 0:8, :], 0.0)
                UE[c, xi, 0:8, :] = rim
                UE[c, xi, 24:32, :] = rim

    def advance(X, emit):
        rim_rows = rim_flags()
        lane16 = iota((16, 128), 1)
        edge_lane = jnp.where(gz == 0, 0, 127)

        @pl.loop(0, 10)
        def _(i):
            xi = i + 1

            def load(c, dx, dy):
                return X[c, xi + dx, 8 + dy:24 + dy, :]

            new = forward_euler(load, lambda c: UE[c, i, 8:24, :])
            for c in range(6):
                F[c, i, 8:24, :] = new[c]

        @pl.loop(0, 8)
        def _(x):
            def load_rim(c, dx, dy):
                start = {0: 0, 1: 1, -1: 23}[dy]
                return X[c, x + 2 + dx, start:start + 8, :]

            new = forward_euler(load_rim, lambda c: UE[c, x + 1, 0:8, :])
            for c in range(6):
                rim = jnp.where(rim_rows, new[c], 0.0)
                F[c, x + 1, 0:8, :] = rim
                F[c, x + 1, 24:32, :] = rim

            def load_edge(c, dx, dy):
                return UE[c, x + 1 + dx, 8 + dy:24 + dy, :]

            new = forward_euler(load_edge, lambda c: X[c, x + 2, 8:24, :])
            for c in range(6):
                FE[c, x] = jnp.where(lane16 == edge_lane, new[c], 0.0)

        @pl.when(gx == 0)
        def _():
            F[:, 0:1] = jnp.zeros((6, 1, 32, 128), F32)

        @pl.when(gx == nx - 1)
        def _():
            F[:, 9:10] = jnp.zeros((6, 1, 32, 128), F32)

        @pl.loop(0, 8)
        def _(x):
            def load(c, dx, dy):
                return F[c, x + 1 + dx, 8 + dy:24 + dy, :]

            new = forward_euler(load, lambda c: FE[c, x])
            for c in range(6):
                emit(c, x, 0.5 * (X[c, x + 2, 8:24, :] + new[c]))

    row_first = gx * 16 - 8
    col_first = gy * 32 - 32
    rows_all, cols_all = nx * 16, ny * 32

    def gauss(cells, centre):
        d = (cells.astype(F32) - centre.astype(F32)) / 6.0
        return jnp.exp(-(d * d))

    def prepare():
        col = col_first + lane8
        col_in = (col >= 0) & (col < cols_all) & (lane8 < 96)
        depth = jnp.exp(-(sub8.astype(F32)) / 4.0)
        for sub in range(4):
            a, b = path_ref[sub, 0], path_ref[sub, 1]
            profile = LASER_POWER * depth * gauss(col, b)

            @pl.loop(0, 32)
            def _(r):
                along = gauss(jnp.full((8, 128), row_first + r, jnp.int32), a)
                SL[sub, pl.ds(pl.multiple_of(r * 8, 8), 8), :] = profile * along

            c48 = gy * 32 - 8 + iota((48, 128), 0)
            d48 = jnp.exp(-(iota((48, 128), 1).astype(F32)) / 4.0)
            LYD[sub] = LASER_POWER * d48 * gauss(c48, b)
            for r in range(12):
                cell = jnp.full((8, 128), (gx * 2 + gz) * 8 - 2 + r, jnp.int32)
                LXB[sub * 12 + r] = gauss(cell, a)

        @pl.loop(0, 32)
        def _(r):
            row = row_first + r
            row_in = flag((row >= 0) & (row < rows_all))
            SM[pl.ds(pl.multiple_of(r * 8, 8), 8), :] = jnp.where(col_in, row_in, 0.0)

        level = jnp.concatenate(
            [lvl_ref[...].astype(F32), jnp.zeros((8, 112), F32)], axis=1)
        SS[4] = level
        eye = jnp.where(iota((16, 128), 0) == iota((16, 128), 1), 1.0, 0.0)
        LO[...] = nt(eye, jnp.concatenate([level, jnp.zeros((120, 128), F32)], axis=0))

    def pack_surface():
        pick = jnp.where(sub8 == lane8, 1.0, 0.0)
        for half in range(2):
            t = TA[2 + 4 * half:6 + 4 * half, 8:40, :].reshape(128, 128)
            m = MA[2 + 4 * half:6 + 4 * half, 8:40, :].reshape(128, 128).astype(F32)
            SS[half] = nt(pick, t)
            SS[2 + half] = nt(pick, m)

    own_slot = (1 + gz) * 3 + 1

    def send_surface():
        for near in (True, False):
            tx = 0 if near else 2 * gz - 1
            block = 1 + gz if near else 3 - 3 * gz
            for ty in (-1, 0, 1):
                for z in (gz, other):
                    if near and ty == 0 and z is gz:
                        continue
                    slot = block * 3 + 1 - ty
                    same = 1 if z is gz else 0
                    n = (6 if near else 0) + (ty + 1) * 2 + same
                    send(SS, SR.at[slot], ss_sem.at[n], sr_sem.at[slot], dev(tx, ty, z))

    def await_surface():
        for slot in range(12):
            if slot in (4, 7):
                @pl.when(own_slot != slot)
                def _():
                    arrive(SR.at[slot], ss_sem.at[0], sr_sem.at[slot])
            else:
                arrive(SR.at[slot], ss_sem.at[0], sr_sem.at[slot])

    def assemble_surface():
        SK[0:8, :] = jnp.zeros((8, 128), F32)
        SK[264:272, :] = jnp.zeros((8, 128), F32)
        SA[0:8, :] = jnp.zeros((8, 128), F32)
        SA[264:272, :] = jnp.zeros((8, 128), F32)
        SB[0:8, :] = jnp.zeros((8, 128), F32)
        SB[264:272, :] = jnp.zeros((8, 128), F32)
        SGX[0:8, :] = jnp.zeros((8, 128), F32)

        def merged(rb, x, first):
            parts = []
            for cb in range(3):
                v = SR[rb * 3 + cb, first + x // 4]
                shift = (32 * cb - 32 * (x % 4)) % 128
                parts.append(pltpu.roll(v, shift, 1) if shift else v)
            return jnp.where(lane8 < 32, parts[0], jnp.where(lane8 < 64, parts[1], parts[2]))

        @pl.loop(0, 4)
        def _(rb):
            for x in range(8):
                at = pl.multiple_of(rb * 64 + x * 8, 8)
                mask = SM[pl.ds(at, 8), :] > 0.5
                phase = merged(rb, x, 2)
                k = jnp.where(phase < 0.5, 0.04, jnp.where(phase < 1.5, 0.15, 0.09))
                SK[pl.ds(at + 8, 8), :] = jnp.where(mask, k, 0.0)
                SA[pl.ds(at + 8, 8), :] = jnp.where(mask, merged(rb, x, 0), 0.0)

        @pl.loop(0, 32)
        def _(r):
            at = pl.multiple_of(r * 8, 8)
            k = SK[pl.ds(at + 8, 8), :]
            SGX[pl.ds(at + 8, 8), :] = 0.5 * (k + SK[pl.ds(at + 16, 8), :])
            SGY[pl.ds(at, 8), :] = 0.5 * (k + pltpu.roll(k, 127, 1))
            SGD[pl.ds(at, 8), :] = jnp.where(sub8 == 7, 0.0, 0.5 * (k + pltpu.roll(k, 7, 0)))
            SGB[pl.ds(at, 8), :] = jnp.where(sub8 == 0, 0.5 * k, 0.0)

        blocks = []
        for rb in (0, 1, 3):
            acc = SR[rb * 3, 4]
            for cb in (1, 2):
                acc = acc + pltpu.roll(SR[rb * 3 + cb, 4], 16 * cb, 1)
            blocks.append(acc)
        blocks.append(jnp.zeros((104, 128), F32))
        eye = jnp.where(iota((48, 128), 0) == iota((48, 128), 1), 1.0, 0.0)
        LL[...] = nt(eye, jnp.concatenate(blocks, axis=0))

    def surface_substep(sub, src, dst, fine_pressure):
        for chunk in range(4):
            base = chunk * 64
            t = src[base + 8:base + 72, :]
            g = SGX[base + 8:base + 72, :]
            change = g * (src[base + 16:base + 80, :] - t) - SGX[base:base + 64, :] * (
                t - src[base:base + 64, :])
            flow = SGY[base:base + 64, :] * (pltpu.roll(t, 127, 1) - t)
            change = change + (flow - pltpu.roll(flow, 1, 1))
            t3 = t.reshape(8, 8, 128)
            gd = SGD[base:base + 64, :].reshape(8, 8, 128)
            flow3 = gd * (pltpu.roll(t3, 7, 1) - t3)
            change = change + (flow3 - pltpu.roll(flow3, 1, 1)).reshape(64, 128)
            change = change - SGB[base:base + 64, :] * t + SL[sub, base:base + 64, :]
            dst[base + 8:base + 72, :] = (t + change) * SM[base:base + 64, :]
        top = src[pl.ds(8, 32, stride=8), :]
        cooling = LATENT_HEAT * softplus(top - 1.0 - 0.5 * fine_pressure)
        cooling = cooling * SM[pl.ds(0, 32, stride=8), :]
        dst[pl.ds(8, 32, stride=8), :] = dst[pl.ds(8, 32, stride=8), :] - cooling

    def pressures(step, X, at_x, at_y):
        lane16 = iota((16, 128), 1)
        height = (lane16 + gz * 128).astype(F32)
        acc = jnp.zeros((16, 128), F32)
        for x in range(8):
            v = X[5, x + at_x, at_y:at_y + 16, :]
            hit = height == LO[:, x:x + 1]
            s = jnp.sum(jnp.where(hit, v, 0.0), axis=1, keepdims=True)
            acc = jnp.where(lane16 == x, s, acc)
        PS[step] = acc

        @pl.when(gz == 0)
        def _():
            PR[step, 4] = acc

    p_targets = [(tx, ty, s) for tx in (-1, 0, 1) for ty in (-1, 0, 1) for s in (0, 1)
                 if (tx, ty, s) != (0, 0, 1)]

    def p_copy(step, n):
        tx, ty, s = p_targets[n]
        slot = (1 - tx) * 3 + 1 - ty
        return pltpu.make_async_remote_copy(
            src_ref=PS.at[step], dst_ref=PR.at[step, slot], send_sem=ps_sem.at[step, n],
            recv_sem=pr_sem.at[step, slot], device_id=dev(tx, ty, gz if s else other),
            device_id_type=MESH)

    def send_pressures(step):
        @pl.when(gz == 0)
        def _():
            for n in range(17):
                p_copy(step, n).start()

    def await_pressures(step):
        for slot in range(9):
            if slot == 4:
                @pl.when(gz == 1)
                def _():
                    arrive(PR.at[step, slot], ps_sem.at[step, 0], pr_sem.at[step, slot])
            else:
                arrive(PR.at[step, slot], ps_sem.at[step, 0], pr_sem.at[step, slot])

    def coarse_pressure(step):
        blocks = []
        for by in range(3):
            acc = PR[step, by]
            for bx in (1, 2):
                acc = acc + pltpu.roll(PR[step, bx * 3 + by], 8 * bx, 1)
            blocks.append(acc)
        return jnp.concatenate(blocks, axis=0)

    def fine_from_coarse(coarse):
        rows = jnp.where(iota((32, 128), 1) == (iota((32, 128), 0) + 8) // 2, 1.0, 0.0)
        cols = jnp.where(iota((128, 128), 0) == iota((128, 128), 1) // 2, 1.0, 0.0)
        padded = jnp.concatenate([coarse, jnp.zeros((80, 128), F32)], axis=0)
        return nn(nt(rows, padded), cols)

    def mass_from_surface(ref, coarse):
        top = jnp.concatenate(
            [ref[pl.ds(8, 32, stride=8), :], jnp.zeros((96, 128), F32)], axis=0)
        cols = jnp.where(iota((48, 128), 0) == iota((48, 128), 1) // 2, 0.25, 0.0)
        i = iota((128, 128), 0)
        rows = jnp.where((iota((128, 128), 1) == (i + 8) // 2) & (i < 32), 1.0, 0.0)
        surface = nn(nt(cols, top), rows)
        mass = softplus(surface - 1.0 - 0.5 * coarse)
        y = gy * 16 - 16 + iota((48, 128), 0)
        x = gx * 8 - 8 + iota((48, 128), 1)
        inside = (y >= 0) & (y < ny * 16) & (x >= 0) & (x < nx * 8)
        return jnp.where(inside, mass, 0.0)

    def with_rim(v):
        rim = jnp.where(sub8 < 4, v[32:40], v[8:16])
        return jnp.concatenate([rim, v[16:32], rim], axis=0)

    row_block = gx * 2 + gz
    dn_row, up_row = -(1 - gz), gz

    def bulk_slots(X):
        slots = [X.at[0:2, 8:40], X.at[10:12, 8:40], X.at[2:10, 0:8], X.at[2:10, 40:48]]
        for r in (1, 10):
            for c in (0, 40):
                slots.append(X.at[r:r + 1, c:c + 8])
        return slots

    def bulk_sources(X, r0, c0):
        def own(r, nr, c, nc):
            return X.at[r0 + r:r0 + r + nr, c0 + c:c0 + c + nc]

        sources = [own(6, 2, 0, 32), own(0, 2, 0, 32), own(0, 8, 24, 8), own(0, 8, 0, 8)]
        for r in (7, 0):
            for c in (24, 0):
                sources.append(own(r, 1, c, 8))
        return sources

    def send_bulk(kind, X, r0, c0, D):
        targets = [dev(up_row, 0, other), dev(dn_row, 0, other), dev(0, 1, gz), dev(0, -1, gz)]
        for tx in (up_row, dn_row):
            for ty in (1, -1):
                targets.append(dev(tx, ty, other))
        sources, slots = bulk_sources(X, r0, c0), bulk_slots(D)
        for n in range(8):
            send(sources[n], slots[n], bs_sem.at[kind, n], br_sem.at[kind, n], targets[n])

    def await_bulk(kind, D):
        slots = bulk_slots(D)
        for n in range(8):
            arrive(slots[n], bs_sem.at[kind, n], br_sem.at[kind, n])

    def clear_bulk(X):
        @pl.when(row_block == 0)
        def _():
            X[0:2] = jnp.zeros((2, 48, 128), F32)

        @pl.when(row_block == 2 * nx - 1)
        def _():
            X[10:12] = jnp.zeros((2, 48, 128), F32)

        @pl.when(gy == 0)
        def _():
            X[:, 0:8] = jnp.zeros((12, 8, 128), F32)

        @pl.when(gy == ny - 1)
        def _():
            X[:, 40:48] = jnp.zeros((12, 8, 128), F32)

    def prepare_bulk():
        @pl.loop(0, 12)
        def _(r):
            m = MA[r]
            KB[r] = jnp.where(m == 0, 0.04, jnp.where(m == 1, 0.15, 0.09))

        clear_bulk(KB)

        @pl.loop(0, 11)
        def _(r):
            k = KB[r]
            GX[r] = 0.5 * (k + KB[r + 1])
            GY[r] = 0.5 * (k + pltpu.roll(k, 47, 0))
            last = iota((48, 128), 1) == 127
            GD[r] = 0.5 * (k + jnp.where(last, 0.0, pltpu.roll(k, 127, 1)))

    def bulk_substep(sub, src, dst, low, high, own_only=False):
        col = gy * 32 - 8 + iota((48, 128), 0)
        col_in = jnp.where((col >= 0) & (col < cols_all), 1.0, 0.0)
        last = iota((48, 128), 1) == 127

        @pl.loop(low, high)
        def _(r):
            t = src[r]
            change = GX[r] * (src[r + 1] - t) - GX[r - 1] * (t - src[r - 1])
            flow = GY[r] * (pltpu.roll(t, 47, 0) - t)
            change = change + (flow - pltpu.roll(flow, 1, 0))
            flow = GD[r] * (jnp.where(last, 0.0, pltpu.roll(t, 127, 1)) - t)
            change = change + (flow - pltpu.roll(flow, 1, 1))
            along = LXB[sub * 12 + r]
            laser = LYD[sub] * jnp.concatenate([along] * 6, axis=0)
            row = row_block * 8 - 2 + r
            row_in = jnp.where((row >= 0) & (row < rows_all), 1.0, 0.0)
            new = (t + change + laser) * (col_in * row_in)
            if own_only:
                dst[r, 8:40, :] = new[8:40]
            else:
                dst[r] = new

    prepare()
    loads[0].wait()
    pack_z(0, A)
    loads[1].wait()
    loads[2].wait()
    pack_surface()
    SR[own_slot] = SS[...]
    pl.semaphore_wait(barrier, 17)

    send_vapor(0, lambda x, n, y, m: u_hbm.at[:, x:x + n, y:y + m], A)
    send_z(0)
    send_surface()
    send_bulk(0, t_hbm, 0, 0, TA)
    send_bulk(1, m_hbm, 0, 0, MA)

    await_z(0)
    unpack_z(0)
    await_vapor(0, A)
    clear_outside(A)

    def to_b(c, x, v):
        B[c, x + 2, 8:24, :] = v

    advance(A, to_b)
    first = len(sent)
    send_vapor(1, lambda x, n, y, m: B.at[:, x + 2:x + 2 + n, y + 8:y + 8 + m], B)
    sent_b = sent[first:]
    del sent[first:]
    pressures(0, B, 2, 8)
    send_pressures(0)
    pack_z(1, B)
    send_z(1)

    await_surface()
    assemble_surface()
    await_bulk(0, TA)
    await_bulk(1, MA)
    clear_bulk(TA)
    prepare_bulk()
    bulk_substep(0, TA, TC, 1, 11)
    bulk_substep(1, TC, TB, 2, 10, True)
    send_bulk(2, TB, 2, 8, TB)

    await_pressures(0)
    coarse = coarse_pressure(0)
    fine = fine_from_coarse(coarse)
    surface_substep(0, SA, SB, fine)
    surface_substep(1, SB, SA, fine)
    MM[...] = with_rim(mass_from_surface(SA, coarse))
    LL[0:32, :] = with_rim(LL[...])

    await_z(1)
    unpack_z(1)
    await_vapor(1, B)
    clear_outside(B)
    for copy in sent_b:
        copy.wait_send()
    lane32 = iota((32, 128), 1)
    height = (lane32 + gz * 128).astype(F32)
    height_edge = (lane32 + other * 128).astype(F32)
    for xi in range(12):
        mass = jnp.broadcast_to(MM[:, xi + 6:xi + 7], (32, 128))
        level = jnp.broadcast_to(LL[0:32, xi + 6:xi + 7], (32, 128))
        field = jnp.where(height == level, mass, 0.0)
        B[0, xi] = B[0, xi] + 0.5 * field
        B[4, xi] = B[4, xi] + 0.4 * field
        B[5, xi] = B[5, xi] + 0.6 * field
        if 1 <= xi <= 10:
            @pl.when(gz == 1)
            def _():
                edge = jnp.where((height_edge == level) & (lane32 >= 126), mass, 0.0)
                UE[0, xi - 1] = UE[0, xi - 1] + 0.5 * edge
                UE[4, xi - 1] = UE[4, xi - 1] + 0.4 * edge
                UE[5, xi - 1] = UE[5, xi - 1] + 0.6 * edge

    def to_out(c, x, v):
        uo_ref[c, x] = v

    advance(B, to_out)
    pressures(1, uo_ref, 0, 0)
    send_pressures(1)

    await_bulk(2, TB)
    clear_bulk(TB)
    bulk_substep(2, TB, TC, 1, 11)
    bulk_substep(3, TC, TA, 2, 10, True)

    await_pressures(1)
    coarse = coarse_pressure(1)
    fine = fine_from_coarse(coarse)
    surface_substep(2, SA, SB, fine)
    surface_substep(3, SB, SA, fine)
    mass_now = mass_from_surface(SA, coarse)[16:32]
    lane16 = iota((16, 128), 1)
    height = (lane16 + gz * 128).astype(F32)
    for x in range(8):
        mass = jnp.broadcast_to(mass_now[:, x + 8:x + 9], (16, 128))
        level = jnp.broadcast_to(LO[:, x:x + 1], (16, 128))
        field = jnp.where(height == level, mass, 0.0)
        uo_ref[0, x] = uo_ref[0, x] + 0.5 * field
        uo_ref[4, x] = uo_ref[4, x] + 0.4 * field
        uo_ref[5, x] = uo_ref[5, x] + 0.6 * field

    eye = jnp.where(iota((128, 128), 0) == iota((128, 128), 1), 1.0, 0.0)
    for half in range(2):
        acc = jnp.zeros((8, 128), F32)
        for i in range(4):
            at = pl.multiple_of((9 + gz * 8 + 4 * half + i) * 8, 8)
            v = SA[pl.ds(at, 8), :]
            shift = (32 * i - 32) % 128
            v = pltpu.roll(v, shift, 1) if shift else v
            acc = jnp.where(lane8 // 32 == i, v, acc)
        turned = nt(eye, jnp.concatenate([acc, jnp.zeros((120, 128), F32)], axis=0))
        turned = turned.reshape(4, 32, 128)
        shallow = iota((4, 32, 128), 2) < 4
        deep = TA[2 + 4 * half:6 + 4 * half, 8:40, :]
        to_ref[4 * half:4 * half + 4] = jnp.where(shallow, turned, deep)

    for copy in sent:
        copy.wait_send()

    @pl.when(gz == 0)
    def _():
        for step in range(2):
            for n in range(17):
                p_copy(step, n).wait_send()


def solution(mesh):
    sizes = (mesh.shape["gx"], mesh.shape["gy"])

    def shards(vapor, thermal, phase, level, path):
        anywhere = pl.BlockSpec(memory_space=pl.ANY)
        vmem = pl.BlockSpec(memory_space=pltpu.VMEM)
        dma = pltpu.SemaphoreType.DMA
        row = (12, 48, 128)
        gas, temp = pl.pallas_call(
            functools.partial(kernel, sizes),
            out_shape=(
                jax.ShapeDtypeStruct((6, 8, 16, 128), F32),
                jax.ShapeDtypeStruct((8, 32, 128), F32),
            ),
            in_specs=[anywhere, anywhere, anywhere, vmem, pl.BlockSpec(memory_space=pltpu.SMEM)],
            out_specs=(vmem, vmem),
            scratch_shapes=[
                pltpu.VMEM((6, 12, 32, 128), F32), pltpu.VMEM((6, 12, 32, 128), F32),
                pltpu.VMEM((6, 10, 32, 128), F32), pltpu.VMEM((6, 10, 32, 128), F32),
                pltpu.VMEM((6, 8, 16, 128), F32),
                pltpu.VMEM((2, 2, 8, 128), F32), pltpu.VMEM((2, 5, 2, 8, 128), F32),
                pltpu.VMEM((5, 8, 128), F32), pltpu.VMEM((12, 5, 8, 128), F32),
                pltpu.VMEM((2, 16, 128), F32), pltpu.VMEM((2, 9, 16, 128), F32),
                pltpu.VMEM(row, F32), pltpu.VMEM(row, jnp.int32), pltpu.VMEM(row, F32),
                pltpu.VMEM(row, F32), pltpu.VMEM(row, F32), pltpu.VMEM(row, F32),
                pltpu.VMEM(row, F32), pltpu.VMEM(row, F32),
                pltpu.VMEM((48, 8, 128), F32), pltpu.VMEM((4, 48, 128), F32),
                pltpu.VMEM((272, 128), F32), pltpu.VMEM((272, 128), F32),
                pltpu.VMEM((272, 128), F32), pltpu.VMEM((264, 128), F32),
                pltpu.VMEM((256, 128), F32), pltpu.VMEM((256, 128), F32),
                pltpu.VMEM((256, 128), F32), pltpu.VMEM((4, 256, 128), F32),
                pltpu.VMEM((256, 128), F32), pltpu.VMEM((16, 128), F32),
                pltpu.VMEM((48, 128), F32), pltpu.VMEM((32, 128), F32),
                dma((3,)), dma((2, 8)), dma((2, 8)), dma((2, 5)), dma((2, 5)),
                dma((12,)), dma((12,)), dma((2, 17)), dma((2, 9)),
                dma((3, 8)), dma((3, 8)),
            ],
            compiler_params=pltpu.CompilerParams(collective_id=0, has_side_effects=True),
        )(vapor, jnp.transpose(thermal, (1, 2, 0)), jnp.transpose(phase, (1, 2, 0)), level, path)
        return gas, jnp.transpose(temp, (2, 0, 1))

    return jax.shard_map(
        shards,
        mesh=mesh,
        in_specs=(
            P(None, "gx", "gy", "gz"),
            P(None, ("gx", "gz"), "gy"),
            P(None, ("gx", "gz"), "gy"),
            P("gx", "gy"),
            P(),
        ),
        out_specs=(P(None, "gx", "gy", "gz"), P(None, ("gx", "gz"), "gy")),
        check_vma=False,
    )
```

```python
import functools
import math

import jax
import jax.numpy as jnp
from jax import lax
from jax.experimental import pallas as pl
from jax.experimental.pallas import tpu as pltpu
from jax.sharding import PartitionSpec as P

MESH = pl.DeviceIdType.MESH
HI = lax.Precision.HIGHEST
F32 = jnp.float32

NU = (0.2, 0.1, 0.15, 0.15, 0.15, 0.2)
BASE = tuple(1.0 - 1.8 * n for n in NU)
SIDE = tuple(0.3 * n for n in NU)
UPC = tuple(0.3 * n - 0.075 for n in NU)
DNC = tuple(0.3 * n + 0.075 for n in NU)
LASER_POWER = 3.0
LATENT_HEAT = 0.3


def softplus(x):
    return jnp.maximum(x, 0.0) + jnp.log1p(jnp.exp(-jnp.abs(x)))


def nt(a, b, precision=HI):
    return lax.dot_general(
        a, b, (((1,), (1,)), ((), ())), precision=precision, preferred_element_type=F32
    )


def nn(a, b):
    return lax.dot_general(
        a, b, (((1,), (0,)), ((), ())), precision=HI, preferred_element_type=F32
    )


def iota(shape, dim):
    return lax.broadcasted_iota(jnp.int32, shape, dim)


def forward_euler(load, edge):
    def vertical(c):
        center, other = load(c, 0, 0), edge(c)
        lane = iota(center.shape, 1)
        up = pltpu.roll(jnp.where(lane == 0, other, center), 127, 1)
        down = pltpu.roll(jnp.where(lane == 127, other, center), 1, 1)
        return up, down

    u_e, u_w = load(2, 1, 0), load(2, -1, 0)
    v_n, v_s = load(3, 0, 1), load(3, 0, -1)
    w_up, w_dn = vertical(4)
    spread = (u_e - u_w) + (v_n - v_s) + (w_up - w_dn)
    p_e, p_w, p_n, p_s = load(5, 1, 0), load(5, -1, 0), load(5, 0, 1), load(5, 0, -1)
    p_up, p_dn = vertical(5)
    coupled = (
        -0.045 * spread,
        -0.105 * spread,
        -0.15 * (p_e - p_w),
        -0.15 * (p_n - p_s),
        -0.15 * (p_up - p_dn),
        -0.15 * spread,
    )
    out = []
    for c in range(6):
        if c == 4:
            up, dn = w_up, w_dn
        elif c == 5:
            up, dn = p_up, p_dn
        else:
            up, dn = vertical(c)
        sides = (load(c, 1, 0) + load(c, -1, 0)) + (load(c, 0, 1) + load(c, 0, -1))
        out.append(
            BASE[c] * load(c, 0, 0) + SIDE[c] * sides + UPC[c] * up + DNC[c] * dn + coupled[c]
        )
    return out


def kernel(
    sizes,
    u_hbm, t_hbm, m_hbm, lvl_ref, path_ref,
    uo_ref, to_ref,
    A, B, F, UE, FE, ZS, ZR, SS, SR, PS, PR,
    TA, MA, TB, TC, KB, GX, GY, GD, LXB, LYD,
    SA, SB, SK, SGX, SGY, SGD, SGB, SL, SM, LO, LL, MM,
    in_sem, us_sem, ur_sem, zs_sem, zr_sem, ss_sem, sr_sem, ps_sem, pr_sem,
    bs_sem, br_sem,
):
    nx, ny = sizes
    gx, gy, gz = lax.axis_index("gx"), lax.axis_index("gy"), lax.axis_index("gz")
    other = 1 - gz

    def dev(dx, dy, z):
        return (lax.rem(gx + dx + nx, nx), lax.rem(gy + dy + ny, ny), z)

    loads = [
        pltpu.make_async_copy(u_hbm, A.at[:, 2:10, 8:24], in_sem.at[0]),
        pltpu.make_async_copy(t_hbm, TA.at[2:10, 8:40], in_sem.at[1]),
        pltpu.make_async_copy(m_hbm, MA.at[2:10, 8:40], in_sem.at[2]),
    ]
    for copy in loads:
        copy.start()

    barrier = pltpu.get_barrier_semaphore()
    for dx in (-1, 0, 1):
        for dy in (-1, 0, 1):
            for z in (gz, other):
                if dx == 0 and dy == 0 and z is gz:
                    continue
                pl.semaphore_signal(
                    barrier, inc=1, device_id=dev(dx, dy, z), device_id_type=MESH
                )

    sent = []

    def send(src, dst, s_sem, r_sem, target):
        copy = pltpu.make_async_remote_copy(
            src_ref=src, dst_ref=dst, send_sem=s_sem, recv_sem=r_sem,
            device_id=target, device_id_type=MESH,
        )
        copy.start()
        sent.append(copy)

    def arrive(dst, s_sem, r_sem):
        pltpu.make_async_remote_copy(
            src_ref=dst, dst_ref=dst, send_sem=s_sem, recv_sem=r_sem,
            device_id=dev(1, 0, gz), device_id_type=MESH,
        ).wait_recv()

    def vapor_slots(X):
        slots = [X.at[:, 0:2, 8:24], X.at[:, 10:12, 8:24], X.at[:, 2:10, 0:8], X.at[:, 2:10, 24:32]]
        for xi in (1, 10):
            for row in (0, 24):
                slots.append(X.at[:, xi:xi + 1, row:row + 8])
        return slots

    def vapor_sources(own):
        sources = [own(6, 2, 0, 16), own(0, 2, 0, 16), own(0, 8, 8, 8), own(0, 8, 0, 8)]
        for x in (7, 0):
            for y in (8, 0):
                sources.append(own(x, 1, y, 8))
        return sources

    vapor_targets = [(1, 0), (-1, 0), (0, 1), (0, -1), (1, 1), (1, -1), (-1, 1), (-1, -1)]

    def send_vapor(step, own, X):
        slots, sources = vapor_slots(X), vapor_sources(own)
        for n in (0, 1, 4, 5, 6, 7, 2, 3):
            send(sources[n], slots[n], us_sem.at[step, n], ur_sem.at[step, n],
                 dev(*vapor_targets[n], gz))

    def await_vapor(step, X):
        slots = vapor_slots(X)
        for n in range(8):
            arrive(slots[n], us_sem.at[step, n], ur_sem.at[step, n])

    lane8 = iota((8, 128), 1)
    sub8 = iota((8, 128), 0)

    def pack_z(step, X):
        shift = jnp.where(gz == 0, 2, 0)
        turned = lax.rem(lane8 + shift, 128) // 2
        for half in range(2):
            acc = jnp.zeros((8, 128), F32)
            for k in range(64 if half == 0 else 32):
                n = half * 64 + k
                c, x, yt = n // 16, (n // 2) % 8, n % 2
                v = X[c, x + 2, 8 + 8 * yt:16 + 8 * yt, :]
                if k:
                    v = pltpu.roll(v, 2 * k, 1)
                acc = jnp.where(turned == k, v, acc)
            ZS[step, half] = acc

    z_targets = [(0, 0), (1, 0), (-1, 0), (0, 1), (0, -1)]

    def send_z(step):
        for n in range(5):
            send(ZS.at[step], ZR.at[step, n], zs_sem.at[step, n], zr_sem.at[step, n],
                 dev(*z_targets[n], other))

    def await_z(step):
        for n in range(5):
            arrive(ZR.at[step, n], zs_sem.at[step, n], zr_sem.at[step, n])

    edge_keep = lax.rem(lane8 + 2 * gz, 128) < 2

    def flag(cond):
        return jnp.where(cond, 1.0, 0.0)

    def rim_flags():
        return jnp.where(sub8 < 4, flag(gy < ny - 1), flag(gy > 0)) > 0.5

    def unpack_z(step):
        def tile(slot, c, x, yt):
            n = c * 16 + x * 2 + yt
            v = ZR[step, slot, n // 64]
            k = 2 * (n % 64)
            if k:
                v = pltpu.roll(v, 128 - k, 1)
            return jnp.where(edge_keep, v, 0.0)

        for c in range(6):
            for yt in range(2):
                rows = slice(8 + 8 * yt, 16 + 8 * yt)
                for x in range(8):
                    UE[c, x + 1, rows, :] = tile(0, c, x, yt)
                UE[c, 0, rows, :] = tile(1, c, 7, yt)
                UE[c, 9, rows, :] = tile(2, c, 0, yt)
            for x in range(8):
                low, high = tile(3, c, x, 1), tile(4, c, x, 0)
                rim = jnp.where(sub8 < 4, high, low)
                UE[c, x + 1, 0:8, :] = rim
                UE[c, x + 1, 24:32, :] = rim

    def clear_outside(X):
        @pl.when(gx == 0)
        def _():
            X[:, 0:2] = jnp.zeros((6, 2, 32, 128), F32)
            UE[:, 0:1] = jnp.zeros((6, 1, 32, 128), F32)

        @pl.when(gx == nx - 1)
        def _():
            X[:, 10:12] = jnp.zeros((6, 2, 32, 128), F32)
            UE[:, 9:10] = jnp.zeros((6, 1, 32, 128), F32)

        rim_valid = rim_flags()

        @pl.loop(1, 11, unroll=5)
        def _(xi):
            for c in range(6):
                rim = jnp.where(sub8 < 4, X[c, xi, 24:32, :], X[c, xi, 0:8, :])
                rim = jnp.where(rim_valid, rim, 0.0)
                X[c, xi, 0:8, :] = rim
                X[c, xi, 24:32, :] = rim

        @pl.when((gy == 0) | (gy == ny - 1))
        def _():
            @pl.loop(0, 10, unroll=2)
            def _(xi):
                for c in range(6):
                    rim = jnp.where(rim_valid, UE[c, xi, 0:8, :], 0.0)
                    UE[c, xi, 0:8, :] = rim
                    UE[c, xi, 24:32, :] = rim

    def advance(X, emit):
        rim_rows = rim_flags()
        lane16 = iota((16, 128), 1)
        edge_lane = jnp.where(gz == 0, 0, 127)

        @pl.loop(0, 10, unroll=2)
        def _(i):
            xi = i + 1

            def load(c, dx, dy):
                return X[c, xi + dx, 8 + dy:24 + dy, :]

            new = forward_euler(load, lambda c: UE[c, i, 8:24, :])
            for c in range(6):
                F[c, i, 8:24, :] = new[c]

        @pl.loop(0, 8, unroll=2)
        def _(x):
            def load_rim(c, dx, dy):
                start = {0: 0, 1: 1, -1: 23}[dy]
                return X[c, x + 2 + dx, start:start + 8, :]

            new = forward_euler(load_rim, lambda c: UE[c, x + 1, 0:8, :])
            for c in range(6):
                rim = jnp.where(rim_rows, new[c], 0.0)
                F[c, x + 1, 0:8, :] = rim
                F[c, x + 1, 24:32, :] = rim

            def load_edge(c, dx, dy):
                return UE[c, x + 1 + dx, 8 + dy:24 + dy, :]

            new = forward_euler(load_edge, lambda c: X[c, x + 2, 8:24, :])
            for c in range(6):
                FE[c, x] = jnp.where(lane16 == edge_lane, new[c], 0.0)

        @pl.when(gx == 0)
        def _():
            F[:, 0:1] = jnp.zeros((6, 1, 32, 128), F32)

        @pl.when(gx == nx - 1)
        def _():
            F[:, 9:10] = jnp.zeros((6, 1, 32, 128), F32)

        @pl.loop(0, 8, unroll=2)
        def _(x):
            def load(c, dx, dy):
                return F[c, x + 1 + dx, 8 + dy:24 + dy, :]

            new = forward_euler(load, lambda c: FE[c, x])
            for c in range(6):
                emit(c, x, 0.5 * (X[c, x + 2, 8:24, :] + new[c]))

    row_first = gx * 16 - 8
    col_first = gy * 32 - 32
    rows_all, cols_all = nx * 16, ny * 32

    def gauss(cells, centre):
        d = (cells.astype(F32) - centre.astype(F32)) / 6.0
        return jnp.exp(-(d * d))

    def prepare():
        col = col_first + lane8
        col_in = (col >= 0) & (col < cols_all) & (lane8 < 96)
        depth = jnp.exp(-(sub8.astype(F32)) / 4.0)
        for sub in range(4):
            a, b = path_ref[0, sub], path_ref[1, sub]
            profile = LASER_POWER * depth * gauss(col, b)

            @pl.loop(0, 32, unroll=8)
            def _(r):
                along = gauss(jnp.full((8, 128), row_first + r, jnp.int32), a)
                SL[sub, pl.ds(pl.multiple_of(r * 8, 8), 8), :] = profile * along

            c48 = gy * 32 - 8 + iota((48, 128), 0)
            d48 = jnp.exp(-(iota((48, 128), 1).astype(F32)) / 4.0)
            LYD[sub] = LASER_POWER * d48 * gauss(c48, b)
            for r in range(12):
                cell = jnp.full((8, 128), (gx * 2 + gz) * 8 - 2 + r, jnp.int32)
                LXB[sub * 12 + r] = gauss(cell, a)

        @pl.loop(0, 32, unroll=8)
        def _(r):
            row = row_first + r
            row_in = flag((row >= 0) & (row < rows_all))
            SM[pl.ds(pl.multiple_of(r * 8, 8), 8), :] = jnp.where(col_in, row_in, 0.0)

        level = jnp.concatenate(
            [lvl_ref[...].astype(F32), jnp.zeros((8, 112), F32)], axis=1)
        SS[4] = level
        eye = jnp.where(iota((16, 128), 0) == iota((16, 128), 1), 1.0, 0.0)
        LO[...] = nt(eye, jnp.concatenate([level, jnp.zeros((120, 128), F32)], axis=0))

    def pack_surface():
        pick = jnp.where(sub8 == lane8, 1.0, 0.0)
        for half in range(2):
            t = TA[2 + 4 * half:6 + 4 * half, 8:40, :].reshape(128, 128)
            m = MA[2 + 4 * half:6 + 4 * half, 8:40, :].reshape(128, 128).astype(F32)
            SS[half] = nt(pick, t)
            SS[2 + half] = nt(pick, m)

    own_slot = (1 + gz) * 3 + 1

    def send_surface():
        for near in (True, False):
            tx = 0 if near else 2 * gz - 1
            block = 1 + gz if near else 3 - 3 * gz
            for ty in (-1, 0, 1):
                for z in (gz, other):
                    if near and ty == 0 and z is gz:
                        continue
                    slot = block * 3 + 1 - ty
                    same = 1 if z is gz else 0
                    n = (6 if near else 0) + (ty + 1) * 2 + same
                    send(SS, SR.at[slot], ss_sem.at[n], sr_sem.at[slot], dev(tx, ty, z))

    def await_surface():
        for slot in range(12):
            if slot in (4, 7):
                @pl.when(own_slot != slot)
                def _():
                    arrive(SR.at[slot], ss_sem.at[0], sr_sem.at[slot])
            else:
                arrive(SR.at[slot], ss_sem.at[0], sr_sem.at[slot])

    def assemble_surface():
        SK[0:8, :] = jnp.zeros((8, 128), F32)
        SK[264:272, :] = jnp.zeros((8, 128), F32)
        SA[0:8, :] = jnp.zeros((8, 128), F32)
        SA[264:272, :] = jnp.zeros((8, 128), F32)
        SB[0:8, :] = jnp.zeros((8, 128), F32)
        SB[264:272, :] = jnp.zeros((8, 128), F32)
        SGX[0:8, :] = jnp.zeros((8, 128), F32)

        def merged(rb, x, first):
            parts = []
            for cb in range(3):
                v = SR[rb * 3 + cb, first + x // 4]
                shift = (32 * cb - 32 * (x % 4)) % 128
                parts.append(pltpu.roll(v, shift, 1) if shift else v)
            return jnp.where(lane8 < 32, parts[0], jnp.where(lane8 < 64, parts[1], parts[2]))

        @pl.loop(0, 4)
        def _(rb):
            for x in range(8):
                at = pl.multiple_of(rb * 64 + x * 8, 8)
                mask = SM[pl.ds(at, 8), :] > 0.5
                phase = merged(rb, x, 2)
                k = jnp.where(phase < 0.5, 0.04, jnp.where(phase < 1.5, 0.15, 0.09))
                SK[pl.ds(at + 8, 8), :] = jnp.where(mask, k, 0.0)
                SA[pl.ds(at + 8, 8), :] = jnp.where(mask, merged(rb, x, 0), 0.0)

        @pl.loop(0, 32, unroll=8)
        def _(r):
            at = pl.multiple_of(r * 8, 8)
            k = SK[pl.ds(at + 8, 8), :]
            SGX[pl.ds(at + 8, 8), :] = 0.5 * (k + SK[pl.ds(at + 16, 8), :])
            SGY[pl.ds(at, 8), :] = 0.5 * (k + pltpu.roll(k, 127, 1))
            SGD[pl.ds(at, 8), :] = jnp.where(sub8 == 7, 0.0, 0.5 * (k + pltpu.roll(k, 7, 0)))
            SGB[pl.ds(at, 8), :] = jnp.where(sub8 == 0, 0.5 * k, 0.0)

        blocks = []
        for rb in (0, 1, 3):
            acc = SR[rb * 3, 4]
            for cb in (1, 2):
                acc = acc + pltpu.roll(SR[rb * 3 + cb, 4], 16 * cb, 1)
            blocks.append(acc)
        blocks.append(jnp.zeros((104, 128), F32))
        eye = jnp.where(iota((48, 128), 0) == iota((48, 128), 1), 1.0, 0.0)
        LL[...] = nt(eye, jnp.concatenate(blocks, axis=0))

    def surface_substep(sub, src, dst, fine_pressure):
        for chunk in range(4):
            base = chunk * 64
            t = src[base + 8:base + 72, :]
            g = SGX[base + 8:base + 72, :]
            change = g * (src[base + 16:base + 80, :] - t) - SGX[base:base + 64, :] * (
                t - src[base:base + 64, :])
            flow = SGY[base:base + 64, :] * (pltpu.roll(t, 127, 1) - t)
            change = change + (flow - pltpu.roll(flow, 1, 1))
            t3 = t.reshape(8, 8, 128)
            gd = SGD[base:base + 64, :].reshape(8, 8, 128)
            flow3 = gd * (pltpu.roll(t3, 7, 1) - t3)
            change = change + (flow3 - pltpu.roll(flow3, 1, 1)).reshape(64, 128)
            change = change - SGB[base:base + 64, :] * t + SL[sub, base:base + 64, :]
            dst[base + 8:base + 72, :] = (t + change) * SM[base:base + 64, :]
        top = src[pl.ds(8, 32, stride=8), :]
        cooling = LATENT_HEAT * softplus(top - 1.0 - 0.5 * fine_pressure)
        cooling = cooling * SM[pl.ds(0, 32, stride=8), :]
        dst[pl.ds(8, 32, stride=8), :] = dst[pl.ds(8, 32, stride=8), :] - cooling

    def pressures(step, X, at_x, at_y):
        lane16 = iota((16, 128), 1)
        height = (lane16 + gz * 128).astype(F32)
        acc = jnp.zeros((16, 128), F32)
        for x in range(8):
            v = X[5, x + at_x, at_y:at_y + 16, :]
            hit = height == LO[:, x:x + 1]
            s = jnp.sum(jnp.where(hit, v, 0.0), axis=1, keepdims=True)
            acc = jnp.where(lane16 == x, s, acc)
        PS[step] = acc

        @pl.when(gz == 0)
        def _():
            PR[step, 4] = acc

    p_targets = [(tx, ty, s) for tx in (-1, 0, 1) for ty in (-1, 0, 1) for s in (0, 1)
                 if (tx, ty, s) != (0, 0, 1)]

    def p_copy(step, n):
        tx, ty, s = p_targets[n]
        slot = (1 - tx) * 3 + 1 - ty
        return pltpu.make_async_remote_copy(
            src_ref=PS.at[step], dst_ref=PR.at[step, slot], send_sem=ps_sem.at[step, n],
            recv_sem=pr_sem.at[step, slot], device_id=dev(tx, ty, gz if s else other),
            device_id_type=MESH)

    def send_pressures(step):
        @pl.when(gz == 0)
        def _():
            for n in range(17):
                p_copy(step, n).start()

    def await_pressures(step):
        for slot in range(9):
            if slot == 4:
                @pl.when(gz == 1)
                def _():
                    arrive(PR.at[step, slot], ps_sem.at[step, 0], pr_sem.at[step, slot])
            else:
                arrive(PR.at[step, slot], ps_sem.at[step, 0], pr_sem.at[step, slot])

    def coarse_pressure(step):
        blocks = []
        for by in range(3):
            acc = PR[step, by]
            for bx in (1, 2):
                acc = acc + pltpu.roll(PR[step, bx * 3 + by], 8 * bx, 1)
            blocks.append(acc)
        return jnp.concatenate(blocks, axis=0)

    def fine_from_coarse(coarse):
        rows = jnp.where(iota((32, 128), 1) == (iota((32, 128), 0) + 8) // 2, 1.0, 0.0)
        cols = jnp.where(iota((128, 128), 0) == iota((128, 128), 1) // 2, 1.0, 0.0)
        padded = jnp.concatenate([coarse, jnp.zeros((80, 128), F32)], axis=0)
        return nn(nt(rows, padded), cols)

    def mass_from_surface(ref, coarse):
        top = jnp.concatenate(
            [ref[pl.ds(8, 32, stride=8), :], jnp.zeros((96, 128), F32)], axis=0)
        cols = jnp.where(iota((48, 128), 0) == iota((48, 128), 1) // 2, 0.25, 0.0)
        i = iota((128, 128), 0)
        rows = jnp.where((iota((128, 128), 1) == (i + 8) // 2) & (i < 32), 1.0, 0.0)
        surface = nn(nt(cols, top), rows)
        mass = softplus(surface - 1.0 - 0.5 * coarse)
        y = gy * 16 - 16 + iota((48, 128), 0)
        x = gx * 8 - 8 + iota((48, 128), 1)
        inside = (y >= 0) & (y < ny * 16) & (x >= 0) & (x < nx * 8)
        return jnp.where(inside, mass, 0.0)

    def with_rim(v):
        rim = jnp.where(sub8 < 4, v[32:40], v[8:16])
        return jnp.concatenate([rim, v[16:32], rim], axis=0)

    row_block = gx * 2 + gz
    dn_row, up_row = -(1 - gz), gz

    def bulk_slots(X):
        slots = [X.at[0:2, 8:40], X.at[10:12, 8:40], X.at[2:10, 0:8], X.at[2:10, 40:48]]
        for r in (1, 10):
            for c in (0, 40):
                slots.append(X.at[r:r + 1, c:c + 8])
        return slots

    def bulk_sources(X, r0, c0):
        def own(r, nr, c, nc):
            return X.at[r0 + r:r0 + r + nr, c0 + c:c0 + c + nc]

        sources = [own(6, 2, 0, 32), own(0, 2, 0, 32), own(0, 8, 24, 8), own(0, 8, 0, 8)]
        for r in (7, 0):
            for c in (24, 0):
                sources.append(own(r, 1, c, 8))
        return sources

    def send_bulk(kind, X, r0, c0, D):
        targets = [dev(up_row, 0, other), dev(dn_row, 0, other), dev(0, 1, gz), dev(0, -1, gz)]
        for tx in (up_row, dn_row):
            for ty in (1, -1):
                targets.append(dev(tx, ty, other))
        sources, slots = bulk_sources(X, r0, c0), bulk_slots(D)
        for n in range(8):
            send(sources[n], slots[n], bs_sem.at[kind, n], br_sem.at[kind, n], targets[n])

    def await_bulk(kind, D):
        slots = bulk_slots(D)
        for n in range(8):
            arrive(slots[n], bs_sem.at[kind, n], br_sem.at[kind, n])

    def clear_bulk(X):
        @pl.when(row_block == 0)
        def _():
            X[0:2] = jnp.zeros((2, 48, 128), F32)

        @pl.when(row_block == 2 * nx - 1)
        def _():
            X[10:12] = jnp.zeros((2, 48, 128), F32)

        @pl.when(gy == 0)
        def _():
            X[:, 0:8] = jnp.zeros((12, 8, 128), F32)

        @pl.when(gy == ny - 1)
        def _():
            X[:, 40:48] = jnp.zeros((12, 8, 128), F32)

    def prepare_bulk():
        @pl.loop(0, 12, unroll=6)
        def _(r):
            m = MA[r]
            KB[r] = jnp.where(m == 0, 0.04, jnp.where(m == 1, 0.15, 0.09))

        clear_bulk(KB)

        @pl.loop(0, 11, unroll=11)
        def _(r):
            k = KB[r]
            GX[r] = 0.5 * (k + KB[r + 1])
            GY[r] = 0.5 * (k + pltpu.roll(k, 47, 0))
            last = iota((48, 128), 1) == 127
            GD[r] = 0.5 * (k + jnp.where(last, 0.0, pltpu.roll(k, 127, 1)))

    def bulk_substep(sub, src, dst, low, high, own_only=False):
        col = gy * 32 - 8 + iota((48, 128), 0)
        col_in = jnp.where((col >= 0) & (col < cols_all), 1.0, 0.0)
        last = iota((48, 128), 1) == 127

        @pl.loop(low, high, unroll=(high - low) // 2)
        def _(r):
            t = src[r]
            change = GX[r] * (src[r + 1] - t) - GX[r - 1] * (t - src[r - 1])
            flow = GY[r] * (pltpu.roll(t, 47, 0) - t)
            change = change + (flow - pltpu.roll(flow, 1, 0))
            flow = GD[r] * (jnp.where(last, 0.0, pltpu.roll(t, 127, 1)) - t)
            change = change + (flow - pltpu.roll(flow, 1, 1))
            along = LXB[sub * 12 + r]
            laser = LYD[sub] * jnp.concatenate([along] * 6, axis=0)
            row = row_block * 8 - 2 + r
            row_in = jnp.where((row >= 0) & (row < rows_all), 1.0, 0.0)
            new = (t + change + laser) * (col_in * row_in)
            if own_only:
                dst[r, 8:40, :] = new[8:40]
            else:
                dst[r] = new

    pl.semaphore_wait(barrier, 17)
    send_vapor(0, lambda x, n, y, m: u_hbm.at[:, x:x + n, y:y + m], A)
    loads[0].wait()
    pack_z(0, A)
    send_z(0)
    prepare()
    loads[1].wait()
    loads[2].wait()
    pack_surface()
    SR[own_slot] = SS[...]
    send_surface()
    send_bulk(0, t_hbm, 0, 0, TA)
    send_bulk(1, m_hbm, 0, 0, MA)

    await_z(0)
    unpack_z(0)
    await_vapor(0, A)
    clear_outside(A)

    def to_b(c, x, v):
        B[c, x + 2, 8:24, :] = v

    advance(A, to_b)
    first = len(sent)
    send_vapor(1, lambda x, n, y, m: B.at[:, x + 2:x + 2 + n, y + 8:y + 8 + m], B)
    sent_b = sent[first:]
    del sent[first:]
    pressures(0, B, 2, 8)
    send_pressures(0)
    pack_z(1, B)
    send_z(1)

    await_surface()
    assemble_surface()
    await_bulk(0, TA)
    await_bulk(1, MA)
    clear_bulk(TA)
    prepare_bulk()
    bulk_substep(0, TA, TC, 1, 11)
    bulk_substep(1, TC, TB, 2, 10, True)
    send_bulk(2, TB, 2, 8, TB)

    await_pressures(0)
    coarse = coarse_pressure(0)
    fine = fine_from_coarse(coarse)
    surface_substep(0, SA, SB, fine)
    surface_substep(1, SB, SA, fine)
    MM[...] = with_rim(mass_from_surface(SA, coarse))
    LL[0:32, :] = with_rim(LL[...])

    await_z(1)
    unpack_z(1)
    await_vapor(1, B)
    clear_outside(B)
    for copy in sent_b:
        copy.wait_send()
    lane32 = iota((32, 128), 1)
    height = (lane32 + gz * 128).astype(F32)
    height_edge = (lane32 + other * 128).astype(F32)
    for xi in range(12):
        mass = jnp.broadcast_to(MM[:, xi + 6:xi + 7], (32, 128))
        level = jnp.broadcast_to(LL[0:32, xi + 6:xi + 7], (32, 128))
        field = jnp.where(height == level, mass, 0.0)
        B[0, xi] = B[0, xi] + 0.5 * field
        B[4, xi] = B[4, xi] + 0.4 * field
        B[5, xi] = B[5, xi] + 0.6 * field
        if 1 <= xi <= 10:
            @pl.when(gz == 1)
            def _():
                edge = jnp.where((height_edge == level) & (lane32 >= 126), mass, 0.0)
                UE[0, xi - 1] = UE[0, xi - 1] + 0.5 * edge
                UE[4, xi - 1] = UE[4, xi - 1] + 0.4 * edge
                UE[5, xi - 1] = UE[5, xi - 1] + 0.6 * edge

    def to_out(c, x, v):
        uo_ref[c, x] = v

    advance(B, to_out)
    pressures(1, uo_ref, 0, 0)
    send_pressures(1)

    await_bulk(2, TB)
    clear_bulk(TB)
    bulk_substep(2, TB, TC, 1, 11)
    bulk_substep(3, TC, TA, 2, 10, True)

    await_pressures(1)
    coarse = coarse_pressure(1)
    fine = fine_from_coarse(coarse)
    surface_substep(2, SA, SB, fine)
    surface_substep(3, SB, SA, fine)
    mass_now = mass_from_surface(SA, coarse)[16:32]
    lane16 = iota((16, 128), 1)
    height = (lane16 + gz * 128).astype(F32)
    for x in range(8):
        mass = jnp.broadcast_to(mass_now[:, x + 8:x + 9], (16, 128))
        level = jnp.broadcast_to(LO[:, x:x + 1], (16, 128))
        field = jnp.where(height == level, mass, 0.0)
        uo_ref[0, x] = uo_ref[0, x] + 0.5 * field
        uo_ref[4, x] = uo_ref[4, x] + 0.4 * field
        uo_ref[5, x] = uo_ref[5, x] + 0.6 * field

    eye = jnp.where(iota((128, 128), 0) == iota((128, 128), 1), 1.0, 0.0)
    for half in range(2):
        acc = jnp.zeros((8, 128), F32)
        for i in range(4):
            at = pl.multiple_of((9 + gz * 8 + 4 * half + i) * 8, 8)
            v = SA[pl.ds(at, 8), :]
            shift = (32 * i - 32) % 128
            v = pltpu.roll(v, shift, 1) if shift else v
            acc = jnp.where(lane8 // 32 == i, v, acc)
        turned = nt(eye, jnp.concatenate([acc, jnp.zeros((120, 128), F32)], axis=0))
        turned = turned.reshape(4, 32, 128)
        shallow = iota((4, 32, 128), 2) < 4
        deep = TA[2 + 4 * half:6 + 4 * half, 8:40, :]
        to_ref[4 * half:4 * half + 4] = jnp.where(shallow, turned, deep)

    for copy in sent:
        copy.wait_send()

    @pl.when(gz == 0)
    def _():
        for step in range(2):
            for n in range(17):
                p_copy(step, n).wait_send()


def solution(mesh):
    sizes = (mesh.shape["gx"], mesh.shape["gy"])

    def shards(vapor, thermal, phase, level, path):
        anywhere = pl.BlockSpec(memory_space=pl.ANY)
        vmem = pl.BlockSpec(memory_space=pltpu.VMEM)
        dma = pltpu.SemaphoreType.DMA
        row = (12, 48, 128)
        gas, temp = pl.pallas_call(
            functools.partial(kernel, sizes),
            out_shape=(
                pltpu.VMEM((6, 8, 16, 128), F32),
                pltpu.VMEM((8, 32, 128), F32),
            ),
            in_specs=[anywhere, anywhere, anywhere, vmem, pl.BlockSpec(memory_space=pltpu.SMEM)],
            out_specs=(vmem, vmem),
            scratch_shapes=[
                pltpu.VMEM((6, 12, 32, 128), F32), pltpu.VMEM((6, 12, 32, 128), F32),
                pltpu.VMEM((6, 10, 32, 128), F32), pltpu.VMEM((6, 10, 32, 128), F32),
                pltpu.VMEM((6, 8, 16, 128), F32),
                pltpu.VMEM((2, 2, 8, 128), F32), pltpu.VMEM((2, 5, 2, 8, 128), F32),
                pltpu.VMEM((5, 8, 128), F32), pltpu.VMEM((12, 5, 8, 128), F32),
                pltpu.VMEM((2, 16, 128), F32), pltpu.VMEM((2, 9, 16, 128), F32),
                pltpu.VMEM(row, F32), pltpu.VMEM(row, jnp.int32), pltpu.VMEM(row, F32),
                pltpu.VMEM(row, F32), pltpu.VMEM(row, F32), pltpu.VMEM(row, F32),
                pltpu.VMEM(row, F32), pltpu.VMEM(row, F32),
                pltpu.VMEM((48, 8, 128), F32), pltpu.VMEM((4, 48, 128), F32),
                pltpu.VMEM((272, 128), F32), pltpu.VMEM((272, 128), F32),
                pltpu.VMEM((272, 128), F32), pltpu.VMEM((264, 128), F32),
                pltpu.VMEM((256, 128), F32), pltpu.VMEM((256, 128), F32),
                pltpu.VMEM((256, 128), F32), pltpu.VMEM((4, 256, 128), F32),
                pltpu.VMEM((256, 128), F32), pltpu.VMEM((16, 128), F32),
                pltpu.VMEM((48, 128), F32), pltpu.VMEM((32, 128), F32),
                dma((3,)), dma((2, 8)), dma((2, 8)), dma((2, 5)), dma((2, 5)),
                dma((12,)), dma((12,)), dma((2, 17)), dma((2, 9)),
                dma((3, 8)), dma((3, 8)),
            ],
            compiler_params=pltpu.CompilerParams(collective_id=0, has_side_effects=True),
        )(vapor, jnp.transpose(thermal, (1, 2, 0)), jnp.transpose(phase, (1, 2, 0)), level, path.T)
        return gas, jnp.transpose(temp, (2, 0, 1))

    return jax.shard_map(
        shards,
        mesh=mesh,
        in_specs=(
            P(None, "gx", "gy", "gz"),
            P(None, ("gx", "gz"), "gy"),
            P(None, ("gx", "gz"), "gy"),
            P("gx", "gy"),
            P(),
        ),
        out_specs=(P(None, "gx", "gy", "gz"), P(None, ("gx", "gz"), "gy")),
        check_vma=False,
    )
```

```python
import functools
import math

import jax
import jax.numpy as jnp
from jax import lax
from jax.experimental import pallas as pl
from jax.experimental.pallas import tpu as pltpu
from jax.sharding import PartitionSpec as P

MESH = pl.DeviceIdType.MESH
HI = lax.Precision.HIGHEST
F32 = jnp.float32

NU = (0.2, 0.1, 0.15, 0.15, 0.15, 0.2)
BASE = tuple(1.0 - 1.8 * n for n in NU)
SIDE = tuple(0.3 * n for n in NU)
UPC = tuple(0.3 * n - 0.075 for n in NU)
DNC = tuple(0.3 * n + 0.075 for n in NU)
LASER_POWER = 3.0
LATENT_HEAT = 0.3


def softplus(x):
    return jnp.maximum(x, 0.0) + jnp.log1p(jnp.exp(-jnp.abs(x)))


def nt(a, b, precision=HI):
    return lax.dot_general(
        a, b, (((1,), (1,)), ((), ())), precision=precision, preferred_element_type=F32
    )


def nn(a, b):
    return lax.dot_general(
        a, b, (((1,), (0,)), ((), ())), precision=HI, preferred_element_type=F32
    )


def iota(shape, dim):
    return lax.broadcasted_iota(jnp.int32, shape, dim)


def forward_euler(load, edge):
    def vertical(c):
        center, other = load(c, 0, 0), edge(c)
        lane = iota(center.shape, 1)
        up = pltpu.roll(jnp.where(lane == 0, other, center), 127, 1)
        down = pltpu.roll(jnp.where(lane == 127, other, center), 1, 1)
        return up, down

    u_e, u_w = load(2, 1, 0), load(2, -1, 0)
    v_n, v_s = load(3, 0, 1), load(3, 0, -1)
    w_up, w_dn = vertical(4)
    spread = (u_e - u_w) + (v_n - v_s) + (w_up - w_dn)
    p_e, p_w, p_n, p_s = load(5, 1, 0), load(5, -1, 0), load(5, 0, 1), load(5, 0, -1)
    p_up, p_dn = vertical(5)
    coupled = (
        -0.045 * spread,
        -0.105 * spread,
        -0.15 * (p_e - p_w),
        -0.15 * (p_n - p_s),
        -0.15 * (p_up - p_dn),
        -0.15 * spread,
    )
    out = []
    for c in range(6):
        if c == 4:
            up, dn = w_up, w_dn
        elif c == 5:
            up, dn = p_up, p_dn
        else:
            up, dn = vertical(c)
        sides = (load(c, 1, 0) + load(c, -1, 0)) + (load(c, 0, 1) + load(c, 0, -1))
        out.append(
            BASE[c] * load(c, 0, 0) + SIDE[c] * sides + UPC[c] * up + DNC[c] * dn + coupled[c]
        )
    return out


def kernel(
    sizes,
    u_hbm, t_hbm, m_hbm, lvl_ref, path_ref,
    uo_ref, to_ref,
    A, B, F, UE, FE, ZS, ZR, SS, SR, PS, PR,
    TA, MA, TB, TC, KB, GX, GY, GD, LXB, LYD,
    SA, SB, SK, SGX, SGY, SGD, SGB, SL, SM, LO, LL, MM,
    in_sem, us_sem, ur_sem, zs_sem, zr_sem, ss_sem, sr_sem, ps_sem, pr_sem,
    bs_sem, br_sem,
):
    nx, ny = sizes
    gx, gy, gz = lax.axis_index("gx"), lax.axis_index("gy"), lax.axis_index("gz")
    other = 1 - gz

    def dev(dx, dy, z):
        return (lax.rem(gx + dx + nx, nx), lax.rem(gy + dy + ny, ny), z)

    loads = [
        pltpu.make_async_copy(u_hbm, A.at[:, 2:10, 8:24], in_sem.at[0]),
        pltpu.make_async_copy(t_hbm, TA.at[2:10, 8:40], in_sem.at[1]),
        pltpu.make_async_copy(m_hbm, MA.at[2:10, 8:40], in_sem.at[2]),
    ]
    for copy in loads:
        copy.start()

    def exists(dx, dy):
        tests = []
        for at, d, size in ((gx, dx, nx), (gy, dy, ny)):
            if not (isinstance(d, int) and d == 0):
                tests.append((at + d >= 0) & (at + d < size))
        if not tests:
            return None
        return tests[0] if len(tests) == 1 else tests[0] & tests[1]

    def when(cond, body):
        if cond is None:
            body()
        else:
            pl.when(cond)(body)

    SR[...] = jnp.zeros((12, 5, 8, 128), F32)
    PR[...] = jnp.zeros((2, 9, 16, 128), F32)

    barrier = pltpu.get_barrier_semaphore()

    def greet(dx, dy, z):
        when(exists(dx, dy), lambda: pl.semaphore_signal(
            barrier, inc=1, device_id=dev(dx, dy, z), device_id_type=MESH))

    for dx in (-1, 0, 1):
        for dy in (-1, 0, 1):
            for z in (gz, other):
                if not (dx == 0 and dy == 0 and z is gz):
                    greet(dx, dy, z)
    beside_x = 3 - jnp.where(gx == 0, 1, 0) - jnp.where(gx == nx - 1, 1, 0)
    beside_y = 3 - jnp.where(gy == 0, 1, 0) - jnp.where(gy == ny - 1, 1, 0)

    sent = []

    def remote(src, dst, s_sem, r_sem, target):
        return pltpu.make_async_remote_copy(
            src_ref=src, dst_ref=dst, send_sem=s_sem, recv_sem=r_sem,
            device_id=dev(*target), device_id_type=MESH,
        )

    def send(src, dst, s_sem, r_sem, target):
        args = (src, dst, s_sem, r_sem, target)
        cond = exists(target[0], target[1])
        when(cond, lambda: remote(*args).start())
        sent.append((cond, args))

    def drain(items):
        for cond, args in items:
            when(cond, lambda: remote(*args).wait_send())

    def arrive(dst, s_sem, r_sem, dx, dy):
        when(exists(dx, dy), lambda: remote(dst, dst, s_sem, r_sem, (1, 0, gz)).wait_recv())

    def vapor_slots(X):
        slots = [X.at[:, 0:2, 8:24], X.at[:, 10:12, 8:24], X.at[:, 2:10, 6:8], X.at[:, 2:10, 24:26]]
        for xi in (1, 10):
            for row in (7, 24):
                slots.append(X.at[:, xi:xi + 1, row:row + 1])
        return slots

    def vapor_sources(own):
        sources = [own(6, 2, 0, 16), own(0, 2, 0, 16), own(0, 8, 14, 2), own(0, 8, 0, 2)]
        for x in (7, 0):
            for y in (15, 0):
                sources.append(own(x, 1, y, 1))
        return sources

    vapor_targets = [(1, 0), (-1, 0), (0, 1), (0, -1), (1, 1), (1, -1), (-1, 1), (-1, -1)]

    def send_vapor(step, own, X):
        slots, sources = vapor_slots(X), vapor_sources(own)
        for n in (0, 1, 4, 5, 6, 7, 2, 3):
            send(sources[n], slots[n], us_sem.at[step, n], ur_sem.at[step, n],
                 (*vapor_targets[n], gz))

    def await_vapor(step, X):
        slots = vapor_slots(X)
        for n in range(8):
            arrive(slots[n], us_sem.at[step, n], ur_sem.at[step, n],
                   -vapor_targets[n][0], -vapor_targets[n][1])

    lane8 = iota((8, 128), 1)
    sub8 = iota((8, 128), 0)

    def pack_z(step, X):
        shift = jnp.where(gz == 0, 2, 0)
        turned = lax.rem(lane8 + shift, 128) // 2
        for half in range(2):
            acc = jnp.zeros((8, 128), F32)
            for k in range(64 if half == 0 else 32):
                n = half * 64 + k
                c, x, yt = n // 16, (n // 2) % 8, n % 2
                v = X[c, x + 2, 8 + 8 * yt:16 + 8 * yt, :]
                if k:
                    v = pltpu.roll(v, 2 * k, 1)
                acc = jnp.where(turned == k, v, acc)
            ZS[step, half] = acc

    z_targets = [(0, 0), (1, 0), (-1, 0), (0, 1), (0, -1)]

    def send_z(step):
        for n in range(5):
            send(ZS.at[step], ZR.at[step, n], zs_sem.at[step, n], zr_sem.at[step, n],
                 (*z_targets[n], other))

    def await_z(step):
        for n in range(5):
            arrive(ZR.at[step, n], zs_sem.at[step, n], zr_sem.at[step, n],
                   -z_targets[n][0], -z_targets[n][1])

    edge_keep = lax.rem(lane8 + 2 * gz, 128) < 2

    def flag(cond):
        return jnp.where(cond, 1.0, 0.0)

    def rim_flags():
        return jnp.where(sub8 < 4, flag(gy < ny - 1), flag(gy > 0)) > 0.5

    def unpack_z(step):
        def tile(slot, c, x, yt):
            n = c * 16 + x * 2 + yt
            v = ZR[step, slot, n // 64]
            k = 2 * (n % 64)
            if k:
                v = pltpu.roll(v, 128 - k, 1)
            return jnp.where(edge_keep, v, 0.0)

        for c in range(6):
            for yt in range(2):
                rows = slice(8 + 8 * yt, 16 + 8 * yt)
                for x in range(8):
                    UE[c, x + 1, rows, :] = tile(0, c, x, yt)
                UE[c, 0, rows, :] = tile(1, c, 7, yt)
                UE[c, 9, rows, :] = tile(2, c, 0, yt)
            for x in range(8):
                low, high = tile(3, c, x, 1), tile(4, c, x, 0)
                rim = jnp.where(sub8 < 4, high, low)
                UE[c, x + 1, 0:8, :] = rim
                UE[c, x + 1, 24:32, :] = rim

    def clear_outside(X):
        @pl.when(gx == 0)
        def _():
            X[:, 0:2] = jnp.zeros((6, 2, 32, 128), F32)
            UE[:, 0:1] = jnp.zeros((6, 1, 32, 128), F32)

        @pl.when(gx == nx - 1)
        def _():
            X[:, 10:12] = jnp.zeros((6, 2, 32, 128), F32)
            UE[:, 9:10] = jnp.zeros((6, 1, 32, 128), F32)

        rim_valid = rim_flags()

        @pl.loop(1, 11, unroll=5)
        def _(xi):
            for c in range(6):
                rim = jnp.where(sub8 < 4, X[c, xi, 24:32, :], X[c, xi, 0:8, :])
                rim = jnp.where(rim_valid, rim, 0.0)
                X[c, xi, 0:8, :] = rim
                X[c, xi, 24:32, :] = rim

        @pl.when((gy == 0) | (gy == ny - 1))
        def _():
            @pl.loop(0, 10, unroll=2)
            def _(xi):
                for c in range(6):
                    rim = jnp.where(rim_valid, UE[c, xi, 0:8, :], 0.0)
                    UE[c, xi, 0:8, :] = rim
                    UE[c, xi, 24:32, :] = rim

    def advance(X, emit):
        rim_rows = rim_flags()
        lane16 = iota((16, 128), 1)
        edge_lane = jnp.where(gz == 0, 0, 127)

        @pl.loop(0, 10, unroll=2)
        def _(i):
            xi = i + 1

            def load(c, dx, dy):
                return X[c, xi + dx, 8 + dy:24 + dy, :]

            new = forward_euler(load, lambda c: UE[c, i, 8:24, :])
            for c in range(6):
                F[c, i, 8:24, :] = new[c]

        @pl.loop(0, 8, unroll=2)
        def _(x):
            def load_rim(c, dx, dy):
                start = {0: 0, 1: 1, -1: 23}[dy]
                return X[c, x + 2 + dx, start:start + 8, :]

            new = forward_euler(load_rim, lambda c: UE[c, x + 1, 0:8, :])
            for c in range(6):
                rim = jnp.where(rim_rows, new[c], 0.0)
                F[c, x + 1, 0:8, :] = rim
                F[c, x + 1, 24:32, :] = rim

            def load_edge(c, dx, dy):
                return UE[c, x + 1 + dx, 8 + dy:24 + dy, :]

            new = forward_euler(load_edge, lambda c: X[c, x + 2, 8:24, :])
            for c in range(6):
                FE[c, x] = jnp.where(lane16 == edge_lane, new[c], 0.0)

        @pl.when(gx == 0)
        def _():
            F[:, 0:1] = jnp.zeros((6, 1, 32, 128), F32)

        @pl.when(gx == nx - 1)
        def _():
            F[:, 9:10] = jnp.zeros((6, 1, 32, 128), F32)

        @pl.loop(0, 8, unroll=2)
        def _(x):
            def load(c, dx, dy):
                return F[c, x + 1 + dx, 8 + dy:24 + dy, :]

            new = forward_euler(load, lambda c: FE[c, x])
            for c in range(6):
                emit(c, x, 0.5 * (X[c, x + 2, 8:24, :] + new[c]))

    row_first = gx * 16 - 8
    col_first = gy * 32 - 32
    rows_all, cols_all = nx * 16, ny * 32

    def gauss(cells, centre):
        d = (cells.astype(F32) - centre.astype(F32)) / 6.0
        return jnp.exp(-(d * d))

    def prepare():
        col = col_first + lane8
        col_in = (col >= 0) & (col < cols_all) & (lane8 < 96)
        depth = jnp.exp(-(sub8.astype(F32)) / 4.0)
        for sub in range(4):
            a, b = path_ref[0, sub], path_ref[1, sub]
            profile = LASER_POWER * depth * gauss(col, b)

            @pl.loop(0, 32, unroll=8)
            def _(r):
                along = gauss(jnp.full((8, 128), row_first + r, jnp.int32), a)
                SL[sub, pl.ds(pl.multiple_of(r * 8, 8), 8), :] = profile * along

            c48 = gy * 32 - 8 + iota((48, 128), 0)
            d48 = jnp.exp(-(iota((48, 128), 1).astype(F32)) / 4.0)
            LYD[sub] = LASER_POWER * d48 * gauss(c48, b)
            for r in range(12):
                cell = jnp.full((8, 128), (gx * 2 + gz) * 8 - 2 + r, jnp.int32)
                LXB[sub * 12 + r] = gauss(cell, a)

        @pl.loop(0, 32, unroll=8)
        def _(r):
            row = row_first + r
            row_in = flag((row >= 0) & (row < rows_all))
            SM[pl.ds(pl.multiple_of(r * 8, 8), 8), :] = jnp.where(col_in, row_in, 0.0)

        level = jnp.concatenate(
            [lvl_ref[...].astype(F32), jnp.zeros((8, 112), F32)], axis=1)
        SS[4] = level
        eye = jnp.where(iota((16, 128), 0) == iota((16, 128), 1), 1.0, 0.0)
        LO[...] = nt(eye, jnp.concatenate([level, jnp.zeros((120, 128), F32)], axis=0))

    def pack_surface():
        pick = jnp.where(sub8 == lane8, 1.0, 0.0)
        for half in range(2):
            t = TA[2 + 4 * half:6 + 4 * half, 8:40, :].reshape(128, 128)
            m = MA[2 + 4 * half:6 + 4 * half, 8:40, :].reshape(128, 128).astype(F32)
            SS[half] = nt(pick, t)
            SS[2 + half] = nt(pick, m)

    own_slot = (1 + gz) * 3 + 1

    def send_surface():
        for near in (True, False):
            tx = 0 if near else 2 * gz - 1
            block = 1 + gz if near else 3 - 3 * gz
            for ty in (-1, 0, 1):
                for z in (gz, other):
                    if near and ty == 0 and z is gz:
                        continue
                    slot = block * 3 + 1 - ty
                    same = 1 if z is gz else 0
                    n = (6 if near else 0) + (ty + 1) * 2 + same
                    send(SS, SR.at[slot], ss_sem.at[n], sr_sem.at[slot], (tx, ty, z))

    def await_surface():
        for slot in range(12):
            if slot in (4, 7):
                @pl.when(own_slot != slot)
                def _():
                    arrive(SR.at[slot], ss_sem.at[0], sr_sem.at[slot], 0, 0)
            else:
                arrive(SR.at[slot], ss_sem.at[0], sr_sem.at[slot],
                       (-1, 0, 0, 1)[slot // 3], slot % 3 - 1)

    def assemble_surface():
        SK[0:8, :] = jnp.zeros((8, 128), F32)
        SK[264:272, :] = jnp.zeros((8, 128), F32)
        SA[0:8, :] = jnp.zeros((8, 128), F32)
        SA[264:272, :] = jnp.zeros((8, 128), F32)
        SB[0:8, :] = jnp.zeros((8, 128), F32)
        SB[264:272, :] = jnp.zeros((8, 128), F32)
        SGX[0:8, :] = jnp.zeros((8, 128), F32)

        def merged(rb, x, first):
            parts = []
            for cb in range(3):
                v = SR[rb * 3 + cb, first + x // 4]
                shift = (32 * cb - 32 * (x % 4)) % 128
                parts.append(pltpu.roll(v, shift, 1) if shift else v)
            return jnp.where(lane8 < 32, parts[0], jnp.where(lane8 < 64, parts[1], parts[2]))

        @pl.loop(0, 4)
        def _(rb):
            for x in range(8):
                at = pl.multiple_of(rb * 64 + x * 8, 8)
                mask = SM[pl.ds(at, 8), :] > 0.5
                phase = merged(rb, x, 2)
                k = jnp.where(phase < 0.5, 0.04, jnp.where(phase < 1.5, 0.15, 0.09))
                SK[pl.ds(at + 8, 8), :] = jnp.where(mask, k, 0.0)
                SA[pl.ds(at + 8, 8), :] = jnp.where(mask, merged(rb, x, 0), 0.0)

        @pl.loop(0, 32, unroll=8)
        def _(r):
            at = pl.multiple_of(r * 8, 8)
            k = SK[pl.ds(at + 8, 8), :]
            SGX[pl.ds(at + 8, 8), :] = 0.5 * (k + SK[pl.ds(at + 16, 8), :])
            SGY[pl.ds(at, 8), :] = 0.5 * (k + pltpu.roll(k, 127, 1))
            SGD[pl.ds(at, 8), :] = jnp.where(sub8 == 7, 0.0, 0.5 * (k + pltpu.roll(k, 7, 0)))
            SGB[pl.ds(at, 8), :] = jnp.where(sub8 == 0, 0.5 * k, 0.0)

        blocks = []
        for rb in (0, 1, 3):
            acc = SR[rb * 3, 4]
            for cb in (1, 2):
                acc = acc + pltpu.roll(SR[rb * 3 + cb, 4], 16 * cb, 1)
            blocks.append(acc)
        blocks.append(jnp.zeros((104, 128), F32))
        eye = jnp.where(iota((48, 128), 0) == iota((48, 128), 1), 1.0, 0.0)
        LL[...] = nt(eye, jnp.concatenate(blocks, axis=0))

    def surface_substep(sub, src, dst, fine_pressure):
        for chunk in range(4):
            base = chunk * 64
            t = src[base + 8:base + 72, :]
            g = SGX[base + 8:base + 72, :]
            change = g * (src[base + 16:base + 80, :] - t) - SGX[base:base + 64, :] * (
                t - src[base:base + 64, :])
            flow = SGY[base:base + 64, :] * (pltpu.roll(t, 127, 1) - t)
            change = change + (flow - pltpu.roll(flow, 1, 1))
            t3 = t.reshape(8, 8, 128)
            gd = SGD[base:base + 64, :].reshape(8, 8, 128)
            flow3 = gd * (pltpu.roll(t3, 7, 1) - t3)
            change = change + (flow3 - pltpu.roll(flow3, 1, 1)).reshape(64, 128)
            change = change - SGB[base:base + 64, :] * t + SL[sub, base:base + 64, :]
            dst[base + 8:base + 72, :] = (t + change) * SM[base:base + 64, :]
        top = src[pl.ds(8, 32, stride=8), :]
        cooling = LATENT_HEAT * softplus(top - 1.0 - 0.5 * fine_pressure)
        cooling = cooling * SM[pl.ds(0, 32, stride=8), :]
        dst[pl.ds(8, 32, stride=8), :] = dst[pl.ds(8, 32, stride=8), :] - cooling

    def pressures(step, X, at_x, at_y):
        lane16 = iota((16, 128), 1)
        height = (lane16 + gz * 128).astype(F32)
        acc = jnp.zeros((16, 128), F32)
        for x in range(8):
            v = X[5, x + at_x, at_y:at_y + 16, :]
            hit = height == LO[:, x:x + 1]
            s = jnp.sum(jnp.where(hit, v, 0.0), axis=1, keepdims=True)
            acc = jnp.where(lane16 == x, s, acc)
        PS[step] = acc

        @pl.when(gz == 0)
        def _():
            PR[step, 4] = acc

    p_targets = [(tx, ty, s) for tx in (-1, 0, 1) for ty in (-1, 0, 1) for s in (0, 1)
                 if (tx, ty, s) != (0, 0, 1)]

    def p_copy(step, n):
        tx, ty, s = p_targets[n]
        slot = (1 - tx) * 3 + 1 - ty
        return pltpu.make_async_remote_copy(
            src_ref=PS.at[step], dst_ref=PR.at[step, slot], send_sem=ps_sem.at[step, n],
            recv_sem=pr_sem.at[step, slot], device_id=dev(tx, ty, gz if s else other),
            device_id_type=MESH)

    def send_pressures(step):
        @pl.when(gz == 0)
        def _():
            for n in range(17):
                when(exists(*p_targets[n][:2]), lambda: p_copy(step, n).start())

    def await_pressures(step):
        for slot in range(9):
            if slot == 4:
                @pl.when(gz == 1)
                def _():
                    arrive(PR.at[step, slot], ps_sem.at[step, 0], pr_sem.at[step, slot], 0, 0)
            else:
                arrive(PR.at[step, slot], ps_sem.at[step, 0], pr_sem.at[step, slot],
                       slot // 3 - 1, slot % 3 - 1)

    def coarse_pressure(step):
        blocks = []
        for by in range(3):
            acc = PR[step, by]
            for bx in (1, 2):
                acc = acc + pltpu.roll(PR[step, bx * 3 + by], 8 * bx, 1)
            blocks.append(acc)
        return jnp.concatenate(blocks, axis=0)

    def fine_from_coarse(coarse):
        rows = jnp.where(iota((32, 128), 1) == (iota((32, 128), 0) + 8) // 2, 1.0, 0.0)
        cols = jnp.where(iota((128, 128), 0) == iota((128, 128), 1) // 2, 1.0, 0.0)
        padded = jnp.concatenate([coarse, jnp.zeros((80, 128), F32)], axis=0)
        return nn(nt(rows, padded), cols)

    def mass_from_surface(ref, coarse):
        top = jnp.concatenate(
            [ref[pl.ds(8, 32, stride=8), :], jnp.zeros((96, 128), F32)], axis=0)
        cols = jnp.where(iota((48, 128), 0) == iota((48, 128), 1) // 2, 0.25, 0.0)
        i = iota((128, 128), 0)
        rows = jnp.where((iota((128, 128), 1) == (i + 8) // 2) & (i < 32), 1.0, 0.0)
        surface = nn(nt(cols, top), rows)
        mass = softplus(surface - 1.0 - 0.5 * coarse)
        y = gy * 16 - 16 + iota((48, 128), 0)
        x = gx * 8 - 8 + iota((48, 128), 1)
        inside = (y >= 0) & (y < ny * 16) & (x >= 0) & (x < nx * 8)
        return jnp.where(inside, mass, 0.0)

    def with_rim(v):
        rim = jnp.where(sub8 < 4, v[32:40], v[8:16])
        return jnp.concatenate([rim, v[16:32], rim], axis=0)

    row_block = gx * 2 + gz
    dn_row, up_row = -(1 - gz), gz

    def bulk_slots(X):
        slots = [X.at[0:2, 8:40], X.at[10:12, 8:40], X.at[2:10, 6:8], X.at[2:10, 40:42]]
        for r in (1, 10):
            for c in (7, 40):
                slots.append(X.at[r:r + 1, c:c + 1])
        return slots

    def bulk_sources(X, r0, c0):
        def own(r, nr, c, nc):
            return X.at[r0 + r:r0 + r + nr, c0 + c:c0 + c + nc]

        sources = [own(6, 2, 0, 32), own(0, 2, 0, 32), own(0, 8, 30, 2), own(0, 8, 0, 2)]
        for r in (7, 0):
            for c in (31, 0):
                sources.append(own(r, 1, c, 1))
        return sources

    bulk_targets = [(up_row, 0, other), (dn_row, 0, other), (0, 1, gz), (0, -1, gz)]
    bulk_origins = [(dn_row, 0), (up_row, 0), (0, -1), (0, 1)]
    for tx, ox in ((up_row, dn_row), (dn_row, up_row)):
        for ty in (1, -1):
            bulk_targets.append((tx, ty, other))
            bulk_origins.append((ox, -ty))

    def send_bulk(kind, X, r0, c0, D):
        sources, slots = bulk_sources(X, r0, c0), bulk_slots(D)
        for n in range(8):
            send(sources[n], slots[n], bs_sem.at[kind, n], br_sem.at[kind, n], bulk_targets[n])

    def await_bulk(kind, D):
        slots = bulk_slots(D)
        for n in range(8):
            arrive(slots[n], bs_sem.at[kind, n], br_sem.at[kind, n], *bulk_origins[n])

    def clear_bulk(X):
        @pl.when(row_block == 0)
        def _():
            X[0:2] = jnp.zeros((2, 48, 128), F32)

        @pl.when(row_block == 2 * nx - 1)
        def _():
            X[10:12] = jnp.zeros((2, 48, 128), F32)

        @pl.when(gy == 0)
        def _():
            X[:, 0:8] = jnp.zeros((12, 8, 128), F32)

        @pl.when(gy == ny - 1)
        def _():
            X[:, 40:48] = jnp.zeros((12, 8, 128), F32)

    def prepare_bulk():
        @pl.loop(0, 12, unroll=6)
        def _(r):
            m = MA[r]
            KB[r] = jnp.where(m == 0, 0.04, jnp.where(m == 1, 0.15, 0.09))

        clear_bulk(KB)

        @pl.loop(0, 11, unroll=11)
        def _(r):
            k = KB[r]
            GX[r] = 0.5 * (k + KB[r + 1])
            GY[r] = 0.5 * (k + pltpu.roll(k, 47, 0))
            last = iota((48, 128), 1) == 127
            GD[r] = 0.5 * (k + jnp.where(last, 0.0, pltpu.roll(k, 127, 1)))

    def bulk_substep(sub, src, dst, low, high, own_only=False):
        col = gy * 32 - 8 + iota((48, 128), 0)
        col_in = jnp.where((col >= 0) & (col < cols_all), 1.0, 0.0)
        last = iota((48, 128), 1) == 127

        @pl.loop(low, high, unroll=(high - low) // 2)
        def _(r):
            t = src[r]
            change = GX[r] * (src[r + 1] - t) - GX[r - 1] * (t - src[r - 1])
            flow = GY[r] * (pltpu.roll(t, 47, 0) - t)
            change = change + (flow - pltpu.roll(flow, 1, 0))
            flow = GD[r] * (jnp.where(last, 0.0, pltpu.roll(t, 127, 1)) - t)
            change = change + (flow - pltpu.roll(flow, 1, 1))
            along = LXB[sub * 12 + r]
            laser = LYD[sub] * jnp.concatenate([along] * 6, axis=0)
            row = row_block * 8 - 2 + r
            row_in = jnp.where((row >= 0) & (row < rows_all), 1.0, 0.0)
            new = (t + change + laser) * (col_in * row_in)
            if own_only:
                dst[r, 8:40, :] = new[8:40]
            else:
                dst[r] = new

    pl.semaphore_wait(barrier, 2 * beside_x * beside_y - 1)
    send_vapor(0, lambda x, n, y, m: u_hbm.at[:, x:x + n, y:y + m], A)
    loads[0].wait()
    pack_z(0, A)
    send_z(0)
    prepare()
    loads[1].wait()
    loads[2].wait()
    pack_surface()
    SR[own_slot] = SS[...]
    send_surface()
    send_bulk(0, t_hbm, 0, 0, TA)
    send_bulk(1, m_hbm, 0, 0, MA)

    await_z(0)
    unpack_z(0)
    await_vapor(0, A)
    clear_outside(A)

    def to_b(c, x, v):
        B[c, x + 2, 8:24, :] = v

    advance(A, to_b)
    pressures(0, B, 2, 8)
    send_pressures(0)
    pack_z(1, B)
    send_z(1)
    first = len(sent)
    send_vapor(1, lambda x, n, y, m: B.at[:, x + 2:x + 2 + n, y + 8:y + 8 + m], B)
    sent_b = sent[first:]
    del sent[first:]

    await_surface()
    assemble_surface()
    await_bulk(0, TA)
    await_bulk(1, MA)
    clear_bulk(TA)
    prepare_bulk()
    bulk_substep(0, TA, TC, 1, 11)
    bulk_substep(1, TC, TB, 2, 10, True)
    send_bulk(2, TB, 2, 8, TB)

    await_pressures(0)
    coarse = coarse_pressure(0)
    fine = fine_from_coarse(coarse)
    surface_substep(0, SA, SB, fine)
    surface_substep(1, SB, SA, fine)
    MM[...] = with_rim(mass_from_surface(SA, coarse))
    LL[0:32, :] = with_rim(LL[...])

    await_z(1)
    unpack_z(1)
    await_vapor(1, B)
    clear_outside(B)
    drain(sent_b)
    lane32 = iota((32, 128), 1)
    height = (lane32 + gz * 128).astype(F32)
    height_edge = (lane32 + other * 128).astype(F32)
    for xi in range(12):
        mass = jnp.broadcast_to(MM[:, xi + 6:xi + 7], (32, 128))
        level = jnp.broadcast_to(LL[0:32, xi + 6:xi + 7], (32, 128))
        field = jnp.where(height == level, mass, 0.0)
        B[0, xi] = B[0, xi] + 0.5 * field
        B[4, xi] = B[4, xi] + 0.4 * field
        B[5, xi] = B[5, xi] + 0.6 * field
        if 1 <= xi <= 10:
            @pl.when(gz == 1)
            def _():
                edge = jnp.where((height_edge == level) & (lane32 >= 126), mass, 0.0)
                UE[0, xi - 1] = UE[0, xi - 1] + 0.5 * edge
                UE[4, xi - 1] = UE[4, xi - 1] + 0.4 * edge
                UE[5, xi - 1] = UE[5, xi - 1] + 0.6 * edge

    def to_out(c, x, v):
        uo_ref[c, x] = v

    advance(B, to_out)
    pressures(1, uo_ref, 0, 0)
    send_pressures(1)

    await_bulk(2, TB)
    clear_bulk(TB)
    bulk_substep(2, TB, TC, 1, 11)
    bulk_substep(3, TC, TA, 2, 10, True)

    await_pressures(1)
    coarse = coarse_pressure(1)
    fine = fine_from_coarse(coarse)
    surface_substep(2, SA, SB, fine)
    surface_substep(3, SB, SA, fine)
    mass_now = mass_from_surface(SA, coarse)[16:32]
    lane16 = iota((16, 128), 1)
    height = (lane16 + gz * 128).astype(F32)
    for x in range(8):
        mass = jnp.broadcast_to(mass_now[:, x + 8:x + 9], (16, 128))
        level = jnp.broadcast_to(LO[:, x:x + 1], (16, 128))
        field = jnp.where(height == level, mass, 0.0)
        uo_ref[0, x] = uo_ref[0, x] + 0.5 * field
        uo_ref[4, x] = uo_ref[4, x] + 0.4 * field
        uo_ref[5, x] = uo_ref[5, x] + 0.6 * field

    eye = jnp.where(iota((128, 128), 0) == iota((128, 128), 1), 1.0, 0.0)
    for half in range(2):
        acc = jnp.zeros((8, 128), F32)
        for i in range(4):
            at = pl.multiple_of((9 + gz * 8 + 4 * half + i) * 8, 8)
            v = SA[pl.ds(at, 8), :]
            shift = (32 * i - 32) % 128
            v = pltpu.roll(v, shift, 1) if shift else v
            acc = jnp.where(lane8 // 32 == i, v, acc)
        turned = nt(eye, jnp.concatenate([acc, jnp.zeros((120, 128), F32)], axis=0))
        turned = turned.reshape(4, 32, 128)
        shallow = iota((4, 32, 128), 2) < 4
        deep = TA[2 + 4 * half:6 + 4 * half, 8:40, :]
        to_ref[4 * half:4 * half + 4] = jnp.where(shallow, turned, deep)

    drain(sent)

    @pl.when(gz == 0)
    def _():
        for step in range(2):
            for n in range(17):
                when(exists(*p_targets[n][:2]), lambda: p_copy(step, n).wait_send())


def solution(mesh):
    sizes = (mesh.shape["gx"], mesh.shape["gy"])

    def shards(vapor, thermal, phase, level, path):
        anywhere = pl.BlockSpec(memory_space=pl.ANY)
        vmem = pl.BlockSpec(memory_space=pltpu.VMEM)
        dma = pltpu.SemaphoreType.DMA
        row = (12, 48, 128)
        gas, temp = pl.pallas_call(
            functools.partial(kernel, sizes),
            out_shape=(
                pltpu.VMEM((6, 8, 16, 128), F32),
                pltpu.VMEM((8, 32, 128), F32),
            ),
            in_specs=[anywhere, anywhere, anywhere, vmem, pl.BlockSpec(memory_space=pltpu.SMEM)],
            out_specs=(vmem, vmem),
            scratch_shapes=[
                pltpu.VMEM((6, 12, 32, 128), F32), pltpu.VMEM((6, 12, 32, 128), F32),
                pltpu.VMEM((6, 10, 32, 128), F32), pltpu.VMEM((6, 10, 32, 128), F32),
                pltpu.VMEM((6, 8, 16, 128), F32),
                pltpu.VMEM((2, 2, 8, 128), F32), pltpu.VMEM((2, 5, 2, 8, 128), F32),
                pltpu.VMEM((5, 8, 128), F32), pltpu.VMEM((12, 5, 8, 128), F32),
                pltpu.VMEM((2, 16, 128), F32), pltpu.VMEM((2, 9, 16, 128), F32),
                pltpu.VMEM(row, F32), pltpu.VMEM(row, jnp.int32), pltpu.VMEM(row, F32),
                pltpu.VMEM(row, F32), pltpu.VMEM(row, F32), pltpu.VMEM(row, F32),
                pltpu.VMEM(row, F32), pltpu.VMEM(row, F32),
                pltpu.VMEM((48, 8, 128), F32), pltpu.VMEM((4, 48, 128), F32),
                pltpu.VMEM((272, 128), F32), pltpu.VMEM((272, 128), F32),
                pltpu.VMEM((272, 128), F32), pltpu.VMEM((264, 128), F32),
                pltpu.VMEM((256, 128), F32), pltpu.VMEM((256, 128), F32),
                pltpu.VMEM((256, 128), F32), pltpu.VMEM((4, 256, 128), F32),
                pltpu.VMEM((256, 128), F32), pltpu.VMEM((16, 128), F32),
                pltpu.VMEM((48, 128), F32), pltpu.VMEM((32, 128), F32),
                dma((3,)), dma((2, 8)), dma((2, 8)), dma((2, 5)), dma((2, 5)),
                dma((12,)), dma((12,)), dma((2, 17)), dma((2, 9)),
                dma((3, 8)), dma((3, 8)),
            ],
            compiler_params=pltpu.CompilerParams(collective_id=0, has_side_effects=True),
        )(vapor, jnp.transpose(thermal, (1, 2, 0)), jnp.transpose(phase, (1, 2, 0)), level, path.T)
        return gas, jnp.transpose(temp, (2, 0, 1))

    return jax.shard_map(
        shards,
        mesh=mesh,
        in_specs=(
            P(None, "gx", "gy", "gz"),
            P(None, ("gx", "gz"), "gy"),
            P(None, ("gx", "gz"), "gy"),
            P("gx", "gy"),
            P(),
        ),
        out_specs=(P(None, "gx", "gy", "gz"), P(None, ("gx", "gz"), "gy")),
        check_vma=False,
    )
```

```python
import functools
import math

import jax
import jax.numpy as jnp
from jax import lax
from jax.experimental import pallas as pl
from jax.experimental.pallas import tpu as pltpu
from jax.sharding import PartitionSpec as P

MESH = pl.DeviceIdType.MESH
HI = lax.Precision.HIGHEST
F32 = jnp.float32

NU = (0.2, 0.1, 0.15, 0.15, 0.15, 0.2)
BASE = tuple(1.0 - 1.8 * n for n in NU)
SIDE = tuple(0.3 * n for n in NU)
UPC = tuple(0.3 * n - 0.075 for n in NU)
DNC = tuple(0.3 * n + 0.075 for n in NU)
LASER_POWER = 3.0
LATENT_HEAT = 0.3


def softplus(x):
    return jnp.maximum(x, 0.0) + jnp.log1p(jnp.exp(-jnp.abs(x)))


def nt(a, b, precision=HI):
    return lax.dot_general(
        a, b, (((1,), (1,)), ((), ())), precision=precision, preferred_element_type=F32
    )


def nn(a, b):
    return lax.dot_general(
        a, b, (((1,), (0,)), ((), ())), precision=HI, preferred_element_type=F32
    )


def iota(shape, dim):
    return lax.broadcasted_iota(jnp.int32, shape, dim)


def forward_euler(load, edge, which=range(6)):
    def vertical(c):
        center, other = load(c, 0, 0), edge(c)
        lane = iota(center.shape, 1)
        up = pltpu.roll(jnp.where(lane == 0, other, center), 127, 1)
        down = pltpu.roll(jnp.where(lane == 127, other, center), 1, 1)
        return up, down

    u_e, u_w = load(2, 1, 0), load(2, -1, 0)
    v_n, v_s = load(3, 0, 1), load(3, 0, -1)
    w_up, w_dn = vertical(4)
    spread = (u_e - u_w) + (v_n - v_s) + (w_up - w_dn)
    p_e, p_w, p_n, p_s = load(5, 1, 0), load(5, -1, 0), load(5, 0, 1), load(5, 0, -1)
    p_up, p_dn = vertical(5)
    coupled = (
        -0.045 * spread,
        -0.105 * spread,
        -0.15 * (p_e - p_w),
        -0.15 * (p_n - p_s),
        -0.15 * (p_up - p_dn),
        -0.15 * spread,
    )
    out = {}
    for c in which:
        if c == 4:
            up, dn = w_up, w_dn
        elif c == 5:
            up, dn = p_up, p_dn
        else:
            up, dn = vertical(c)
        sides = (load(c, 1, 0) + load(c, -1, 0)) + (load(c, 0, 1) + load(c, 0, -1))
        out[c] = (
            BASE[c] * load(c, 0, 0) + SIDE[c] * sides + UPC[c] * up + DNC[c] * dn + coupled[c]
        )
    return out


def kernel(
    sizes,
    u_hbm, t_hbm, m_hbm, lvl_ref, path_ref,
    uo_ref, to_ref,
    A, B, F, UE, FE, ZS, ZR, SS, SR, PS, PR,
    TA, MA, TB, TC, KB, GX, GY, GD, LXB, LYD,
    SA, SB, SK, SGX, SGY, SGD, SGB, SL, SM, LO, LL, MM,
    in_sem, us_sem, ur_sem, zs_sem, zr_sem, ss_sem, sr_sem, ps_sem, pr_sem,
    bs_sem, br_sem,
):
    nx, ny = sizes
    gx, gy, gz = lax.axis_index("gx"), lax.axis_index("gy"), lax.axis_index("gz")
    other = 1 - gz

    def dev(dx, dy, z):
        return (lax.rem(gx + dx + nx, nx), lax.rem(gy + dy + ny, ny), z)

    loads = [
        pltpu.make_async_copy(u_hbm, A.at[:, 2:10, 8:24], in_sem.at[0]),
        pltpu.make_async_copy(t_hbm, TA.at[2:10, 8:40], in_sem.at[1]),
        pltpu.make_async_copy(m_hbm, MA.at[2:10, 8:40], in_sem.at[2]),
    ]
    for copy in loads:
        copy.start()

    def exists(dx, dy):
        tests = []
        for at, d, size in ((gx, dx, nx), (gy, dy, ny)):
            if not (isinstance(d, int) and d == 0):
                tests.append((at + d >= 0) & (at + d < size))
        if not tests:
            return None
        return tests[0] if len(tests) == 1 else tests[0] & tests[1]

    def when(cond, body):
        if cond is None:
            body()
        else:
            pl.when(cond)(body)

    SR[...] = jnp.zeros((12, 5, 8, 128), F32)
    PR[...] = jnp.zeros((2, 9, 16, 128), F32)

    barrier = pltpu.get_barrier_semaphore()

    def greet(dx, dy, z):
        when(exists(dx, dy), lambda: pl.semaphore_signal(
            barrier, inc=1, device_id=dev(dx, dy, z), device_id_type=MESH))

    for dx in (-1, 0, 1):
        for dy in (-1, 0, 1):
            for z in (gz, other):
                if not (dx == 0 and dy == 0 and z is gz):
                    greet(dx, dy, z)
    beside_x = 3 - jnp.where(gx == 0, 1, 0) - jnp.where(gx == nx - 1, 1, 0)
    beside_y = 3 - jnp.where(gy == 0, 1, 0) - jnp.where(gy == ny - 1, 1, 0)

    sent = []

    def remote(src, dst, s_sem, r_sem, target):
        return pltpu.make_async_remote_copy(
            src_ref=src, dst_ref=dst, send_sem=s_sem, recv_sem=r_sem,
            device_id=dev(*target), device_id_type=MESH,
        )

    def send(src, dst, s_sem, r_sem, target):
        args = (src, dst, s_sem, r_sem, target)
        cond = exists(target[0], target[1])
        when(cond, lambda: remote(*args).start())
        sent.append((cond, args))

    def drain(items):
        for cond, args in items:
            when(cond, lambda: remote(*args).wait_send())

    def arrive(dst, s_sem, r_sem, dx, dy):
        when(exists(dx, dy), lambda: remote(dst, dst, s_sem, r_sem, (1, 0, gz)).wait_recv())

    def vapor_slots(X):
        slots = [X.at[:, 0:2, 8:24], X.at[:, 10:12, 8:24], X.at[:, 2:10, 6:8], X.at[:, 2:10, 24:26]]
        for xi in (1, 10):
            for row in (7, 24):
                slots.append(X.at[:, xi:xi + 1, row:row + 1])
        return slots

    def vapor_sources(own):
        sources = [own(6, 2, 0, 16), own(0, 2, 0, 16), own(0, 8, 14, 2), own(0, 8, 0, 2)]
        for x in (7, 0):
            for y in (15, 0):
                sources.append(own(x, 1, y, 1))
        return sources

    vapor_targets = [(1, 0), (-1, 0), (0, 1), (0, -1), (1, 1), (1, -1), (-1, 1), (-1, -1)]

    def send_vapor(step, own, X):
        slots, sources = vapor_slots(X), vapor_sources(own)
        for n in (0, 1, 4, 5, 6, 7, 2, 3):
            send(sources[n], slots[n], us_sem.at[step, n], ur_sem.at[step, n],
                 (*vapor_targets[n], gz))

    def await_vapor(step, X):
        slots = vapor_slots(X)
        for n in range(8):
            arrive(slots[n], us_sem.at[step, n], ur_sem.at[step, n],
                   -vapor_targets[n][0], -vapor_targets[n][1])

    lane8 = iota((8, 128), 1)
    sub8 = iota((8, 128), 0)

    def pack_z(step, X):
        shift = jnp.where(gz == 0, 2, 0)
        turned = lax.rem(lane8 + shift, 128) // 2
        for half in range(2):
            acc = jnp.zeros((8, 128), F32)
            for k in range(64 if half == 0 else 32):
                n = half * 64 + k
                c, x, yt = n // 16, (n // 2) % 8, n % 2
                v = X[c, x + 2, 8 + 8 * yt:16 + 8 * yt, :]
                if k:
                    v = pltpu.roll(v, 2 * k, 1)
                acc = jnp.where(turned == k, v, acc)
            ZS[step, half] = acc

    z_targets = [(0, 0), (1, 0), (-1, 0), (0, 1), (0, -1)]

    def send_z(step):
        for n in range(5):
            send(ZS.at[step], ZR.at[step, n], zs_sem.at[step, n], zr_sem.at[step, n],
                 (*z_targets[n], other))

    def await_z(step):
        for n in range(5):
            arrive(ZR.at[step, n], zs_sem.at[step, n], zr_sem.at[step, n],
                   -z_targets[n][0], -z_targets[n][1])

    edge_keep = lax.rem(lane8 + 2 * gz, 128) < 2

    def flag(cond):
        return jnp.where(cond, 1.0, 0.0)

    def rim_flags():
        return jnp.where(sub8 < 4, flag(gy < ny - 1), flag(gy > 0)) > 0.5

    def unpack_z(step):
        def tile(slot, c, x, yt):
            n = c * 16 + x * 2 + yt
            v = ZR[step, slot, n // 64]
            k = 2 * (n % 64)
            if k:
                v = pltpu.roll(v, 128 - k, 1)
            return jnp.where(edge_keep, v, 0.0)

        for c in range(6):
            for yt in range(2):
                rows = slice(8 + 8 * yt, 16 + 8 * yt)
                for x in range(8):
                    UE[c, x + 1, rows, :] = tile(0, c, x, yt)
                UE[c, 0, rows, :] = tile(1, c, 7, yt)
                UE[c, 9, rows, :] = tile(2, c, 0, yt)
            for x in range(8):
                low, high = tile(3, c, x, 1), tile(4, c, x, 0)
                rim = jnp.where(sub8 < 4, high, low)
                UE[c, x + 1, 0:8, :] = rim
                UE[c, x + 1, 24:32, :] = rim

    def clear_outside(X):
        @pl.when(gx == 0)
        def _():
            X[:, 0:2] = jnp.zeros((6, 2, 32, 128), F32)
            UE[:, 0:1] = jnp.zeros((6, 1, 32, 128), F32)

        @pl.when(gx == nx - 1)
        def _():
            X[:, 10:12] = jnp.zeros((6, 2, 32, 128), F32)
            UE[:, 9:10] = jnp.zeros((6, 1, 32, 128), F32)

        rim_valid = rim_flags()

        @pl.loop(1, 11, unroll=5)
        def _(xi):
            for c in range(6):
                rim = jnp.where(sub8 < 4, X[c, xi, 24:32, :], X[c, xi, 0:8, :])
                rim = jnp.where(rim_valid, rim, 0.0)
                X[c, xi, 0:8, :] = rim
                X[c, xi, 24:32, :] = rim

        @pl.when((gy == 0) | (gy == ny - 1))
        def _():
            @pl.loop(0, 10, unroll=2)
            def _(xi):
                for c in range(6):
                    rim = jnp.where(rim_valid, UE[c, xi, 0:8, :], 0.0)
                    UE[c, xi, 0:8, :] = rim
                    UE[c, xi, 24:32, :] = rim

    def advance(X, emit, early=None):
        rim_rows = rim_flags()
        lane16 = iota((16, 128), 1)
        edge_lane = jnp.where(gz == 0, 0, 127)

        @pl.loop(0, 10, unroll=2)
        def _(i):
            xi = i + 1

            def load(c, dx, dy):
                return X[c, xi + dx, 8 + dy:24 + dy, :]

            new = forward_euler(load, lambda c: UE[c, i, 8:24, :])
            for c in range(6):
                F[c, i, 8:24, :] = new[c]

        @pl.loop(0, 8, unroll=2)
        def _(x):
            def load_rim(c, dx, dy):
                start = {0: 0, 1: 1, -1: 23}[dy]
                return X[c, x + 2 + dx, start:start + 8, :]

            new = forward_euler(load_rim, lambda c: UE[c, x + 1, 0:8, :])
            for c in range(6):
                rim = jnp.where(rim_rows, new[c], 0.0)
                F[c, x + 1, 0:8, :] = rim
                F[c, x + 1, 24:32, :] = rim

            def load_edge(c, dx, dy):
                return UE[c, x + 1 + dx, 8 + dy:24 + dy, :]

            new = forward_euler(load_edge, lambda c: X[c, x + 2, 8:24, :])
            for c in range(6):
                FE[c, x] = jnp.where(lane16 == edge_lane, new[c], 0.0)

        @pl.when(gx == 0)
        def _():
            F[:, 0:1] = jnp.zeros((6, 1, 32, 128), F32)

        @pl.when(gx == nx - 1)
        def _():
            F[:, 9:10] = jnp.zeros((6, 1, 32, 128), F32)

        def second(which, count):
            @pl.loop(0, 8, unroll=count)
            def _(x):
                def load(c, dx, dy):
                    return F[c, x + 1 + dx, 8 + dy:24 + dy, :]

                new = forward_euler(load, lambda c: FE[c, x], which)
                for c in which:
                    emit(c, x, 0.5 * (X[c, x + 2, 8:24, :] + new[c]))

        if early is None:
            second(range(6), 2)
        else:
            second((5,), 4)
            early()
            second(range(5), 2)

    row_first = gx * 16 - 8
    col_first = gy * 32 - 32
    rows_all, cols_all = nx * 16, ny * 32

    def gauss(cells, centre):
        d = (cells.astype(F32) - centre.astype(F32)) / 6.0
        return jnp.exp(-(d * d))

    def prepare():
        col = col_first + lane8
        col_in = (col >= 0) & (col < cols_all) & (lane8 < 96)
        depth = jnp.exp(-(sub8.astype(F32)) / 4.0)
        for sub in range(4):
            a, b = path_ref[0, sub], path_ref[1, sub]
            profile = LASER_POWER * depth * gauss(col, b)

            @pl.loop(0, 32, unroll=8)
            def _(r):
                along = gauss(jnp.full((8, 128), row_first + r, jnp.int32), a)
                SL[sub, pl.ds(pl.multiple_of(r * 8, 8), 8), :] = profile * along

            c48 = gy * 32 - 8 + iota((48, 128), 0)
            d48 = jnp.exp(-(iota((48, 128), 1).astype(F32)) / 4.0)
            LYD[sub] = LASER_POWER * d48 * gauss(c48, b)
            for r in range(12):
                cell = jnp.full((8, 128), (gx * 2 + gz) * 8 - 2 + r, jnp.int32)
                LXB[sub * 12 + r] = gauss(cell, a)

        @pl.loop(0, 32, unroll=8)
        def _(r):
            row = row_first + r
            row_in = flag((row >= 0) & (row < rows_all))
            SM[pl.ds(pl.multiple_of(r * 8, 8), 8), :] = jnp.where(col_in, row_in, 0.0)

        level = jnp.concatenate(
            [lvl_ref[...].astype(F32), jnp.zeros((8, 112), F32)], axis=1)
        SS[4] = level
        eye = jnp.where(iota((16, 128), 0) == iota((16, 128), 1), 1.0, 0.0)
        LO[...] = nt(eye, jnp.concatenate([level, jnp.zeros((120, 128), F32)], axis=0))

    def pack_surface():
        pick = jnp.where(sub8 == lane8, 1.0, 0.0)
        for half in range(2):
            t = TA[2 + 4 * half:6 + 4 * half, 8:40, :].reshape(128, 128)
            m = MA[2 + 4 * half:6 + 4 * half, 8:40, :].reshape(128, 128).astype(F32)
            SS[half] = nt(pick, t)
            SS[2 + half] = nt(pick, m)

    own_slot = (1 + gz) * 3 + 1

    def send_surface():
        for near in (True, False):
            tx = 0 if near else 2 * gz - 1
            block = 1 + gz if near else 3 - 3 * gz
            for ty in (-1, 0, 1):
                for z in (gz, other):
                    if near and ty == 0 and z is gz:
                        continue
                    slot = block * 3 + 1 - ty
                    same = 1 if z is gz else 0
                    n = (6 if near else 0) + (ty + 1) * 2 + same
                    send(SS, SR.at[slot], ss_sem.at[n], sr_sem.at[slot], (tx, ty, z))

    def await_surface():
        for slot in range(12):
            if slot in (4, 7):
                @pl.when(own_slot != slot)
                def _():
                    arrive(SR.at[slot], ss_sem.at[0], sr_sem.at[slot], 0, 0)
            else:
                arrive(SR.at[slot], ss_sem.at[0], sr_sem.at[slot],
                       (-1, 0, 0, 1)[slot // 3], slot % 3 - 1)

    def assemble_surface():
        SK[0:8, :] = jnp.zeros((8, 128), F32)
        SK[264:272, :] = jnp.zeros((8, 128), F32)
        SA[0:8, :] = jnp.zeros((8, 128), F32)
        SA[264:272, :] = jnp.zeros((8, 128), F32)
        SB[0:8, :] = jnp.zeros((8, 128), F32)
        SB[264:272, :] = jnp.zeros((8, 128), F32)
        SGX[0:8, :] = jnp.zeros((8, 128), F32)

        def merged(rb, x, first):
            parts = []
            for cb in range(3):
                v = SR[rb * 3 + cb, first + x // 4]
                shift = (32 * cb - 32 * (x % 4)) % 128
                parts.append(pltpu.roll(v, shift, 1) if shift else v)
            return jnp.where(lane8 < 32, parts[0], jnp.where(lane8 < 64, parts[1], parts[2]))

        @pl.loop(0, 4)
        def _(rb):
            for x in range(8):
                at = pl.multiple_of(rb * 64 + x * 8, 8)
                mask = SM[pl.ds(at, 8), :] > 0.5
                phase = merged(rb, x, 2)
                k = jnp.where(phase < 0.5, 0.04, jnp.where(phase < 1.5, 0.15, 0.09))
                SK[pl.ds(at + 8, 8), :] = jnp.where(mask, k, 0.0)
                SA[pl.ds(at + 8, 8), :] = jnp.where(mask, merged(rb, x, 0), 0.0)

        @pl.loop(0, 32, unroll=8)
        def _(r):
            at = pl.multiple_of(r * 8, 8)
            k = SK[pl.ds(at + 8, 8), :]
            SGX[pl.ds(at + 8, 8), :] = 0.5 * (k + SK[pl.ds(at + 16, 8), :])
            SGY[pl.ds(at, 8), :] = 0.5 * (k + pltpu.roll(k, 127, 1))
            SGD[pl.ds(at, 8), :] = jnp.where(sub8 == 7, 0.0, 0.5 * (k + pltpu.roll(k, 7, 0)))
            SGB[pl.ds(at, 8), :] = jnp.where(sub8 == 0, 0.5 * k, 0.0)

        blocks = []
        for rb in (0, 1, 3):
            acc = SR[rb * 3, 4]
            for cb in (1, 2):
                acc = acc + pltpu.roll(SR[rb * 3 + cb, 4], 16 * cb, 1)
            blocks.append(acc)
        blocks.append(jnp.zeros((104, 128), F32))
        eye = jnp.where(iota((48, 128), 0) == iota((48, 128), 1), 1.0, 0.0)
        LL[...] = nt(eye, jnp.concatenate(blocks, axis=0))

    def surface_substep(sub, src, dst, fine_pressure):
        for chunk in range(4):
            base = chunk * 64
            t = src[base + 8:base + 72, :]
            g = SGX[base + 8:base + 72, :]
            change = g * (src[base + 16:base + 80, :] - t) - SGX[base:base + 64, :] * (
                t - src[base:base + 64, :])
            flow = SGY[base:base + 64, :] * (pltpu.roll(t, 127, 1) - t)
            change = change + (flow - pltpu.roll(flow, 1, 1))
            t3 = t.reshape(8, 8, 128)
            gd = SGD[base:base + 64, :].reshape(8, 8, 128)
            flow3 = gd * (pltpu.roll(t3, 7, 1) - t3)
            change = change + (flow3 - pltpu.roll(flow3, 1, 1)).reshape(64, 128)
            change = change - SGB[base:base + 64, :] * t + SL[sub, base:base + 64, :]
            dst[base + 8:base + 72, :] = (t + change) * SM[base:base + 64, :]
        top = src[pl.ds(8, 32, stride=8), :]
        cooling = LATENT_HEAT * softplus(top - 1.0 - 0.5 * fine_pressure)
        cooling = cooling * SM[pl.ds(0, 32, stride=8), :]
        dst[pl.ds(8, 32, stride=8), :] = dst[pl.ds(8, 32, stride=8), :] - cooling

    def pressures(step, X, at_x, at_y):
        lane16 = iota((16, 128), 1)
        height = (lane16 + gz * 128).astype(F32)
        acc = jnp.zeros((16, 128), F32)
        for x in range(8):
            v = X[5, x + at_x, at_y:at_y + 16, :]
            hit = height == LO[:, x:x + 1]
            s = jnp.sum(jnp.where(hit, v, 0.0), axis=1, keepdims=True)
            acc = jnp.where(lane16 == x, s, acc)
        PS[step] = acc

        @pl.when(gz == 0)
        def _():
            PR[step, 4] = acc

    p_targets = [(tx, ty, s) for tx in (-1, 0, 1) for ty in (-1, 0, 1) for s in (0, 1)
                 if (tx, ty, s) != (0, 0, 1)]

    def p_needed(step, n):
        tx, ty, same = p_targets[n]
        return step == 0 or (not (tx and ty) and (same or tx != 1))

    def p_copy(step, n):
        tx, ty, s = p_targets[n]
        slot = (1 - tx) * 3 + 1 - ty
        return pltpu.make_async_remote_copy(
            src_ref=PS.at[step], dst_ref=PR.at[step, slot], send_sem=ps_sem.at[step, n],
            recv_sem=pr_sem.at[step, slot], device_id=dev(tx, ty, gz if s else other),
            device_id_type=MESH)

    def send_pressures(step):
        @pl.when(gz == 0)
        def _():
            for n in range(17):
                if p_needed(step, n):
                    when(exists(*p_targets[n][:2]), lambda: p_copy(step, n).start())

    def await_pressures(step):
        for slot in range(9):
            if slot == 4:
                @pl.when(gz == 1)
                def _():
                    arrive(PR.at[step, slot], ps_sem.at[step, 0], pr_sem.at[step, slot], 0, 0)
            elif step == 1 and slot == 1:
                @pl.when((gz == 0) & (gx > 0))
                def _():
                    arrive(PR.at[step, slot], ps_sem.at[step, 0], pr_sem.at[step, slot], 0, 0)
            elif step == 0 or slot in (3, 5, 7):
                arrive(PR.at[step, slot], ps_sem.at[step, 0], pr_sem.at[step, slot],
                       slot // 3 - 1, slot % 3 - 1)

    def coarse_pressure(step):
        blocks = []
        for by in range(3):
            acc = PR[step, by]
            for bx in (1, 2):
                acc = acc + pltpu.roll(PR[step, bx * 3 + by], 8 * bx, 1)
            blocks.append(acc)
        return jnp.concatenate(blocks, axis=0)

    def fine_from_coarse(coarse):
        rows = jnp.where(iota((32, 128), 1) == (iota((32, 128), 0) + 8) // 2, 1.0, 0.0)
        cols = jnp.where(iota((128, 128), 0) == iota((128, 128), 1) // 2, 1.0, 0.0)
        padded = jnp.concatenate([coarse, jnp.zeros((80, 128), F32)], axis=0)
        return nn(nt(rows, padded), cols)

    def mass_from_surface(ref, coarse):
        top = jnp.concatenate(
            [ref[pl.ds(8, 32, stride=8), :], jnp.zeros((96, 128), F32)], axis=0)
        cols = jnp.where(iota((48, 128), 0) == iota((48, 128), 1) // 2, 0.25, 0.0)
        i = iota((128, 128), 0)
        rows = jnp.where((iota((128, 128), 1) == (i + 8) // 2) & (i < 32), 1.0, 0.0)
        surface = nn(nt(cols, top), rows)
        mass = softplus(surface - 1.0 - 0.5 * coarse)
        y = gy * 16 - 16 + iota((48, 128), 0)
        x = gx * 8 - 8 + iota((48, 128), 1)
        inside = (y >= 0) & (y < ny * 16) & (x >= 0) & (x < nx * 8)
        return jnp.where(inside, mass, 0.0)

    def with_rim(v):
        rim = jnp.where(sub8 < 4, v[32:40], v[8:16])
        return jnp.concatenate([rim, v[16:32], rim], axis=0)

    row_block = gx * 2 + gz
    dn_row, up_row = -(1 - gz), gz

    def bulk_slots(X):
        slots = [X.at[0:2, 8:40], X.at[10:12, 8:40], X.at[2:10, 6:8], X.at[2:10, 40:42]]
        for r in (1, 10):
            for c in (7, 40):
                slots.append(X.at[r:r + 1, c:c + 1])
        return slots

    def bulk_sources(X, r0, c0):
        def own(r, nr, c, nc):
            return X.at[r0 + r:r0 + r + nr, c0 + c:c0 + c + nc]

        sources = [own(6, 2, 0, 32), own(0, 2, 0, 32), own(0, 8, 30, 2), own(0, 8, 0, 2)]
        for r in (7, 0):
            for c in (31, 0):
                sources.append(own(r, 1, c, 1))
        return sources

    bulk_targets = [(up_row, 0, other), (dn_row, 0, other), (0, 1, gz), (0, -1, gz)]
    bulk_origins = [(dn_row, 0), (up_row, 0), (0, -1), (0, 1)]
    for tx, ox in ((up_row, dn_row), (dn_row, up_row)):
        for ty in (1, -1):
            bulk_targets.append((tx, ty, other))
            bulk_origins.append((ox, -ty))

    def send_bulk(kind, X, r0, c0, D):
        sources, slots = bulk_sources(X, r0, c0), bulk_slots(D)
        for n in range(8):
            send(sources[n], slots[n], bs_sem.at[kind, n], br_sem.at[kind, n], bulk_targets[n])

    def await_bulk(kind, D):
        slots = bulk_slots(D)
        for n in range(8):
            arrive(slots[n], bs_sem.at[kind, n], br_sem.at[kind, n], *bulk_origins[n])

    def clear_bulk(X):
        @pl.when(row_block == 0)
        def _():
            X[0:2] = jnp.zeros((2, 48, 128), F32)

        @pl.when(row_block == 2 * nx - 1)
        def _():
            X[10:12] = jnp.zeros((2, 48, 128), F32)

        @pl.when(gy == 0)
        def _():
            X[:, 0:8] = jnp.zeros((12, 8, 128), F32)

        @pl.when(gy == ny - 1)
        def _():
            X[:, 40:48] = jnp.zeros((12, 8, 128), F32)

    def prepare_bulk():
        @pl.loop(0, 12, unroll=6)
        def _(r):
            m = MA[r]
            KB[r] = jnp.where(m == 0, 0.04, jnp.where(m == 1, 0.15, 0.09))

        clear_bulk(KB)

        @pl.loop(0, 11, unroll=11)
        def _(r):
            k = KB[r]
            GX[r] = 0.5 * (k + KB[r + 1])
            GY[r] = 0.5 * (k + pltpu.roll(k, 47, 0))
            last = iota((48, 128), 1) == 127
            GD[r] = 0.5 * (k + jnp.where(last, 0.0, pltpu.roll(k, 127, 1)))

    def bulk_substep(sub, src, dst, low, high, own_only=False):
        col = gy * 32 - 8 + iota((48, 128), 0)
        col_in = jnp.where((col >= 0) & (col < cols_all), 1.0, 0.0)
        last = iota((48, 128), 1) == 127

        @pl.loop(low, high, unroll=(high - low) // 2)
        def _(r):
            t = src[r]
            change = GX[r] * (src[r + 1] - t) - GX[r - 1] * (t - src[r - 1])
            flow = GY[r] * (pltpu.roll(t, 47, 0) - t)
            change = change + (flow - pltpu.roll(flow, 1, 0))
            flow = GD[r] * (jnp.where(last, 0.0, pltpu.roll(t, 127, 1)) - t)
            change = change + (flow - pltpu.roll(flow, 1, 1))
            along = LXB[sub * 12 + r]
            laser = LYD[sub] * jnp.concatenate([along] * 6, axis=0)
            row = row_block * 8 - 2 + r
            row_in = jnp.where((row >= 0) & (row < rows_all), 1.0, 0.0)
            new = (t + change + laser) * (col_in * row_in)
            if own_only:
                dst[r, 8:40, :] = new[8:40]
            else:
                dst[r] = new

    pl.semaphore_wait(barrier, 2 * beside_x * beside_y - 1)
    send_vapor(0, lambda x, n, y, m: u_hbm.at[:, x:x + n, y:y + m], A)
    loads[0].wait()
    pack_z(0, A)
    send_z(0)
    prepare()
    loads[1].wait()
    loads[2].wait()
    pack_surface()
    SR[own_slot] = SS[...]
    send_surface()
    send_bulk(0, t_hbm, 0, 0, TA)
    send_bulk(1, m_hbm, 0, 0, MA)

    await_z(0)
    unpack_z(0)
    await_vapor(0, A)
    clear_outside(A)

    def to_b(c, x, v):
        B[c, x + 2, 8:24, :] = v

    def share_first():
        pressures(0, B, 2, 8)
        send_pressures(0)

    advance(A, to_b, share_first)
    pack_z(1, B)
    send_z(1)
    first = len(sent)
    send_vapor(1, lambda x, n, y, m: B.at[:, x + 2:x + 2 + n, y + 8:y + 8 + m], B)
    sent_b = sent[first:]
    del sent[first:]

    await_surface()
    assemble_surface()
    await_bulk(0, TA)
    await_bulk(1, MA)
    clear_bulk(TA)
    prepare_bulk()
    bulk_substep(0, TA, TC, 1, 11)
    bulk_substep(1, TC, TB, 2, 10, True)
    send_bulk(2, TB, 2, 8, TB)

    await_pressures(0)
    coarse = coarse_pressure(0)
    fine = fine_from_coarse(coarse)
    surface_substep(0, SA, SB, fine)
    surface_substep(1, SB, SA, fine)
    MM[...] = with_rim(mass_from_surface(SA, coarse))
    LL[0:32, :] = with_rim(LL[...])

    await_z(1)
    unpack_z(1)
    await_vapor(1, B)
    clear_outside(B)
    drain(sent_b)
    lane32 = iota((32, 128), 1)
    height = (lane32 + gz * 128).astype(F32)
    height_edge = (lane32 + other * 128).astype(F32)
    for xi in range(12):
        mass = jnp.broadcast_to(MM[:, xi + 6:xi + 7], (32, 128))
        level = jnp.broadcast_to(LL[0:32, xi + 6:xi + 7], (32, 128))
        field = jnp.where(height == level, mass, 0.0)
        B[0, xi] = B[0, xi] + 0.5 * field
        B[4, xi] = B[4, xi] + 0.4 * field
        B[5, xi] = B[5, xi] + 0.6 * field
        if 1 <= xi <= 10:
            @pl.when(gz == 1)
            def _():
                edge = jnp.where((height_edge == level) & (lane32 >= 126), mass, 0.0)
                UE[0, xi - 1] = UE[0, xi - 1] + 0.5 * edge
                UE[4, xi - 1] = UE[4, xi - 1] + 0.4 * edge
                UE[5, xi - 1] = UE[5, xi - 1] + 0.6 * edge

    def to_out(c, x, v):
        uo_ref[c, x] = v

    def share_pressure():
        pressures(1, uo_ref, 0, 0)
        send_pressures(1)

    advance(B, to_out, share_pressure)

    await_bulk(2, TB)
    clear_bulk(TB)
    bulk_substep(2, TB, TC, 1, 11)
    bulk_substep(3, TC, TA, 2, 10, True)

    await_pressures(1)
    coarse = coarse_pressure(1)
    fine = fine_from_coarse(coarse)
    surface_substep(2, SA, SB, fine)
    surface_substep(3, SB, SA, fine)
    mass_now = mass_from_surface(SA, coarse)[16:32]
    lane16 = iota((16, 128), 1)
    height = (lane16 + gz * 128).astype(F32)
    for x in range(8):
        mass = jnp.broadcast_to(mass_now[:, x + 8:x + 9], (16, 128))
        level = jnp.broadcast_to(LO[:, x:x + 1], (16, 128))
        field = jnp.where(height == level, mass, 0.0)
        uo_ref[0, x] = uo_ref[0, x] + 0.5 * field
        uo_ref[4, x] = uo_ref[4, x] + 0.4 * field
        uo_ref[5, x] = uo_ref[5, x] + 0.6 * field

    eye = jnp.where(iota((128, 128), 0) == iota((128, 128), 1), 1.0, 0.0)
    for half in range(2):
        acc = jnp.zeros((8, 128), F32)
        for i in range(4):
            at = pl.multiple_of((9 + gz * 8 + 4 * half + i) * 8, 8)
            v = SA[pl.ds(at, 8), :]
            shift = (32 * i - 32) % 128
            v = pltpu.roll(v, shift, 1) if shift else v
            acc = jnp.where(lane8 // 32 == i, v, acc)
        turned = nt(eye, jnp.concatenate([acc, jnp.zeros((120, 128), F32)], axis=0))
        turned = turned.reshape(4, 32, 128)
        shallow = iota((4, 32, 128), 2) < 4
        deep = TA[2 + 4 * half:6 + 4 * half, 8:40, :]
        to_ref[4 * half:4 * half + 4] = jnp.where(shallow, turned, deep)

    drain(sent)

    @pl.when(gz == 0)
    def _():
        for step in range(2):
            for n in range(17):
                if p_needed(step, n):
                    when(exists(*p_targets[n][:2]), lambda: p_copy(step, n).wait_send())


def write_back(gas_ref, temp_ref, gas_out, temp_out, sem):
    copies = [
        pltpu.make_async_copy(gas_ref, gas_out, sem.at[0]),
        pltpu.make_async_copy(temp_ref, temp_out, sem.at[1]),
    ]
    for copy in copies:
        copy.start()
    for copy in copies:
        copy.wait()


def solution(mesh):
    sizes = (mesh.shape["gx"], mesh.shape["gy"])

    def shards(vapor, thermal, phase, level, path):
        anywhere = pl.BlockSpec(memory_space=pl.ANY)
        vmem = pl.BlockSpec(memory_space=pltpu.VMEM)
        dma = pltpu.SemaphoreType.DMA
        row = (12, 48, 128)
        gas, temp = pl.pallas_call(
            functools.partial(kernel, sizes),
            out_shape=(
                pltpu.VMEM((6, 8, 16, 128), F32),
                pltpu.VMEM((8, 32, 128), F32),
            ),
            in_specs=[anywhere, anywhere, anywhere, vmem, pl.BlockSpec(memory_space=pltpu.SMEM)],
            out_specs=(vmem, vmem),
            scratch_shapes=[
                pltpu.VMEM((6, 12, 32, 128), F32), pltpu.VMEM((6, 12, 32, 128), F32),
                pltpu.VMEM((6, 10, 32, 128), F32), pltpu.VMEM((6, 10, 32, 128), F32),
                pltpu.VMEM((6, 8, 16, 128), F32),
                pltpu.VMEM((2, 2, 8, 128), F32), pltpu.VMEM((2, 5, 2, 8, 128), F32),
                pltpu.VMEM((5, 8, 128), F32), pltpu.VMEM((12, 5, 8, 128), F32),
                pltpu.VMEM((2, 16, 128), F32), pltpu.VMEM((2, 9, 16, 128), F32),
                pltpu.VMEM(row, F32), pltpu.VMEM(row, jnp.int32), pltpu.VMEM(row, F32),
                pltpu.VMEM(row, F32), pltpu.VMEM(row, F32), pltpu.VMEM(row, F32),
                pltpu.VMEM(row, F32), pltpu.VMEM(row, F32),
                pltpu.VMEM((48, 8, 128), F32), pltpu.VMEM((4, 48, 128), F32),
                pltpu.VMEM((272, 128), F32), pltpu.VMEM((272, 128), F32),
                pltpu.VMEM((272, 128), F32), pltpu.VMEM((264, 128), F32),
                pltpu.VMEM((256, 128), F32), pltpu.VMEM((256, 128), F32),
                pltpu.VMEM((256, 128), F32), pltpu.VMEM((4, 256, 128), F32),
                pltpu.VMEM((256, 128), F32), pltpu.VMEM((16, 128), F32),
                pltpu.VMEM((48, 128), F32), pltpu.VMEM((32, 128), F32),
                dma((3,)), dma((2, 8)), dma((2, 8)), dma((2, 5)), dma((2, 5)),
                dma((12,)), dma((12,)), dma((2, 17)), dma((2, 9)),
                dma((3, 8)), dma((3, 8)),
            ],
            compiler_params=pltpu.CompilerParams(collective_id=0, has_side_effects=True),
        )(vapor, jnp.transpose(thermal, (1, 2, 0)), jnp.transpose(phase, (1, 2, 0)), level, path.T)
        gas = pltpu.with_memory_space_constraint(gas, pltpu.VMEM)
        temp = pltpu.with_memory_space_constraint(temp, pltpu.VMEM)
        gas, temp = pl.pallas_call(
            write_back,
            out_shape=(
                jax.ShapeDtypeStruct((6, 8, 16, 128), F32),
                jax.ShapeDtypeStruct((8, 32, 128), F32),
            ),
            in_specs=[vmem, vmem],
            out_specs=(anywhere, anywhere),
            scratch_shapes=[dma((2,))],
        )(gas, temp)
        return gas, jnp.transpose(temp, (2, 0, 1))

    return jax.shard_map(
        shards,
        mesh=mesh,
        in_specs=(
            P(None, "gx", "gy", "gz"),
            P(None, ("gx", "gz"), "gy"),
            P(None, ("gx", "gz"), "gy"),
            P("gx", "gy"),
            P(),
        ),
        out_specs=(P(None, "gx", "gy", "gz"), P(None, ("gx", "gz"), "gy")),
        check_vma=False,
    )
```

```python
import functools
import math

import jax
import jax.numpy as jnp
from jax import lax
from jax.experimental import pallas as pl
from jax.experimental.pallas import tpu as pltpu
from jax.sharding import PartitionSpec as P

MESH = pl.DeviceIdType.MESH
HI = lax.Precision.HIGHEST
F32 = jnp.float32

NU = (0.2, 0.1, 0.15, 0.15, 0.15, 0.2)
BASE = tuple(1.0 - 1.8 * n for n in NU)
SIDE = tuple(0.3 * n for n in NU)
UPC = tuple(0.3 * n - 0.075 for n in NU)
DNC = tuple(0.3 * n + 0.075 for n in NU)
LASER_POWER = 3.0
LATENT_HEAT = 0.3


def softplus(x):
    return jnp.maximum(x, 0.0) + jnp.log1p(jnp.exp(-jnp.abs(x)))


def nt(a, b, precision=HI):
    return lax.dot_general(
        a, b, (((1,), (1,)), ((), ())), precision=precision, preferred_element_type=F32
    )


def nn(a, b):
    return lax.dot_general(
        a, b, (((1,), (0,)), ((), ())), precision=HI, preferred_element_type=F32
    )


def iota(shape, dim):
    return lax.broadcasted_iota(jnp.int32, shape, dim)


def forward_euler(load, edge, which=range(6)):
    def vertical(c):
        center, other = load(c, 0, 0), edge(c)
        lane = iota(center.shape, 1)
        up = pltpu.roll(jnp.where(lane == 0, other, center), 127, 1)
        down = pltpu.roll(jnp.where(lane == 127, other, center), 1, 1)
        return up, down

    u_e, u_w = load(2, 1, 0), load(2, -1, 0)
    v_n, v_s = load(3, 0, 1), load(3, 0, -1)
    w_up, w_dn = vertical(4)
    spread = (u_e - u_w) + (v_n - v_s) + (w_up - w_dn)
    p_e, p_w, p_n, p_s = load(5, 1, 0), load(5, -1, 0), load(5, 0, 1), load(5, 0, -1)
    p_up, p_dn = vertical(5)
    coupled = (
        -0.045 * spread,
        -0.105 * spread,
        -0.15 * (p_e - p_w),
        -0.15 * (p_n - p_s),
        -0.15 * (p_up - p_dn),
        -0.15 * spread,
    )
    out = {}
    for c in which:
        if c == 4:
            up, dn = w_up, w_dn
        elif c == 5:
            up, dn = p_up, p_dn
        else:
            up, dn = vertical(c)
        sides = (load(c, 1, 0) + load(c, -1, 0)) + (load(c, 0, 1) + load(c, 0, -1))
        out[c] = (
            BASE[c] * load(c, 0, 0) + SIDE[c] * sides + UPC[c] * up + DNC[c] * dn + coupled[c]
        )
    return out


def kernel(
    sizes,
    u_hbm, t_hbm, m_hbm, lvl_ref, path_ref,
    uo_ref, to_ref,
    A, B, F, UE, FE, ZS, ZR, SS, SR, PS, PR,
    TA, MA, TB, TC, KB, GX, GY, GD, LXB, LYD,
    SA, SB, SK, SGX, SGY, SGD, SGB, SL, SM, HIT, LL, MM,
    in_sem, us_sem, ur_sem, zs_sem, zr_sem, ss_sem, sr_sem, ps_sem, pr_sem,
    bs_sem, br_sem,
):
    nx, ny = sizes
    gx, gy, gz = lax.axis_index("gx"), lax.axis_index("gy"), lax.axis_index("gz")
    other = 1 - gz

    def dev(dx, dy, z):
        return (lax.rem(gx + dx + nx, nx), lax.rem(gy + dy + ny, ny), z)

    loads = [
        pltpu.make_async_copy(u_hbm, A.at[:, 2:10, 8:24], in_sem.at[0]),
        pltpu.make_async_copy(t_hbm, TA.at[2:10, 8:40], in_sem.at[1]),
        pltpu.make_async_copy(m_hbm, MA.at[2:10, 8:40], in_sem.at[2]),
    ]
    for copy in loads:
        copy.start()

    def exists(dx, dy):
        tests = []
        for at, d, size in ((gx, dx, nx), (gy, dy, ny)):
            if not (isinstance(d, int) and d == 0):
                tests.append((at + d >= 0) & (at + d < size))
        if not tests:
            return None
        return tests[0] if len(tests) == 1 else tests[0] & tests[1]

    def when(cond, body):
        if cond is None:
            body()
        else:
            pl.when(cond)(body)

    SR[...] = jnp.zeros((12, 5, 8, 128), F32)
    PR[...] = jnp.zeros((2, 9, 16, 128), F32)

    barrier = pltpu.get_barrier_semaphore()

    def greet(dx, dy, z):
        when(exists(dx, dy), lambda: pl.semaphore_signal(
            barrier, inc=1, device_id=dev(dx, dy, z), device_id_type=MESH))

    for dx in (-1, 0, 1):
        for dy in (-1, 0, 1):
            for z in (gz, other):
                if not (dx == 0 and dy == 0 and z is gz):
                    greet(dx, dy, z)
    beside_x = 3 - jnp.where(gx == 0, 1, 0) - jnp.where(gx == nx - 1, 1, 0)
    beside_y = 3 - jnp.where(gy == 0, 1, 0) - jnp.where(gy == ny - 1, 1, 0)

    sent = []

    def remote(src, dst, s_sem, r_sem, target):
        return pltpu.make_async_remote_copy(
            src_ref=src, dst_ref=dst, send_sem=s_sem, recv_sem=r_sem,
            device_id=dev(*target), device_id_type=MESH,
        )

    def send(src, dst, s_sem, r_sem, target):
        args = (src, dst, s_sem, r_sem, target)
        cond = exists(target[0], target[1])
        when(cond, lambda: remote(*args).start())
        sent.append((cond, args))

    def drain(items):
        for cond, args in items:
            when(cond, lambda: remote(*args).wait_send())

    def arrive(dst, s_sem, r_sem, dx, dy):
        when(exists(dx, dy), lambda: remote(dst, dst, s_sem, r_sem, (1, 0, gz)).wait_recv())

    def vapor_slots(X):
        slots = [X.at[:, 0:2, 8:24], X.at[:, 10:12, 8:24], X.at[:, 2:10, 6:8], X.at[:, 2:10, 24:26]]
        for xi in (1, 10):
            for row in (7, 24):
                slots.append(X.at[:, xi:xi + 1, row:row + 1])
        return slots

    def vapor_sources(own):
        sources = [own(6, 2, 0, 16), own(0, 2, 0, 16), own(0, 8, 14, 2), own(0, 8, 0, 2)]
        for x in (7, 0):
            for y in (15, 0):
                sources.append(own(x, 1, y, 1))
        return sources

    vapor_targets = [(1, 0), (-1, 0), (0, 1), (0, -1), (1, 1), (1, -1), (-1, 1), (-1, -1)]

    def send_vapor(step, own, X):
        slots, sources = vapor_slots(X), vapor_sources(own)
        for n in (0, 1, 4, 5, 6, 7, 2, 3):
            send(sources[n], slots[n], us_sem.at[step, n], ur_sem.at[step, n],
                 (*vapor_targets[n], gz))

    def await_vapor(step, X):
        slots = vapor_slots(X)
        for n in range(8):
            arrive(slots[n], us_sem.at[step, n], ur_sem.at[step, n],
                   -vapor_targets[n][0], -vapor_targets[n][1])

    lane8 = iota((8, 128), 1)
    sub8 = iota((8, 128), 0)

    def pack_z(step, X):
        shift = jnp.where(gz == 0, 2, 0)
        turned = lax.rem(lane8 + shift, 128) // 2
        for half in range(2):
            acc = jnp.zeros((8, 128), F32)
            for k in range(64 if half == 0 else 32):
                n = half * 64 + k
                c, x, yt = n // 16, (n // 2) % 8, n % 2
                v = X[c, x + 2, 8 + 8 * yt:16 + 8 * yt, :]
                if k:
                    v = pltpu.roll(v, 2 * k, 1)
                acc = jnp.where(turned == k, v, acc)
            ZS[step, half] = acc

    z_targets = [(0, 0), (1, 0), (-1, 0), (0, 1), (0, -1)]

    def send_z(step):
        for n in range(5):
            send(ZS.at[step], ZR.at[step, n], zs_sem.at[step, n], zr_sem.at[step, n],
                 (*z_targets[n], other))

    def await_z(step):
        for n in range(5):
            arrive(ZR.at[step, n], zs_sem.at[step, n], zr_sem.at[step, n],
                   -z_targets[n][0], -z_targets[n][1])

    edge_keep = lax.rem(lane8 + 2 * gz, 128) < 2

    def flag(cond):
        return jnp.where(cond, 1.0, 0.0)

    def rim_flags():
        return jnp.where(sub8 < 4, flag(gy < ny - 1), flag(gy > 0)) > 0.5

    def unpack_z(step):
        def tile(slot, c, x, yt):
            n = c * 16 + x * 2 + yt
            v = ZR[step, slot, n // 64]
            k = 2 * (n % 64)
            if k:
                v = pltpu.roll(v, 128 - k, 1)
            return jnp.where(edge_keep, v, 0.0)

        for c in range(6):
            for yt in range(2):
                rows = slice(8 + 8 * yt, 16 + 8 * yt)
                for x in range(8):
                    UE[c, x + 1, rows, :] = tile(0, c, x, yt)
                UE[c, 0, rows, :] = tile(1, c, 7, yt)
                UE[c, 9, rows, :] = tile(2, c, 0, yt)
            for x in range(8):
                low, high = tile(3, c, x, 1), tile(4, c, x, 0)
                rim = jnp.where(sub8 < 4, high, low)
                UE[c, x + 1, 0:8, :] = rim
                UE[c, x + 1, 24:32, :] = rim

    def clear_outside(X):
        @pl.when(gx == 0)
        def _():
            X[:, 0:2] = jnp.zeros((6, 2, 32, 128), F32)
            UE[:, 0:1] = jnp.zeros((6, 1, 32, 128), F32)

        @pl.when(gx == nx - 1)
        def _():
            X[:, 10:12] = jnp.zeros((6, 2, 32, 128), F32)
            UE[:, 9:10] = jnp.zeros((6, 1, 32, 128), F32)

        rim_valid = rim_flags()

        @pl.loop(1, 11, unroll=5)
        def _(xi):
            for c in range(6):
                rim = jnp.where(sub8 < 4, X[c, xi, 24:32, :], X[c, xi, 0:8, :])
                rim = jnp.where(rim_valid, rim, 0.0)
                X[c, xi, 0:8, :] = rim
                X[c, xi, 24:32, :] = rim

        @pl.when((gy == 0) | (gy == ny - 1))
        def _():
            @pl.loop(0, 10, unroll=2)
            def _(xi):
                for c in range(6):
                    rim = jnp.where(rim_valid, UE[c, xi, 0:8, :], 0.0)
                    UE[c, xi, 0:8, :] = rim
                    UE[c, xi, 24:32, :] = rim

    def advance(X, emit, early=None):
        rim_rows = rim_flags()
        lane16 = iota((16, 128), 1)
        edge_lane = jnp.where(gz == 0, 0, 127)

        @pl.loop(0, 10, unroll=2)
        def _(i):
            xi = i + 1

            def load(c, dx, dy):
                return X[c, xi + dx, 8 + dy:24 + dy, :]

            new = forward_euler(load, lambda c: UE[c, i, 8:24, :])
            for c in range(6):
                F[c, i, 8:24, :] = new[c]

        @pl.loop(0, 8, unroll=2)
        def _(x):
            def load_rim(c, dx, dy):
                start = {0: 0, 1: 1, -1: 23}[dy]
                return X[c, x + 2 + dx, start:start + 8, :]

            new = forward_euler(load_rim, lambda c: UE[c, x + 1, 0:8, :])
            for c in range(6):
                rim = jnp.where(rim_rows, new[c], 0.0)
                F[c, x + 1, 0:8, :] = rim
                F[c, x + 1, 24:32, :] = rim

            def load_edge(c, dx, dy):
                return UE[c, x + 1 + dx, 8 + dy:24 + dy, :]

            new = forward_euler(load_edge, lambda c: X[c, x + 2, 8:24, :])
            for c in range(6):
                FE[c, x] = jnp.where(lane16 == edge_lane, new[c], 0.0)

        @pl.when(gx == 0)
        def _():
            F[:, 0:1] = jnp.zeros((6, 1, 32, 128), F32)

        @pl.when(gx == nx - 1)
        def _():
            F[:, 9:10] = jnp.zeros((6, 1, 32, 128), F32)

        def second(which, count):
            @pl.loop(0, 8, unroll=count)
            def _(x):
                def load(c, dx, dy):
                    return F[c, x + 1 + dx, 8 + dy:24 + dy, :]

                new = forward_euler(load, lambda c: FE[c, x], which)
                for c in which:
                    emit(c, x, 0.5 * (X[c, x + 2, 8:24, :] + new[c]))

        if early is None:
            second(range(6), 2)
        else:
            second((5,), 4)
            early()
            second(range(5), 2)

    row_first = gx * 16 - 8
    col_first = gy * 32 - 32
    rows_all, cols_all = nx * 16, ny * 32

    def gauss(cells, centre):
        d = (cells.astype(F32) - centre.astype(F32)) / 6.0
        return jnp.exp(-(d * d))

    def prepare():
        col = col_first + lane8
        col_in = (col >= 0) & (col < cols_all) & (lane8 < 96)
        depth = jnp.exp(-(sub8.astype(F32)) / 4.0)
        for sub in range(4):
            a, b = path_ref[0, sub], path_ref[1, sub]
            profile = LASER_POWER * depth * gauss(col, b)

            @pl.loop(0, 32, unroll=8)
            def _(r):
                along = gauss(jnp.full((8, 128), row_first + r, jnp.int32), a)
                SL[sub, pl.ds(pl.multiple_of(r * 8, 8), 8), :] = profile * along

            c48 = gy * 32 - 8 + iota((48, 128), 0)
            d48 = jnp.exp(-(iota((48, 128), 1).astype(F32)) / 4.0)
            LYD[sub] = LASER_POWER * d48 * gauss(c48, b)
            for r in range(12):
                cell = jnp.full((8, 128), (gx * 2 + gz) * 8 - 2 + r, jnp.int32)
                LXB[sub * 12 + r] = gauss(cell, a)

        @pl.loop(0, 32, unroll=8)
        def _(r):
            row = row_first + r
            row_in = flag((row >= 0) & (row < rows_all))
            SM[pl.ds(pl.multiple_of(r * 8, 8), 8), :] = jnp.where(col_in, row_in, 0.0)

        level = jnp.concatenate(
            [lvl_ref[...].astype(F32), jnp.zeros((8, 112), F32)], axis=1)
        SS[4] = level
        eye = jnp.where(iota((16, 128), 0) == iota((16, 128), 1), 1.0, 0.0)
        own = nt(eye, jnp.concatenate([level, jnp.zeros((120, 128), F32)], axis=0))
        heights = (iota((16, 128), 1) + gz * 128).astype(F32)
        for x in range(8):
            HIT[x] = jnp.where(heights == own[:, x:x + 1], 1.0, 0.0)

    def pack_surface():
        pick = jnp.where(sub8 == lane8, 1.0, 0.0)
        for half in range(2):
            t = TA[2 + 4 * half:6 + 4 * half, 8:40, :].reshape(128, 128)
            m = MA[2 + 4 * half:6 + 4 * half, 8:40, :].reshape(128, 128).astype(F32)
            SS[half] = nt(pick, t)
            SS[2 + half] = nt(pick, m)

    own_slot = (1 + gz) * 3 + 1

    def send_surface():
        for near in (True, False):
            tx = 0 if near else 2 * gz - 1
            block = 1 + gz if near else 3 - 3 * gz
            for ty in (-1, 0, 1):
                for z in (gz, other):
                    if near and ty == 0 and z is gz:
                        continue
                    slot = block * 3 + 1 - ty
                    same = 1 if z is gz else 0
                    n = (6 if near else 0) + (ty + 1) * 2 + same
                    send(SS, SR.at[slot], ss_sem.at[n], sr_sem.at[slot], (tx, ty, z))

    def await_surface():
        for slot in range(12):
            if slot in (4, 7):
                @pl.when(own_slot != slot)
                def _():
                    arrive(SR.at[slot], ss_sem.at[0], sr_sem.at[slot], 0, 0)
            else:
                arrive(SR.at[slot], ss_sem.at[0], sr_sem.at[slot],
                       (-1, 0, 0, 1)[slot // 3], slot % 3 - 1)

    def assemble_surface():
        SK[0:8, :] = jnp.zeros((8, 128), F32)
        SK[264:272, :] = jnp.zeros((8, 128), F32)
        SA[0:8, :] = jnp.zeros((8, 128), F32)
        SA[264:272, :] = jnp.zeros((8, 128), F32)
        SB[0:8, :] = jnp.zeros((8, 128), F32)
        SB[264:272, :] = jnp.zeros((8, 128), F32)
        SGX[0:8, :] = jnp.zeros((8, 128), F32)

        def merged(rb, x, first):
            parts = []
            for cb in range(3):
                v = SR[rb * 3 + cb, first + x // 4]
                shift = (32 * cb - 32 * (x % 4)) % 128
                parts.append(pltpu.roll(v, shift, 1) if shift else v)
            return jnp.where(lane8 < 32, parts[0], jnp.where(lane8 < 64, parts[1], parts[2]))

        @pl.loop(0, 4)
        def _(rb):
            for x in range(8):
                at = pl.multiple_of(rb * 64 + x * 8, 8)
                mask = SM[pl.ds(at, 8), :] > 0.5
                phase = merged(rb, x, 2)
                k = jnp.where(phase < 0.5, 0.04, jnp.where(phase < 1.5, 0.15, 0.09))
                SK[pl.ds(at + 8, 8), :] = jnp.where(mask, k, 0.0)
                SA[pl.ds(at + 8, 8), :] = jnp.where(mask, merged(rb, x, 0), 0.0)

        @pl.loop(0, 32, unroll=8)
        def _(r):
            at = pl.multiple_of(r * 8, 8)
            k = SK[pl.ds(at + 8, 8), :]
            SGX[pl.ds(at + 8, 8), :] = 0.5 * (k + SK[pl.ds(at + 16, 8), :])
            SGY[pl.ds(at, 8), :] = 0.5 * (k + pltpu.roll(k, 127, 1))
            SGD[pl.ds(at, 8), :] = jnp.where(sub8 == 7, 0.0, 0.5 * (k + pltpu.roll(k, 7, 0)))
            SGB[pl.ds(at, 8), :] = jnp.where(sub8 == 0, 0.5 * k, 0.0)

        blocks = []
        for rb in (0, 1, 3):
            acc = SR[rb * 3, 4]
            for cb in (1, 2):
                acc = acc + pltpu.roll(SR[rb * 3 + cb, 4], 16 * cb, 1)
            blocks.append(acc)
        blocks.append(jnp.zeros((104, 128), F32))
        eye = jnp.where(iota((48, 128), 0) == iota((48, 128), 1), 1.0, 0.0)
        LL[...] = nt(eye, jnp.concatenate(blocks, axis=0))

    def surface_conduct(sub, src, dst):
        for chunk in range(4):
            base = chunk * 64
            t = src[base + 8:base + 72, :]
            g = SGX[base + 8:base + 72, :]
            change = g * (src[base + 16:base + 80, :] - t) - SGX[base:base + 64, :] * (
                t - src[base:base + 64, :])
            flow = SGY[base:base + 64, :] * (pltpu.roll(t, 127, 1) - t)
            change = change + (flow - pltpu.roll(flow, 1, 1))
            t3 = t.reshape(8, 8, 128)
            gd = SGD[base:base + 64, :].reshape(8, 8, 128)
            flow3 = gd * (pltpu.roll(t3, 7, 1) - t3)
            change = change + (flow3 - pltpu.roll(flow3, 1, 1)).reshape(64, 128)
            change = change - SGB[base:base + 64, :] * t + SL[sub, base:base + 64, :]
            dst[base + 8:base + 72, :] = (t + change) * SM[base:base + 64, :]

    def surface_cool(src, dst, fine_pressure):
        top = src[pl.ds(8, 32, stride=8), :]
        cooling = LATENT_HEAT * softplus(top - 1.0 - 0.5 * fine_pressure)
        cooling = cooling * SM[pl.ds(0, 32, stride=8), :]
        dst[pl.ds(8, 32, stride=8), :] = dst[pl.ds(8, 32, stride=8), :] - cooling

    def pressures(step, X, at_x, at_y):
        lane16 = iota((16, 128), 1)
        acc = jnp.zeros((16, 128), F32)
        for x in range(8):
            v = X[5, x + at_x, at_y:at_y + 16, :]
            s = jnp.sum(HIT[x] * v, axis=1, keepdims=True)
            acc = jnp.where(lane16 == x, s, acc)
        PS[step] = acc

        @pl.when(gz == 0)
        def _():
            PR[step, 4] = acc

    p_targets = [(tx, ty, s) for tx in (-1, 0, 1) for ty in (-1, 0, 1) for s in (0, 1)
                 if (tx, ty, s) != (0, 0, 1)]

    def p_needed(step, n):
        tx, ty, same = p_targets[n]
        return step == 0 or (not (tx and ty) and (same or tx != 1))

    def p_copy(step, n):
        tx, ty, s = p_targets[n]
        slot = (1 - tx) * 3 + 1 - ty
        return pltpu.make_async_remote_copy(
            src_ref=PS.at[step], dst_ref=PR.at[step, slot], send_sem=ps_sem.at[step, n],
            recv_sem=pr_sem.at[step, slot], device_id=dev(tx, ty, gz if s else other),
            device_id_type=MESH)

    def send_pressures(step):
        @pl.when(gz == 0)
        def _():
            for n in range(17):
                if p_needed(step, n):
                    when(exists(*p_targets[n][:2]), lambda: p_copy(step, n).start())

    def await_pressures(step):
        for slot in range(9):
            if slot == 4:
                @pl.when(gz == 1)
                def _():
                    arrive(PR.at[step, slot], ps_sem.at[step, 0], pr_sem.at[step, slot], 0, 0)
            elif step == 1 and slot == 1:
                @pl.when((gz == 0) & (gx > 0))
                def _():
                    arrive(PR.at[step, slot], ps_sem.at[step, 0], pr_sem.at[step, slot], 0, 0)
            elif step == 0 or slot in (3, 5, 7):
                arrive(PR.at[step, slot], ps_sem.at[step, 0], pr_sem.at[step, slot],
                       slot // 3 - 1, slot % 3 - 1)

    def coarse_pressure(step):
        blocks = []
        for by in range(3):
            acc = PR[step, by]
            for bx in (1, 2):
                acc = acc + pltpu.roll(PR[step, bx * 3 + by], 8 * bx, 1)
            blocks.append(acc)
        return jnp.concatenate(blocks, axis=0)

    def fine_from_coarse(coarse):
        rows = jnp.where(iota((32, 128), 1) == (iota((32, 128), 0) + 8) // 2, 1.0, 0.0)
        cols = jnp.where(iota((128, 128), 0) == iota((128, 128), 1) // 2, 1.0, 0.0)
        padded = jnp.concatenate([coarse, jnp.zeros((80, 128), F32)], axis=0)
        return nn(nt(rows, padded), cols)

    def mass_from_surface(ref, coarse):
        top = jnp.concatenate(
            [ref[pl.ds(8, 32, stride=8), :], jnp.zeros((96, 128), F32)], axis=0)
        cols = jnp.where(iota((48, 128), 0) == iota((48, 128), 1) // 2, 0.25, 0.0)
        i = iota((128, 128), 0)
        rows = jnp.where((iota((128, 128), 1) == (i + 8) // 2) & (i < 32), 1.0, 0.0)
        surface = nn(nt(cols, top), rows)
        mass = softplus(surface - 1.0 - 0.5 * coarse)
        y = gy * 16 - 16 + iota((48, 128), 0)
        x = gx * 8 - 8 + iota((48, 128), 1)
        inside = (y >= 0) & (y < ny * 16) & (x >= 0) & (x < nx * 8)
        return jnp.where(inside, mass, 0.0)

    def with_rim(v):
        rim = jnp.where(sub8 < 4, v[32:40], v[8:16])
        return jnp.concatenate([rim, v[16:32], rim], axis=0)

    row_block = gx * 2 + gz
    dn_row, up_row = -(1 - gz), gz

    def bulk_slots(X):
        slots = [X.at[0:2, 8:40], X.at[10:12, 8:40], X.at[2:10, 6:8], X.at[2:10, 40:42]]
        for r in (1, 10):
            for c in (7, 40):
                slots.append(X.at[r:r + 1, c:c + 1])
        return slots

    def bulk_sources(X, r0, c0):
        def own(r, nr, c, nc):
            return X.at[r0 + r:r0 + r + nr, c0 + c:c0 + c + nc]

        sources = [own(6, 2, 0, 32), own(0, 2, 0, 32), own(0, 8, 30, 2), own(0, 8, 0, 2)]
        for r in (7, 0):
            for c in (31, 0):
                sources.append(own(r, 1, c, 1))
        return sources

    bulk_targets = [(up_row, 0, other), (dn_row, 0, other), (0, 1, gz), (0, -1, gz)]
    bulk_origins = [(dn_row, 0), (up_row, 0), (0, -1), (0, 1)]
    for tx, ox in ((up_row, dn_row), (dn_row, up_row)):
        for ty in (1, -1):
            bulk_targets.append((tx, ty, other))
            bulk_origins.append((ox, -ty))

    def send_bulk(kind, X, r0, c0, D):
        sources, slots = bulk_sources(X, r0, c0), bulk_slots(D)
        for n in range(8):
            send(sources[n], slots[n], bs_sem.at[kind, n], br_sem.at[kind, n], bulk_targets[n])

    def await_bulk(kind, D):
        slots = bulk_slots(D)
        for n in range(8):
            arrive(slots[n], bs_sem.at[kind, n], br_sem.at[kind, n], *bulk_origins[n])

    def clear_bulk(X):
        @pl.when(row_block == 0)
        def _():
            X[0:2] = jnp.zeros((2, 48, 128), F32)

        @pl.when(row_block == 2 * nx - 1)
        def _():
            X[10:12] = jnp.zeros((2, 48, 128), F32)

        @pl.when(gy == 0)
        def _():
            X[:, 0:8] = jnp.zeros((12, 8, 128), F32)

        @pl.when(gy == ny - 1)
        def _():
            X[:, 40:48] = jnp.zeros((12, 8, 128), F32)

    def prepare_bulk():
        @pl.loop(0, 12, unroll=6)
        def _(r):
            m = MA[r]
            KB[r] = jnp.where(m == 0, 0.04, jnp.where(m == 1, 0.15, 0.09))

        clear_bulk(KB)

        @pl.loop(0, 11, unroll=11)
        def _(r):
            k = KB[r]
            GX[r] = 0.5 * (k + KB[r + 1])
            GY[r] = 0.5 * (k + pltpu.roll(k, 47, 0))
            last = iota((48, 128), 1) == 127
            GD[r] = 0.5 * (k + jnp.where(last, 0.0, pltpu.roll(k, 127, 1)))

    def bulk_substep(sub, src, dst, low, high, own_only=False):
        col = gy * 32 - 8 + iota((48, 128), 0)
        col_in = jnp.where((col >= 0) & (col < cols_all), 1.0, 0.0)
        last = iota((48, 128), 1) == 127

        @pl.loop(low, high, unroll=(high - low) // 2)
        def _(r):
            t = src[r]
            change = GX[r] * (src[r + 1] - t) - GX[r - 1] * (t - src[r - 1])
            flow = GY[r] * (pltpu.roll(t, 47, 0) - t)
            change = change + (flow - pltpu.roll(flow, 1, 0))
            flow = GD[r] * (jnp.where(last, 0.0, pltpu.roll(t, 127, 1)) - t)
            change = change + (flow - pltpu.roll(flow, 1, 1))
            along = LXB[sub * 12 + r]
            laser = LYD[sub] * jnp.concatenate([along] * 6, axis=0)
            row = row_block * 8 - 2 + r
            row_in = jnp.where((row >= 0) & (row < rows_all), 1.0, 0.0)
            new = (t + change + laser) * (col_in * row_in)
            if own_only:
                dst[r, 8:40, :] = new[8:40]
            else:
                dst[r] = new

    pl.semaphore_wait(barrier, 2 * beside_x * beside_y - 1)
    send_vapor(0, lambda x, n, y, m: u_hbm.at[:, x:x + n, y:y + m], A)
    loads[0].wait()
    pack_z(0, A)
    send_z(0)
    prepare()
    loads[1].wait()
    loads[2].wait()
    pack_surface()
    SR[own_slot] = SS[...]
    send_surface()
    send_bulk(0, t_hbm, 0, 0, TA)
    send_bulk(1, m_hbm, 0, 0, MA)

    await_z(0)
    unpack_z(0)
    await_vapor(0, A)
    clear_outside(A)

    def to_b(c, x, v):
        B[c, x + 2, 8:24, :] = v

    def share_first():
        pressures(0, B, 2, 8)
        send_pressures(0)

    advance(A, to_b, share_first)
    pack_z(1, B)
    send_z(1)
    first = len(sent)
    send_vapor(1, lambda x, n, y, m: B.at[:, x + 2:x + 2 + n, y + 8:y + 8 + m], B)
    sent_b = sent[first:]
    del sent[first:]

    await_surface()
    assemble_surface()
    await_bulk(0, TA)
    await_bulk(1, MA)
    clear_bulk(TA)
    prepare_bulk()
    bulk_substep(0, TA, TC, 1, 11)
    bulk_substep(1, TC, TB, 2, 10, True)
    send_bulk(2, TB, 2, 8, TB)

    surface_conduct(0, SA, SB)
    LL[0:32, :] = with_rim(LL[...])
    await_pressures(0)
    coarse = coarse_pressure(0)
    fine = fine_from_coarse(coarse)
    surface_cool(SA, SB, fine)
    surface_conduct(1, SB, SA)
    surface_cool(SB, SA, fine)
    MM[...] = with_rim(mass_from_surface(SA, coarse))

    await_z(1)
    unpack_z(1)
    await_vapor(1, B)
    clear_outside(B)
    drain(sent_b)
    lane32 = iota((32, 128), 1)
    height = (lane32 + gz * 128).astype(F32)
    height_edge = (lane32 + other * 128).astype(F32)
    def field_at(xi, heights):
        mass = jnp.broadcast_to(MM[:, xi + 6:xi + 7], (32, 128))
        level = jnp.broadcast_to(LL[0:32, xi + 6:xi + 7], (32, 128))
        return jnp.where(heights == level, mass, 0.0)

    @pl.when(gz == 0)
    def _():
        for xi in range(12):
            field = field_at(xi, height)
            B[0, xi] = B[0, xi] + 0.5 * field
            B[4, xi] = B[4, xi] + 0.4 * field
            B[5, xi] = B[5, xi] + 0.6 * field

    @pl.when(gz == 1)
    def _():
        for xi in range(1, 11):
            field = jnp.where(lane32 >= 126, field_at(xi, height_edge), 0.0)
            UE[0, xi - 1] = UE[0, xi - 1] + 0.5 * field
            UE[4, xi - 1] = UE[4, xi - 1] + 0.4 * field
            UE[5, xi - 1] = UE[5, xi - 1] + 0.6 * field

    def to_out(c, x, v):
        uo_ref[c, x] = v

    def share_pressure():
        pressures(1, uo_ref, 0, 0)
        send_pressures(1)

    advance(B, to_out, share_pressure)

    await_bulk(2, TB)
    clear_bulk(TB)
    bulk_substep(2, TB, TC, 1, 11)
    bulk_substep(3, TC, TA, 2, 10, True)

    surface_conduct(2, SA, SB)
    await_pressures(1)
    coarse = coarse_pressure(1)
    fine = fine_from_coarse(coarse)
    surface_cool(SA, SB, fine)
    surface_conduct(3, SB, SA)
    surface_cool(SB, SA, fine)
    mass_now = mass_from_surface(SA, coarse)[16:32]
    for x in range(8):
        mass = jnp.broadcast_to(mass_now[:, x + 8:x + 9], (16, 128))
        field = HIT[x] * mass
        uo_ref[0, x] = uo_ref[0, x] + 0.5 * field
        uo_ref[4, x] = uo_ref[4, x] + 0.4 * field
        uo_ref[5, x] = uo_ref[5, x] + 0.6 * field

    eye = jnp.where(iota((128, 128), 0) == iota((128, 128), 1), 1.0, 0.0)
    for half in range(2):
        acc = jnp.zeros((8, 128), F32)
        for i in range(4):
            at = pl.multiple_of((9 + gz * 8 + 4 * half + i) * 8, 8)
            v = SA[pl.ds(at, 8), :]
            shift = (32 * i - 32) % 128
            v = pltpu.roll(v, shift, 1) if shift else v
            acc = jnp.where(lane8 // 32 == i, v, acc)
        turned = nt(eye, jnp.concatenate([acc, jnp.zeros((120, 128), F32)], axis=0))
        turned = turned.reshape(4, 32, 128)
        shallow = iota((4, 32, 128), 2) < 4
        deep = TA[2 + 4 * half:6 + 4 * half, 8:40, :]
        to_ref[4 * half:4 * half + 4] = jnp.where(shallow, turned, deep)

    drain(sent)

    @pl.when(gz == 0)
    def _():
        for step in range(2):
            for n in range(17):
                if p_needed(step, n):
                    when(exists(*p_targets[n][:2]), lambda: p_copy(step, n).wait_send())


def write_back(gas_ref, temp_ref, gas_out, temp_out, sem):
    copies = [
        pltpu.make_async_copy(gas_ref, gas_out, sem.at[0]),
        pltpu.make_async_copy(temp_ref, temp_out, sem.at[1]),
    ]
    for copy in copies:
        copy.start()
    for copy in copies:
        copy.wait()


def solution(mesh):
    sizes = (mesh.shape["gx"], mesh.shape["gy"])

    def shards(vapor, thermal, phase, level, path):
        anywhere = pl.BlockSpec(memory_space=pl.ANY)
        vmem = pl.BlockSpec(memory_space=pltpu.VMEM)
        dma = pltpu.SemaphoreType.DMA
        row = (12, 48, 128)
        gas, temp = pl.pallas_call(
            functools.partial(kernel, sizes),
            out_shape=(
                pltpu.VMEM((6, 8, 16, 128), F32),
                pltpu.VMEM((8, 32, 128), F32),
            ),
            in_specs=[anywhere, anywhere, anywhere, vmem, pl.BlockSpec(memory_space=pltpu.SMEM)],
            out_specs=(vmem, vmem),
            scratch_shapes=[
                pltpu.VMEM((6, 12, 32, 128), F32), pltpu.VMEM((6, 12, 32, 128), F32),
                pltpu.VMEM((6, 10, 32, 128), F32), pltpu.VMEM((6, 10, 32, 128), F32),
                pltpu.VMEM((6, 8, 16, 128), F32),
                pltpu.VMEM((2, 2, 8, 128), F32), pltpu.VMEM((2, 5, 2, 8, 128), F32),
                pltpu.VMEM((5, 8, 128), F32), pltpu.VMEM((12, 5, 8, 128), F32),
                pltpu.VMEM((2, 16, 128), F32), pltpu.VMEM((2, 9, 16, 128), F32),
                pltpu.VMEM(row, F32), pltpu.VMEM(row, jnp.int32), pltpu.VMEM(row, F32),
                pltpu.VMEM(row, F32), pltpu.VMEM(row, F32), pltpu.VMEM(row, F32),
                pltpu.VMEM(row, F32), pltpu.VMEM(row, F32),
                pltpu.VMEM((48, 8, 128), F32), pltpu.VMEM((4, 48, 128), F32),
                pltpu.VMEM((272, 128), F32), pltpu.VMEM((272, 128), F32),
                pltpu.VMEM((272, 128), F32), pltpu.VMEM((264, 128), F32),
                pltpu.VMEM((256, 128), F32), pltpu.VMEM((256, 128), F32),
                pltpu.VMEM((256, 128), F32), pltpu.VMEM((4, 256, 128), F32),
                pltpu.VMEM((256, 128), F32), pltpu.VMEM((8, 16, 128), F32),
                pltpu.VMEM((48, 128), F32), pltpu.VMEM((32, 128), F32),
                dma((3,)), dma((2, 8)), dma((2, 8)), dma((2, 5)), dma((2, 5)),
                dma((12,)), dma((12,)), dma((2, 17)), dma((2, 9)),
                dma((3, 8)), dma((3, 8)),
            ],
            compiler_params=pltpu.CompilerParams(collective_id=0, has_side_effects=True),
        )(vapor, jnp.transpose(thermal, (1, 2, 0)), jnp.transpose(phase, (1, 2, 0)), level, path.T)
        gas = pltpu.with_memory_space_constraint(gas, pltpu.VMEM)
        temp = pltpu.with_memory_space_constraint(temp, pltpu.VMEM)
        gas, temp = pl.pallas_call(
            write_back,
            out_shape=(
                jax.ShapeDtypeStruct((6, 8, 16, 128), F32),
                jax.ShapeDtypeStruct((8, 32, 128), F32),
            ),
            in_specs=[vmem, vmem],
            out_specs=(anywhere, anywhere),
            scratch_shapes=[dma((2,))],
        )(gas, temp)
        return gas, jnp.transpose(temp, (2, 0, 1))

    return jax.shard_map(
        shards,
        mesh=mesh,
        in_specs=(
            P(None, "gx", "gy", "gz"),
            P(None, ("gx", "gz"), "gy"),
            P(None, ("gx", "gz"), "gy"),
            P("gx", "gy"),
            P(),
        ),
        out_specs=(P(None, "gx", "gy", "gz"), P(None, ("gx", "gz"), "gy")),
        check_vma=False,
    )
```

```python
import functools
import math

import jax
import jax.numpy as jnp
from jax import lax
from jax.experimental import pallas as pl
from jax.experimental.pallas import tpu as pltpu
from jax.sharding import PartitionSpec as P

MESH = pl.DeviceIdType.MESH
HI = lax.Precision.HIGHEST
F32 = jnp.float32

NU = (0.2, 0.1, 0.15, 0.15, 0.15, 0.2)
BASE = tuple(1.0 - 1.8 * n for n in NU)
SIDE = tuple(0.3 * n for n in NU)
UPC = tuple(0.3 * n - 0.075 for n in NU)
DNC = tuple(0.3 * n + 0.075 for n in NU)
LASER_POWER = 3.0
LATENT_HEAT = 0.3


def softplus(x):
    return jnp.maximum(x, 0.0) + jnp.log1p(jnp.exp(-jnp.abs(x)))


def nt(a, b, precision=HI):
    return lax.dot_general(
        a, b, (((1,), (1,)), ((), ())), precision=precision, preferred_element_type=F32
    )


def nn(a, b):
    return lax.dot_general(
        a, b, (((1,), (0,)), ((), ())), precision=HI, preferred_element_type=F32
    )


def iota(shape, dim):
    return lax.broadcasted_iota(jnp.int32, shape, dim)


def forward_euler(load, edge, which=range(6)):
    def vertical(c):
        center, other = load(c, 0, 0), edge(c)
        lane = iota(center.shape, 1)
        up = pltpu.roll(jnp.where(lane == 0, other, center), 127, 1)
        down = pltpu.roll(jnp.where(lane == 127, other, center), 1, 1)
        return up, down

    u_e, u_w = load(2, 1, 0), load(2, -1, 0)
    v_n, v_s = load(3, 0, 1), load(3, 0, -1)
    w_up, w_dn = vertical(4)
    spread = (u_e - u_w) + (v_n - v_s) + (w_up - w_dn)
    p_e, p_w, p_n, p_s = load(5, 1, 0), load(5, -1, 0), load(5, 0, 1), load(5, 0, -1)
    p_up, p_dn = vertical(5)
    coupled = (
        -0.045 * spread,
        -0.105 * spread,
        -0.15 * (p_e - p_w),
        -0.15 * (p_n - p_s),
        -0.15 * (p_up - p_dn),
        -0.15 * spread,
    )
    out = {}
    for c in which:
        if c == 4:
            up, dn = w_up, w_dn
        elif c == 5:
            up, dn = p_up, p_dn
        else:
            up, dn = vertical(c)
        sides = (load(c, 1, 0) + load(c, -1, 0)) + (load(c, 0, 1) + load(c, 0, -1))
        out[c] = (
            BASE[c] * load(c, 0, 0) + SIDE[c] * sides + UPC[c] * up + DNC[c] * dn + coupled[c]
        )
    return out


def kernel(
    sizes,
    u_hbm, t_hbm, m_hbm, lvl_ref, path_ref,
    uo_ref, to_ref,
    A, B, F, UE, FE, ZS, ZR, SS, SR, PS, PR,
    TA, MA, TB, TC, KB, GX, GY, GD, LXB, LYD,
    SA, SB, SK, SGX, SGY, SGD, SGB, SL, SM, HIT, LL, MM,
    in_sem, us_sem, ur_sem, zs_sem, zr_sem, ss_sem, sr_sem, ps_sem, pr_sem,
    bs_sem, br_sem,
):
    nx, ny = sizes
    gx, gy, gz = lax.axis_index("gx"), lax.axis_index("gy"), lax.axis_index("gz")
    other = 1 - gz

    def dev(dx, dy, z):
        return (lax.rem(gx + dx + nx, nx), lax.rem(gy + dy + ny, ny), z)

    loads = [
        pltpu.make_async_copy(u_hbm, A.at[:, 2:10, 8:24], in_sem.at[0]),
        pltpu.make_async_copy(t_hbm, TA.at[2:10, 8:40], in_sem.at[1]),
        pltpu.make_async_copy(m_hbm, MA.at[2:10, 8:40], in_sem.at[2]),
    ]
    for copy in loads:
        copy.start()

    def exists(dx, dy):
        tests = []
        for at, d, size in ((gx, dx, nx), (gy, dy, ny)):
            if not (isinstance(d, int) and d == 0):
                tests.append((at + d >= 0) & (at + d < size))
        if not tests:
            return None
        return tests[0] if len(tests) == 1 else tests[0] & tests[1]

    def when(cond, body):
        if cond is None:
            body()
        else:
            pl.when(cond)(body)

    SR[...] = jnp.zeros((12, 5, 8, 128), F32)
    PR[...] = jnp.zeros((2, 9, 16, 128), F32)

    barrier = pltpu.get_barrier_semaphore()

    def greet(dx, dy, z):
        when(exists(dx, dy), lambda: pl.semaphore_signal(
            barrier, inc=1, device_id=dev(dx, dy, z), device_id_type=MESH))

    for dx in (-1, 0, 1):
        for dy in (-1, 0, 1):
            for z in (gz, other):
                if not (dx == 0 and dy == 0 and z is gz):
                    greet(dx, dy, z)
    beside_x = 3 - jnp.where(gx == 0, 1, 0) - jnp.where(gx == nx - 1, 1, 0)
    beside_y = 3 - jnp.where(gy == 0, 1, 0) - jnp.where(gy == ny - 1, 1, 0)

    sent = []

    def remote(src, dst, s_sem, r_sem, target):
        return pltpu.make_async_remote_copy(
            src_ref=src, dst_ref=dst, send_sem=s_sem, recv_sem=r_sem,
            device_id=dev(*target), device_id_type=MESH,
        )

    def send(src, dst, s_sem, r_sem, target):
        args = (src, dst, s_sem, r_sem, target)
        cond = exists(target[0], target[1])
        when(cond, lambda: remote(*args).start())
        sent.append((cond, args))

    def drain(items):
        for cond, args in items:
            when(cond, lambda: remote(*args).wait_send())

    def arrive(dst, s_sem, r_sem, dx, dy):
        when(exists(dx, dy), lambda: remote(dst, dst, s_sem, r_sem, (1, 0, gz)).wait_recv())

    def vapor_slots(X):
        slots = [X.at[:, 0:2, 8:24], X.at[:, 10:12, 8:24], X.at[:, 2:10, 6:8], X.at[:, 2:10, 24:26]]
        for xi in (1, 10):
            for row in (7, 24):
                slots.append(X.at[:, xi:xi + 1, row:row + 1])
        return slots

    def vapor_sources(own):
        sources = [own(6, 2, 0, 16), own(0, 2, 0, 16), own(0, 8, 14, 2), own(0, 8, 0, 2)]
        for x in (7, 0):
            for y in (15, 0):
                sources.append(own(x, 1, y, 1))
        return sources

    vapor_targets = [(1, 0), (-1, 0), (0, 1), (0, -1), (1, 1), (1, -1), (-1, 1), (-1, -1)]

    def send_vapor(step, own, X):
        slots, sources = vapor_slots(X), vapor_sources(own)
        for n in (0, 1, 4, 5, 6, 7, 2, 3):
            send(sources[n], slots[n], us_sem.at[step, n], ur_sem.at[step, n],
                 (*vapor_targets[n], gz))

    def await_vapor(step, X):
        slots = vapor_slots(X)
        for n in range(8):
            arrive(slots[n], us_sem.at[step, n], ur_sem.at[step, n],
                   -vapor_targets[n][0], -vapor_targets[n][1])

    lane8 = iota((8, 128), 1)
    sub8 = iota((8, 128), 0)

    def pack_z(step, X):
        shift = jnp.where(gz == 0, 2, 0)
        turned = lax.rem(lane8 + shift, 128) // 2
        for half in range(2):
            acc = jnp.zeros((8, 128), F32)
            for k in range(64 if half == 0 else 32):
                n = half * 64 + k
                c, x, yt = n // 16, (n // 2) % 8, n % 2
                v = X[c, x + 2, 8 + 8 * yt:16 + 8 * yt, :]
                if k:
                    v = pltpu.roll(v, 2 * k, 1)
                acc = jnp.where(turned == k, v, acc)
            ZS[step, half] = acc

    z_targets = [(0, 0), (1, 0), (-1, 0), (0, 1), (0, -1)]

    def send_z(step):
        for n in range(5):
            send(ZS.at[step], ZR.at[step, n], zs_sem.at[step, n], zr_sem.at[step, n],
                 (*z_targets[n], other))

    def await_z(step):
        for n in range(5):
            arrive(ZR.at[step, n], zs_sem.at[step, n], zr_sem.at[step, n],
                   -z_targets[n][0], -z_targets[n][1])

    edge_keep = lax.rem(lane8 + 2 * gz, 128) < 2

    def flag(cond):
        return jnp.where(cond, 1.0, 0.0)

    def rim_flags():
        return jnp.where(sub8 < 4, flag(gy < ny - 1), flag(gy > 0)) > 0.5

    def unpack_z(step):
        def tile(slot, c, x, yt):
            n = c * 16 + x * 2 + yt
            v = ZR[step, slot, n // 64]
            k = 2 * (n % 64)
            if k:
                v = pltpu.roll(v, 128 - k, 1)
            return jnp.where(edge_keep, v, 0.0)

        for c in range(6):
            for yt in range(2):
                rows = slice(8 + 8 * yt, 16 + 8 * yt)
                for x in range(8):
                    UE[c, x + 1, rows, :] = tile(0, c, x, yt)
                UE[c, 0, rows, :] = tile(1, c, 7, yt)
                UE[c, 9, rows, :] = tile(2, c, 0, yt)
            for x in range(8):
                low, high = tile(3, c, x, 1), tile(4, c, x, 0)
                rim = jnp.where(sub8 < 4, high, low)
                UE[c, x + 1, 0:8, :] = rim
                UE[c, x + 1, 24:32, :] = rim

    def clear_outside(X):
        @pl.when(gx == 0)
        def _():
            X[:, 0:2] = jnp.zeros((6, 2, 32, 128), F32)
            UE[:, 0:1] = jnp.zeros((6, 1, 32, 128), F32)

        @pl.when(gx == nx - 1)
        def _():
            X[:, 10:12] = jnp.zeros((6, 2, 32, 128), F32)
            UE[:, 9:10] = jnp.zeros((6, 1, 32, 128), F32)

        rim_valid = rim_flags()

        @pl.loop(1, 11, unroll=5)
        def _(xi):
            for c in range(6):
                rim = jnp.where(sub8 < 4, X[c, xi, 24:32, :], X[c, xi, 0:8, :])
                rim = jnp.where(rim_valid, rim, 0.0)
                X[c, xi, 0:8, :] = rim
                X[c, xi, 24:32, :] = rim

        @pl.when((gy == 0) | (gy == ny - 1))
        def _():
            @pl.loop(0, 10, unroll=2)
            def _(xi):
                for c in range(6):
                    rim = jnp.where(rim_valid, UE[c, xi, 0:8, :], 0.0)
                    UE[c, xi, 0:8, :] = rim
                    UE[c, xi, 24:32, :] = rim

    def advance(X, emit, early=None):
        rim_rows = rim_flags()
        lane16 = iota((16, 128), 1)
        edge_lane = jnp.where(gz == 0, 0, 127)

        @pl.loop(0, 10, unroll=10)
        def _(i):
            xi = i + 1

            def load(c, dx, dy):
                return X[c, xi + dx, 8 + dy:24 + dy, :]

            new = forward_euler(load, lambda c: UE[c, i, 8:24, :])
            for c in range(6):
                F[c, i, 8:24, :] = new[c]

        @pl.loop(0, 8, unroll=8)
        def _(x):
            def load_rim(c, dx, dy):
                start = {0: 0, 1: 1, -1: 23}[dy]
                return X[c, x + 2 + dx, start:start + 8, :]

            new = forward_euler(load_rim, lambda c: UE[c, x + 1, 0:8, :])
            for c in range(6):
                rim = jnp.where(rim_rows, new[c], 0.0)
                F[c, x + 1, 0:8, :] = rim
                F[c, x + 1, 24:32, :] = rim

            def load_edge(c, dx, dy):
                return UE[c, x + 1 + dx, 8 + dy:24 + dy, :]

            new = forward_euler(load_edge, lambda c: X[c, x + 2, 8:24, :])
            for c in range(6):
                FE[c, x] = jnp.where(lane16 == edge_lane, new[c], 0.0)

        @pl.when(gx == 0)
        def _():
            F[:, 0:1] = jnp.zeros((6, 1, 32, 128), F32)

        @pl.when(gx == nx - 1)
        def _():
            F[:, 9:10] = jnp.zeros((6, 1, 32, 128), F32)

        def second(which, count):
            @pl.loop(0, 8, unroll=count)
            def _(x):
                def load(c, dx, dy):
                    return F[c, x + 1 + dx, 8 + dy:24 + dy, :]

                new = forward_euler(load, lambda c: FE[c, x], which)
                for c in which:
                    emit(c, x, 0.5 * (X[c, x + 2, 8:24, :] + new[c]))

        if early is None:
            second(range(6), 4)
        else:
            second((5,), 8)
            early()
            second(range(5), 4)

    row_first = gx * 16 - 8
    col_first = gy * 32 - 32
    rows_all, cols_all = nx * 16, ny * 32

    def gauss(cells, centre):
        d = (cells.astype(F32) - centre.astype(F32)) / 6.0
        return jnp.exp(-(d * d))

    def prepare():
        col = col_first + lane8
        col_in = (col >= 0) & (col < cols_all) & (lane8 < 96)
        depth = jnp.exp(-(sub8.astype(F32)) / 4.0)
        for sub in range(4):
            a, b = path_ref[0, sub], path_ref[1, sub]
            profile = LASER_POWER * depth * gauss(col, b)

            @pl.loop(0, 32, unroll=8)
            def _(r):
                along = gauss(jnp.full((8, 128), row_first + r, jnp.int32), a)
                SL[sub, pl.ds(pl.multiple_of(r * 8, 8), 8), :] = profile * along

            c48 = gy * 32 - 8 + iota((48, 128), 0)
            d48 = jnp.exp(-(iota((48, 128), 1).astype(F32)) / 4.0)
            LYD[sub] = LASER_POWER * d48 * gauss(c48, b)
            for r in range(12):
                cell = jnp.full((8, 128), (gx * 2 + gz) * 8 - 2 + r, jnp.int32)
                LXB[sub * 12 + r] = gauss(cell, a)

        @pl.loop(0, 32, unroll=8)
        def _(r):
            row = row_first + r
            row_in = flag((row >= 0) & (row < rows_all))
            SM[pl.ds(pl.multiple_of(r * 8, 8), 8), :] = jnp.where(col_in, row_in, 0.0)

        level = jnp.concatenate(
            [lvl_ref[...].astype(F32), jnp.zeros((8, 112), F32)], axis=1)
        SS[4] = level
        eye = jnp.where(iota((16, 128), 0) == iota((16, 128), 1), 1.0, 0.0)
        own = nt(eye, jnp.concatenate([level, jnp.zeros((120, 128), F32)], axis=0))
        heights = (iota((16, 128), 1) + gz * 128).astype(F32)
        for x in range(8):
            HIT[x] = jnp.where(heights == own[:, x:x + 1], 1.0, 0.0)

    def pack_surface():
        pick = jnp.where(sub8 == lane8, 1.0, 0.0)
        for half in range(2):
            t = TA[2 + 4 * half:6 + 4 * half, 8:40, :].reshape(128, 128)
            m = MA[2 + 4 * half:6 + 4 * half, 8:40, :].reshape(128, 128).astype(F32)
            SS[half] = nt(pick, t)
            SS[2 + half] = nt(pick, m)

    own_slot = (1 + gz) * 3 + 1

    def send_surface():
        for near in (True, False):
            tx = 0 if near else 2 * gz - 1
            block = 1 + gz if near else 3 - 3 * gz
            for ty in (-1, 0, 1):
                for z in (gz, other):
                    if near and ty == 0 and z is gz:
                        continue
                    slot = block * 3 + 1 - ty
                    same = 1 if z is gz else 0
                    n = (6 if near else 0) + (ty + 1) * 2 + same
                    send(SS, SR.at[slot], ss_sem.at[n], sr_sem.at[slot], (tx, ty, z))

    def await_surface():
        for slot in range(12):
            if slot in (4, 7):
                @pl.when(own_slot != slot)
                def _():
                    arrive(SR.at[slot], ss_sem.at[0], sr_sem.at[slot], 0, 0)
            else:
                arrive(SR.at[slot], ss_sem.at[0], sr_sem.at[slot],
                       (-1, 0, 0, 1)[slot // 3], slot % 3 - 1)

    def assemble_surface():
        SK[0:8, :] = jnp.zeros((8, 128), F32)
        SK[264:272, :] = jnp.zeros((8, 128), F32)
        SA[0:8, :] = jnp.zeros((8, 128), F32)
        SA[264:272, :] = jnp.zeros((8, 128), F32)
        SB[0:8, :] = jnp.zeros((8, 128), F32)
        SB[264:272, :] = jnp.zeros((8, 128), F32)
        SGX[0:8, :] = jnp.zeros((8, 128), F32)

        def merged(rb, x, first):
            parts = []
            for cb in range(3):
                v = SR[rb * 3 + cb, first + x // 4]
                shift = (32 * cb - 32 * (x % 4)) % 128
                parts.append(pltpu.roll(v, shift, 1) if shift else v)
            return jnp.where(lane8 < 32, parts[0], jnp.where(lane8 < 64, parts[1], parts[2]))

        @pl.loop(0, 4)
        def _(rb):
            for x in range(8):
                at = pl.multiple_of(rb * 64 + x * 8, 8)
                mask = SM[pl.ds(at, 8), :] > 0.5
                phase = merged(rb, x, 2)
                k = jnp.where(phase < 0.5, 0.04, jnp.where(phase < 1.5, 0.15, 0.09))
                SK[pl.ds(at + 8, 8), :] = jnp.where(mask, k, 0.0)
                SA[pl.ds(at + 8, 8), :] = jnp.where(mask, merged(rb, x, 0), 0.0)

        @pl.loop(0, 32, unroll=8)
        def _(r):
            at = pl.multiple_of(r * 8, 8)
            k = SK[pl.ds(at + 8, 8), :]
            SGX[pl.ds(at + 8, 8), :] = 0.5 * (k + SK[pl.ds(at + 16, 8), :])
            SGY[pl.ds(at, 8), :] = 0.5 * (k + pltpu.roll(k, 127, 1))
            SGD[pl.ds(at, 8), :] = jnp.where(sub8 == 7, 0.0, 0.5 * (k + pltpu.roll(k, 7, 0)))
            SGB[pl.ds(at, 8), :] = jnp.where(sub8 == 0, 0.5 * k, 0.0)

        blocks = []
        for rb in (0, 1, 3):
            acc = SR[rb * 3, 4]
            for cb in (1, 2):
                acc = acc + pltpu.roll(SR[rb * 3 + cb, 4], 16 * cb, 1)
            blocks.append(acc)
        blocks.append(jnp.zeros((104, 128), F32))
        eye = jnp.where(iota((48, 128), 0) == iota((48, 128), 1), 1.0, 0.0)
        LL[...] = nt(eye, jnp.concatenate(blocks, axis=0))

    def surface_conduct(sub, src, dst):
        for chunk in range(4):
            base = chunk * 64
            t = src[base + 8:base + 72, :]
            g = SGX[base + 8:base + 72, :]
            change = g * (src[base + 16:base + 80, :] - t) - SGX[base:base + 64, :] * (
                t - src[base:base + 64, :])
            flow = SGY[base:base + 64, :] * (pltpu.roll(t, 127, 1) - t)
            change = change + (flow - pltpu.roll(flow, 1, 1))
            t3 = t.reshape(8, 8, 128)
            gd = SGD[base:base + 64, :].reshape(8, 8, 128)
            flow3 = gd * (pltpu.roll(t3, 7, 1) - t3)
            change = change + (flow3 - pltpu.roll(flow3, 1, 1)).reshape(64, 128)
            change = change - SGB[base:base + 64, :] * t + SL[sub, base:base + 64, :]
            dst[base + 8:base + 72, :] = (t + change) * SM[base:base + 64, :]

    def surface_cool(src, dst, fine_pressure):
        top = src[pl.ds(8, 32, stride=8), :]
        cooling = LATENT_HEAT * softplus(top - 1.0 - 0.5 * fine_pressure)
        cooling = cooling * SM[pl.ds(0, 32, stride=8), :]
        dst[pl.ds(8, 32, stride=8), :] = dst[pl.ds(8, 32, stride=8), :] - cooling

    def pressures(step, X, at_x, at_y):
        lane16 = iota((16, 128), 1)
        acc = jnp.zeros((16, 128), F32)
        for x in range(8):
            v = X[5, x + at_x, at_y:at_y + 16, :]
            s = jnp.sum(HIT[x] * v, axis=1, keepdims=True)
            acc = jnp.where(lane16 == x, s, acc)
        PS[step] = acc

        @pl.when(gz == 0)
        def _():
            PR[step, 4] = acc

    p_targets = [(tx, ty, s) for tx in (-1, 0, 1) for ty in (-1, 0, 1) for s in (0, 1)
                 if (tx, ty, s) != (0, 0, 1)]

    def p_needed(step, n):
        tx, ty, same = p_targets[n]
        return step == 0 or (not (tx and ty) and (same or tx != 1))

    def p_copy(step, n):
        tx, ty, s = p_targets[n]
        slot = (1 - tx) * 3 + 1 - ty
        return pltpu.make_async_remote_copy(
            src_ref=PS.at[step], dst_ref=PR.at[step, slot], send_sem=ps_sem.at[step, n],
            recv_sem=pr_sem.at[step, slot], device_id=dev(tx, ty, gz if s else other),
            device_id_type=MESH)

    def send_pressures(step):
        @pl.when(gz == 0)
        def _():
            for n in range(17):
                if p_needed(step, n):
                    when(exists(*p_targets[n][:2]), lambda: p_copy(step, n).start())

    def await_pressures(step):
        for slot in range(9):
            if slot == 4:
                @pl.when(gz == 1)
                def _():
                    arrive(PR.at[step, slot], ps_sem.at[step, 0], pr_sem.at[step, slot], 0, 0)
            elif step == 1 and slot == 1:
                @pl.when((gz == 0) & (gx > 0))
                def _():
                    arrive(PR.at[step, slot], ps_sem.at[step, 0], pr_sem.at[step, slot], 0, 0)
            elif step == 0 or slot in (3, 5, 7):
                arrive(PR.at[step, slot], ps_sem.at[step, 0], pr_sem.at[step, slot],
                       slot // 3 - 1, slot % 3 - 1)

    def coarse_pressure(step):
        blocks = []
        for by in range(3):
            acc = PR[step, by]
            for bx in (1, 2):
                acc = acc + pltpu.roll(PR[step, bx * 3 + by], 8 * bx, 1)
            blocks.append(acc)
        return jnp.concatenate(blocks, axis=0)

    def fine_from_coarse(coarse):
        rows = jnp.where(iota((32, 128), 1) == (iota((32, 128), 0) + 8) // 2, 1.0, 0.0)
        cols = jnp.where(iota((128, 128), 0) == iota((128, 128), 1) // 2, 1.0, 0.0)
        padded = jnp.concatenate([coarse, jnp.zeros((80, 128), F32)], axis=0)
        return nn(nt(rows, padded), cols)

    def mass_from_surface(ref, coarse):
        top = jnp.concatenate(
            [ref[pl.ds(8, 32, stride=8), :], jnp.zeros((96, 128), F32)], axis=0)
        cols = jnp.where(iota((48, 128), 0) == iota((48, 128), 1) // 2, 0.25, 0.0)
        i = iota((128, 128), 0)
        rows = jnp.where((iota((128, 128), 1) == (i + 8) // 2) & (i < 32), 1.0, 0.0)
        surface = nn(nt(cols, top), rows)
        mass = softplus(surface - 1.0 - 0.5 * coarse)
        y = gy * 16 - 16 + iota((48, 128), 0)
        x = gx * 8 - 8 + iota((48, 128), 1)
        inside = (y >= 0) & (y < ny * 16) & (x >= 0) & (x < nx * 8)
        return jnp.where(inside, mass, 0.0)

    def with_rim(v):
        rim = jnp.where(sub8 < 4, v[32:40], v[8:16])
        return jnp.concatenate([rim, v[16:32], rim], axis=0)

    row_block = gx * 2 + gz
    dn_row, up_row = -(1 - gz), gz

    def bulk_slots(X):
        slots = [X.at[0:2, 8:40], X.at[10:12, 8:40], X.at[2:10, 6:8], X.at[2:10, 40:42]]
        for r in (1, 10):
            for c in (7, 40):
                slots.append(X.at[r:r + 1, c:c + 1])
        return slots

    def bulk_sources(X, r0, c0):
        def own(r, nr, c, nc):
            return X.at[r0 + r:r0 + r + nr, c0 + c:c0 + c + nc]

        sources = [own(6, 2, 0, 32), own(0, 2, 0, 32), own(0, 8, 30, 2), own(0, 8, 0, 2)]
        for r in (7, 0):
            for c in (31, 0):
                sources.append(own(r, 1, c, 1))
        return sources

    bulk_targets = [(up_row, 0, other), (dn_row, 0, other), (0, 1, gz), (0, -1, gz)]
    bulk_origins = [(dn_row, 0), (up_row, 0), (0, -1), (0, 1)]
    for tx, ox in ((up_row, dn_row), (dn_row, up_row)):
        for ty in (1, -1):
            bulk_targets.append((tx, ty, other))
            bulk_origins.append((ox, -ty))

    def send_bulk(kind, X, r0, c0, D):
        sources, slots = bulk_sources(X, r0, c0), bulk_slots(D)
        for n in range(8):
            send(sources[n], slots[n], bs_sem.at[kind, n], br_sem.at[kind, n], bulk_targets[n])

    def await_bulk(kind, D):
        slots = bulk_slots(D)
        for n in range(8):
            arrive(slots[n], bs_sem.at[kind, n], br_sem.at[kind, n], *bulk_origins[n])

    def clear_bulk(X):
        @pl.when(row_block == 0)
        def _():
            X[0:2] = jnp.zeros((2, 48, 128), F32)

        @pl.when(row_block == 2 * nx - 1)
        def _():
            X[10:12] = jnp.zeros((2, 48, 128), F32)

        @pl.when(gy == 0)
        def _():
            X[:, 0:8] = jnp.zeros((12, 8, 128), F32)

        @pl.when(gy == ny - 1)
        def _():
            X[:, 40:48] = jnp.zeros((12, 8, 128), F32)

    def prepare_bulk():
        @pl.loop(0, 12, unroll=6)
        def _(r):
            m = MA[r]
            KB[r] = jnp.where(m == 0, 0.04, jnp.where(m == 1, 0.15, 0.09))

        clear_bulk(KB)

        @pl.loop(0, 11, unroll=11)
        def _(r):
            k = KB[r]
            GX[r] = 0.5 * (k + KB[r + 1])
            GY[r] = 0.5 * (k + pltpu.roll(k, 47, 0))
            last = iota((48, 128), 1) == 127
            GD[r] = 0.5 * (k + jnp.where(last, 0.0, pltpu.roll(k, 127, 1)))

    def bulk_substep(sub, src, dst, low, high, own_only=False):
        col = gy * 32 - 8 + iota((48, 128), 0)
        col_in = jnp.where((col >= 0) & (col < cols_all), 1.0, 0.0)
        last = iota((48, 128), 1) == 127

        @pl.loop(low, high, unroll=(high - low) // 2)
        def _(r):
            t = src[r]
            change = GX[r] * (src[r + 1] - t) - GX[r - 1] * (t - src[r - 1])
            flow = GY[r] * (pltpu.roll(t, 47, 0) - t)
            change = change + (flow - pltpu.roll(flow, 1, 0))
            flow = GD[r] * (jnp.where(last, 0.0, pltpu.roll(t, 127, 1)) - t)
            change = change + (flow - pltpu.roll(flow, 1, 1))
            along = LXB[sub * 12 + r]
            laser = LYD[sub] * jnp.concatenate([along] * 6, axis=0)
            row = row_block * 8 - 2 + r
            row_in = jnp.where((row >= 0) & (row < rows_all), 1.0, 0.0)
            new = (t + change + laser) * (col_in * row_in)
            if own_only:
                dst[r, 8:40, :] = new[8:40]
            else:
                dst[r] = new

    pl.semaphore_wait(barrier, 2 * beside_x * beside_y - 1)
    send_vapor(0, lambda x, n, y, m: u_hbm.at[:, x:x + n, y:y + m], A)
    loads[0].wait()
    pack_z(0, A)
    send_z(0)
    prepare()
    loads[1].wait()
    loads[2].wait()
    pack_surface()
    SR[own_slot] = SS[...]
    send_surface()
    send_bulk(0, t_hbm, 0, 0, TA)
    send_bulk(1, m_hbm, 0, 0, MA)

    await_z(0)
    unpack_z(0)
    await_vapor(0, A)
    clear_outside(A)

    def to_b(c, x, v):
        B[c, x + 2, 8:24, :] = v

    def share_first():
        pressures(0, B, 2, 8)
        send_pressures(0)

    advance(A, to_b, share_first)
    pack_z(1, B)
    send_z(1)
    first = len(sent)
    send_vapor(1, lambda x, n, y, m: B.at[:, x + 2:x + 2 + n, y + 8:y + 8 + m], B)
    sent_b = sent[first:]
    del sent[first:]

    await_surface()
    assemble_surface()
    await_bulk(0, TA)
    await_bulk(1, MA)
    clear_bulk(TA)
    prepare_bulk()
    bulk_substep(0, TA, TC, 1, 11)
    bulk_substep(1, TC, TB, 2, 10, True)
    send_bulk(2, TB, 2, 8, TB)

    surface_conduct(0, SA, SB)
    LL[0:32, :] = with_rim(LL[...])
    await_pressures(0)
    coarse = coarse_pressure(0)
    fine = fine_from_coarse(coarse)
    surface_cool(SA, SB, fine)
    surface_conduct(1, SB, SA)
    surface_cool(SB, SA, fine)
    MM[...] = with_rim(mass_from_surface(SA, coarse))

    await_z(1)
    unpack_z(1)
    await_vapor(1, B)
    clear_outside(B)
    drain(sent_b)
    lane32 = iota((32, 128), 1)
    height = (lane32 + gz * 128).astype(F32)
    height_edge = (lane32 + other * 128).astype(F32)
    def field_at(xi, heights):
        mass = jnp.broadcast_to(MM[:, xi + 6:xi + 7], (32, 128))
        level = jnp.broadcast_to(LL[0:32, xi + 6:xi + 7], (32, 128))
        return jnp.where(heights == level, mass, 0.0)

    @pl.when(gz == 0)
    def _():
        for xi in range(12):
            field = field_at(xi, height)
            B[0, xi] = B[0, xi] + 0.5 * field
            B[4, xi] = B[4, xi] + 0.4 * field
            B[5, xi] = B[5, xi] + 0.6 * field

    @pl.when(gz == 1)
    def _():
        for xi in range(1, 11):
            field = jnp.where(lane32 >= 126, field_at(xi, height_edge), 0.0)
            UE[0, xi - 1] = UE[0, xi - 1] + 0.5 * field
            UE[4, xi - 1] = UE[4, xi - 1] + 0.4 * field
            UE[5, xi - 1] = UE[5, xi - 1] + 0.6 * field

    def to_out(c, x, v):
        uo_ref[c, x] = v

    def share_pressure():
        pressures(1, uo_ref, 0, 0)
        send_pressures(1)

    advance(B, to_out, share_pressure)

    await_bulk(2, TB)
    clear_bulk(TB)
    bulk_substep(2, TB, TC, 1, 11)
    bulk_substep(3, TC, TA, 2, 10, True)

    surface_conduct(2, SA, SB)
    await_pressures(1)
    coarse = coarse_pressure(1)
    fine = fine_from_coarse(coarse)
    surface_cool(SA, SB, fine)
    surface_conduct(3, SB, SA)
    surface_cool(SB, SA, fine)
    mass_now = mass_from_surface(SA, coarse)[16:32]
    for x in range(8):
        mass = jnp.broadcast_to(mass_now[:, x + 8:x + 9], (16, 128))
        field = HIT[x] * mass
        uo_ref[0, x] = uo_ref[0, x] + 0.5 * field
        uo_ref[4, x] = uo_ref[4, x] + 0.4 * field
        uo_ref[5, x] = uo_ref[5, x] + 0.6 * field

    eye = jnp.where(iota((128, 128), 0) == iota((128, 128), 1), 1.0, 0.0)
    for half in range(2):
        acc = jnp.zeros((8, 128), F32)
        for i in range(4):
            at = pl.multiple_of((9 + gz * 8 + 4 * half + i) * 8, 8)
            v = SA[pl.ds(at, 8), :]
            shift = (32 * i - 32) % 128
            v = pltpu.roll(v, shift, 1) if shift else v
            acc = jnp.where(lane8 // 32 == i, v, acc)
        turned = nt(eye, jnp.concatenate([acc, jnp.zeros((120, 128), F32)], axis=0))
        turned = turned.reshape(4, 32, 128)
        shallow = iota((4, 32, 128), 2) < 4
        deep = TA[2 + 4 * half:6 + 4 * half, 8:40, :]
        to_ref[4 * half:4 * half + 4] = jnp.where(shallow, turned, deep)

    drain(sent)

    @pl.when(gz == 0)
    def _():
        for step in range(2):
            for n in range(17):
                if p_needed(step, n):
                    when(exists(*p_targets[n][:2]), lambda: p_copy(step, n).wait_send())


def write_back(gas_ref, temp_ref, gas_out, temp_out, sem):
    copies = [
        pltpu.make_async_copy(gas_ref, gas_out, sem.at[0]),
        pltpu.make_async_copy(temp_ref, temp_out, sem.at[1]),
    ]
    for copy in copies:
        copy.start()
    for copy in copies:
        copy.wait()


def solution(mesh):
    sizes = (mesh.shape["gx"], mesh.shape["gy"])

    def shards(vapor, thermal, phase, level, path):
        anywhere = pl.BlockSpec(memory_space=pl.ANY)
        vmem = pl.BlockSpec(memory_space=pltpu.VMEM)
        dma = pltpu.SemaphoreType.DMA
        row = (12, 48, 128)
        gas, temp = pl.pallas_call(
            functools.partial(kernel, sizes),
            out_shape=(
                pltpu.VMEM((6, 8, 16, 128), F32),
                pltpu.VMEM((8, 32, 128), F32),
            ),
            in_specs=[anywhere, anywhere, anywhere, vmem, pl.BlockSpec(memory_space=pltpu.SMEM)],
            out_specs=(vmem, vmem),
            scratch_shapes=[
                pltpu.VMEM((6, 12, 32, 128), F32), pltpu.VMEM((6, 12, 32, 128), F32),
                pltpu.VMEM((6, 10, 32, 128), F32), pltpu.VMEM((6, 10, 32, 128), F32),
                pltpu.VMEM((6, 8, 16, 128), F32),
                pltpu.VMEM((2, 2, 8, 128), F32), pltpu.VMEM((2, 5, 2, 8, 128), F32),
                pltpu.VMEM((5, 8, 128), F32), pltpu.VMEM((12, 5, 8, 128), F32),
                pltpu.VMEM((2, 16, 128), F32), pltpu.VMEM((2, 9, 16, 128), F32),
                pltpu.VMEM(row, F32), pltpu.VMEM(row, jnp.int32), pltpu.VMEM(row, F32),
                pltpu.VMEM(row, F32), pltpu.VMEM(row, F32), pltpu.VMEM(row, F32),
                pltpu.VMEM(row, F32), pltpu.VMEM(row, F32),
                pltpu.VMEM((48, 8, 128), F32), pltpu.VMEM((4, 48, 128), F32),
                pltpu.VMEM((272, 128), F32), pltpu.VMEM((272, 128), F32),
                pltpu.VMEM((272, 128), F32), pltpu.VMEM((264, 128), F32),
                pltpu.VMEM((256, 128), F32), pltpu.VMEM((256, 128), F32),
                pltpu.VMEM((256, 128), F32), pltpu.VMEM((4, 256, 128), F32),
                pltpu.VMEM((256, 128), F32), pltpu.VMEM((8, 16, 128), F32),
                pltpu.VMEM((48, 128), F32), pltpu.VMEM((32, 128), F32),
                dma((3,)), dma((2, 8)), dma((2, 8)), dma((2, 5)), dma((2, 5)),
                dma((12,)), dma((12,)), dma((2, 17)), dma((2, 9)),
                dma((3, 8)), dma((3, 8)),
            ],
            compiler_params=pltpu.CompilerParams(collective_id=0, has_side_effects=True),
        )(vapor, jnp.transpose(thermal, (1, 2, 0)), jnp.transpose(phase, (1, 2, 0)), level, path.T)
        gas = pltpu.with_memory_space_constraint(gas, pltpu.VMEM)
        temp = pltpu.with_memory_space_constraint(temp, pltpu.VMEM)
        gas, temp = pl.pallas_call(
            write_back,
            out_shape=(
                jax.ShapeDtypeStruct((6, 8, 16, 128), F32),
                jax.ShapeDtypeStruct((8, 32, 128), F32),
            ),
            in_specs=[vmem, vmem],
            out_specs=(anywhere, anywhere),
            scratch_shapes=[dma((2,))],
        )(gas, temp)
        return gas, jnp.transpose(temp, (2, 0, 1))

    return jax.shard_map(
        shards,
        mesh=mesh,
        in_specs=(
            P(None, "gx", "gy", "gz"),
            P(None, ("gx", "gz"), "gy"),
            P(None, ("gx", "gz"), "gy"),
            P("gx", "gy"),
            P(),
        ),
        out_specs=(P(None, "gx", "gy", "gz"), P(None, ("gx", "gz"), "gy")),
        check_vma=False,
    )
```
